32 devices in a mesh: rows: 8 (over y, x, core), rhs: 4 (over z).
Axes of the slice: x: 2, y: 2, z: 4, core: 2. Of those that a mesh axis runs over, the one named last changes fastest.
Arguments:
- win_rows: bfloat16 [4096, 4096], P('rows'), may hold values from -0.09375 to 0.09375
- anc_rows: bfloat16 [16384, 4096], P('rows'), may hold values from -0.09375 to 0.09375
- win_pattern: int32 [64, 64], replicated, may hold values 0 or 1
- anc_pattern: int32 [256, 64], P('rows'), may hold values 0 or 1
- window_owner: int32 [64], replicated, may hold values from 0 to 63, each once
- sn_order: int32 [8], replicated, may hold values from 0 to 7, each once
- diag_inv: bfloat16 [8, 512, 512], replicated, as said below
- rhs_win: bfloat16 [4096, 1024], P(('rows', 'rhs')), may hold values from -0.119628906 to 0.119628906
- rhs_anc: bfloat16 [16384, 1024], P(('rows', 'rhs')), may hold values from -6 to 6
Outputs:
- window_solution: bfloat16 [4096, 1024], P(None, 'rhs')
- anc_residual: bfloat16 [16384, 1024], P('rows', 'rhs')
The draws below stay inside these ranges and needn't reach their ends.
Inputs may be any that keep to these rules, and one draw needn't show every extreme that they name: `window_owner`: each storage slot holds exactly one window block row. `sn_order`: each supernode label appears once. `diag_inv`: each block is lower triangular.
All inputs are finite; a program needn't handle non-finite values. No bound on the sum of `anc_pattern` on one device may be relied on, other than what follows from the above.
Results may differ from the reference program's by a relative error of at most 0.025.
Values may be sent and summed in bfloat16 or wider, within the bound.
No kernel may reach another device: no remote copies, remote signals or barrier semaphores. Data moves between devices by JAX's collectives and lax.ppermute only.
A program may use at most 256 MiB of HBM per device.

```python
import jax
import jax.numpy as jnp
from jax import lax

BS = 64
SB = 8
NSUP = 8
NRHS = 1024
ANC_DEV = 32
SN = 512
NWB = 64
NW = 4096
NANC = 16384
N_ROWS = 8


def draw_diag_inv(key, part):
    first, second = jax.random.split(key, 2)
    shape = (NSUP, SN, SN)
    row_index = lax.broadcasted_iota(jnp.int32, shape, 1)
    col_index = lax.broadcasted_iota(jnp.int32, shape, 2)
    diagonal = jax.random.uniform(first, shape, jnp.float32, 0.6, 1.4)
    off_part = jax.random.normal(second, shape, jnp.float32) * (0.6 / SN ** 0.5)
    row_scale = jnp.full((NSUP, SN, 1), 4.2, jnp.float32)
    lower_part = jnp.where(col_index < row_index, off_part, 0.0)
    return (jnp.where(col_index == row_index, diagonal, lower_part) * row_scale).astype(jnp.bfloat16)


def set_ends(drawn, own_key, low, top_value):
    longest = drawn.shape.index(max(drawn.shape))
    spots = []
    for shift in (0, 1):
        where = [jax.random.randint(jax.random.fold_in(own_key, axis), (), 0, length) for axis, length in enumerate(drawn.shape)]
        where[longest] = (where[longest] + shift) % drawn.shape[longest]
        spots.append(tuple(where))
    return drawn.at[spots[0]].set(low).at[spots[1]].set(top_value)


def block_levels(own_key, dims, cuts, least, high):
    def one(dim, parts):
        steps = jax.random.uniform(jax.random.fold_in(jax.random.fold_in(own_key, 6), dim), (parts,), jnp.float32, least / len(cuts), high / len(cuts))
        return jnp.repeat(jnp.exp(steps), dims[dim] // parts).reshape((-1,) + (1,) * (len(dims) - dim - 1))

    factor_of = one(*cuts[0])
    for cut in cuts[1:]:
        factor_of = factor_of * one(*cut)
    return factor_of


def normal_values(own_key, dims, spread, most, cuts=(), dtype=jnp.bfloat16):
    values = spread * jax.random.normal(own_key, dims, jnp.float32)
    if cuts:
        values = values * block_levels(own_key, dims, cuts, -0.22, 0.18)
    return jnp.clip(values, -most, most).astype(dtype)


def setup_inputs(seed: int = 0) -> dict:
    keys = jax.random.split(jax.random.key(seed), 10)
    win_rows = normal_values(keys[0], (NWB * BS, NW), NW ** -0.5, 0.09375, ((0, 8),))
    anc_rows = normal_values(keys[1], (NANC, NW), NW ** -0.5, 0.09375, ((0, 8),))
    win_pattern = set_ends((jax.random.randint(keys[2], (NWB, NWB), 0, 2) < 1).astype(jnp.int32), jax.random.fold_in(keys[2], 1), 0, 1)
    anc_pattern = set_ends((jax.random.randint(keys[3], (NANC // BS, NWB), 0, 2) < 1).astype(jnp.int32), jax.random.fold_in(keys[3], 1), 0, 1)
    window_owner = jax.random.permutation(keys[4], NWB).astype(jnp.int32)
    sn_order = jax.random.permutation(keys[5], NSUP).astype(jnp.int32)
    diag_inv = draw_diag_inv(jax.random.fold_in(keys[9], 71), 0)
    rhs_win = normal_values(keys[7], (NWB * BS, NRHS), 0.02, 0.119628906, ((0, 32),))
    rhs_anc = normal_values(keys[8], (NANC, NRHS), 1.0, 6.0, ((0, 32),))
    return dict(win_rows=win_rows, anc_rows=anc_rows, win_pattern=win_pattern, anc_pattern=anc_pattern, window_owner=window_owner, sn_order=sn_order, diag_inv=diag_inv, rhs_win=rhs_win, rhs_anc=rhs_anc)


def reference(win_rows, anc_rows, win_pattern, anc_pattern, window_owner, sn_order, diag_inv, rhs_win, rhs_anc):
    solution = jnp.zeros((NW, NRHS), jnp.bfloat16)
    row_blocks = win_rows.reshape(NWB, BS, NW)
    rhs_blocks = rhs_win.reshape(NWB, BS, NRHS)
    for position in range(NSUP):
        node_label = sn_order[position].astype(jnp.int32)
        owners = lax.dynamic_slice_in_dim(window_owner, (node_label * SB).astype(jnp.int32), SB, 0).astype(jnp.int32)
        factor = jnp.take(row_blocks, owners, axis=0)
        pattern = jnp.take(win_pattern, owners, axis=0)
        masked = (factor.reshape(SB, BS, NWB, BS) * pattern[:, None, :, None].astype(jnp.bfloat16)).reshape(SN, NW)
        panel = jnp.take(rhs_blocks, owners, axis=0).reshape(SN, NRHS).astype(jnp.float32)
        panel = panel - jnp.dot(masked, solution, preferred_element_type=jnp.float32)
        inverse = lax.dynamic_index_in_dim(diag_inv, node_label, 0, keepdims=False).astype(jnp.float32)
        solved = jnp.dot(inverse, panel, precision=lax.Precision.HIGHEST, preferred_element_type=jnp.float32).astype(jnp.bfloat16)
        solution = lax.dynamic_update_slice_in_dim(solution, solved, (node_label * SN).astype(jnp.int32), 0)
    group_rows = ANC_DEV * BS
    factor_groups = anc_rows.reshape(N_ROWS, group_rows, NW)
    pattern_groups = anc_pattern.reshape(N_ROWS, ANC_DEV, NWB)
    rhs_groups = rhs_anc.reshape(N_ROWS, group_rows, NRHS)

    def one_group(items):
        factor, pattern, right = items
        masked = (factor.reshape(ANC_DEV, BS, NWB, BS) * pattern[:, None, :, None].astype(jnp.bfloat16)).reshape(group_rows, NW)
        update = jnp.dot(masked, solution, preferred_element_type=jnp.float32)
        return (right.astype(jnp.float32) - update).astype(jnp.bfloat16)

    residual = lax.map(one_group, (factor_groups, pattern_groups, rhs_groups)).reshape(NANC, NRHS)
    return solution, residual
```

```python
import jax
import jax.numpy as jnp
from jax import lax
from jax.experimental import pallas as pl
from jax.experimental.pallas import tpu as pltpu
from jax.sharding import PartitionSpec as P

BS = 64
SB = 8
NSUP = 8
SN = 512
NW = 4096
NWB = 64
GROUPS = 4
PAIR = 2 * SN
F32 = jnp.float32
BF16 = jnp.bfloat16


def masked_columns(factor, pattern, node_label):
    blocks = pattern.shape[0]
    columns = lax.dynamic_slice_in_dim(factor, node_label * SN, SN, 1)
    chosen = lax.dynamic_slice_in_dim(pattern, node_label * SB, SB, 1)
    shaped = columns.reshape(blocks, BS, SB, BS) * chosen[:, None, :, None].astype(BF16)
    return shaped.reshape(blocks * BS, SN)


def general_path(win_rows, anc_rows, win_pattern, anc_pattern, window_owner, sn_order, diag_inv, win_rhs, anc_rhs):
    columns_rhs = win_rhs.shape[1]
    slot_count = win_rows.shape[0] // BS
    first_slot = lax.axis_index("rows") * slot_count
    local_pattern = lax.dynamic_slice_in_dim(win_pattern, first_slot, slot_count, 0)

    def step(position, carry):
        solution, win_resid, anc_resid = carry
        node_label = sn_order[position]
        owners = lax.dynamic_slice_in_dim(window_owner, node_label * SB, SB, 0)
        inverse = lax.dynamic_index_in_dim(diag_inv, node_label, 0, keepdims=False)
        local_place = owners - first_slot
        present = (local_place >= 0) & (local_place < slot_count)
        resid_blocks = win_resid.reshape(slot_count, BS, columns_rhs)
        taken = jnp.take(resid_blocks, jnp.clip(local_place, 0, slot_count - 1), axis=0)
        placed = jnp.where(present[:, None, None], taken, 0.0).reshape(SN, columns_rhs)
        panel = lax.psum(placed.astype(BF16), "rows")
        solved = jnp.dot(inverse, panel, preferred_element_type=F32).astype(BF16)
        solution = lax.dynamic_update_slice_in_dim(solution, solved, node_label * SN, 0)
        win_part = jnp.dot(masked_columns(win_rows, local_pattern, node_label), solved, preferred_element_type=F32)
        anc_part = jnp.dot(masked_columns(anc_rows, anc_pattern, node_label), solved, preferred_element_type=F32)
        return solution, win_resid - win_part, anc_resid - anc_part

    first = (jnp.zeros((NW, columns_rhs), BF16), win_rhs.astype(F32), anc_rhs.astype(F32))
    solution, _, anc_resid = lax.fori_loop(0, NSUP, step, first)
    return solution, anc_resid.astype(BF16)


def expand_mask(rows_pattern, first_block, width):
    block_index = lax.broadcasted_iota(jnp.int32, (NWB, width), 0)
    lane_index = lax.broadcasted_iota(jnp.int32, (NWB, width), 1)
    spread = (block_index == first_block + lane_index // BS).astype(F32).astype(BF16)
    return jnp.dot(rows_pattern.astype(F32).astype(BF16), spread, preferred_element_type=F32).astype(BF16)


def masked_rows(block_of, mask, count):
    return jnp.concatenate([block_of(j) * mask[j:j + 1, :] for j in range(count)], axis=0)


def factor_pack_kernel(owner, order, pattern, win_ref, out_ref, buf, inv_sm, pos_sm, sem):
    row = lax.axis_index("rows")

    def note_slot(w, c):
        slot = owner[w]

        @pl.when(slot // SB == row)
        def _():
            inv_sm[slot % SB] = w

        return c

    lax.fori_loop(0, NWB, note_slot, 0)
    for k in range(NSUP):
        pos_sm[order[k]] = k
    labels = []
    for t in range(SB):
        label = order[(pos_sm[inv_sm[t] // SB] // 2) * 2]
        labels.append(label)
        pltpu.make_async_copy(
            win_ref.at[pl.ds(t * BS, BS), pl.ds(pl.multiple_of(label * SN, SN), SN)],
            buf.at[pl.ds(t * BS, BS), :], sem).start()
    pltpu.make_async_copy(win_ref.at[:, pl.ds(0, SN)], buf, sem).wait()
    own = pattern[pl.ds(pl.multiple_of(row * SB, SB), SB), :]
    for t in range(SB):
        mask = expand_mask(own, labels[t] * SB, SN)
        out_ref[t * BS:(t + 1) * BS, :] = buf[t * BS:(t + 1) * BS, :] * mask[t:t + 1, :]


def place_of(owner, order, i, group):
    w = order[2 * group + i // SB] * SB + i % SB
    return owner[w]


def pack_group(owner, order, resid_ref, p_ref, b_ref, cnt, group):
    row = lax.axis_index("rows")
    chip, core = row // 2, row % 2
    cnt[0] = 0

    def one(i, c):
        slot = place_of(owner, order, i, group)

        @pl.when(slot // (2 * SB) == chip)
        def _():
            rank = cnt[0]
            cnt[0] = rank + 1
            side = jnp.where((slot // SB) % 2 == core, 0, 1)
            at = pl.multiple_of((side * SB + slot % SB) * BS, BS)

            @pl.when(rank < SB)
            def _():
                block = resid_ref[pl.ds(at, BS), :].astype(BF16)
                p_ref[pl.ds(pl.multiple_of(rank * BS, BS), BS), :] = block

                @pl.when(rank // 4 == core)
                def _():
                    b_ref[pl.ds(pl.multiple_of((rank % 4) * BS, BS), BS), :] = block

        return c

    lax.fori_loop(0, 2 * SB, one, 0)


def first_pack_kernel(owner, order, own_ref, other_ref, resid_ref, p_ref, b_ref, cnt):
    half = SB * BS
    resid_ref[0:half, :] = own_ref[...].astype(F32)
    resid_ref[half:2 * half, :] = other_ref[...].astype(F32)
    pack_group(owner, order, resid_ref, p_ref, b_ref, cnt, 0)


def make_group_kernel(group):
    last = group == GROUPS - 1

    def kernel(*refs):
        owner, order, pattern, p_own, a_own, a_swap, b_own, b_swap = refs[:8]
        l_refs = refs[8:16]
        diag_ref = refs[16]
        refs = refs[17:]
        if last:
            x_ref, panel, lbuf, dbuf, cnt, lsem, dsem = refs
        else:
            (w_own, w_other, resid_in, x_ref, resid_ref, p_ref, b_ref,
             panel, lbuf, dbuf, wbuf, cnt, lsem, dsem, wsem) = refs
        row = lax.axis_index("rows")
        chip, core = row // 2, row % 2
        labels = (order[2 * group], order[2 * group + 1])
        for q in range(2):
            pltpu.make_async_copy(diag_ref.at[labels[q]], dbuf.at[q], dsem.at[q]).start()
        for i in range(SB):
            slot = place_of(owner, order, SB + i, group)
            source = jnp.bitwise_xor(slot // SB, row)
            at = pl.multiple_of((slot % SB) * BS, BS)
            for m in range(8):
                @pl.when(source == m)
                def _(m=m, at=at, i=i):
                    pltpu.make_async_copy(l_refs[m].at[pl.ds(at, BS), :], lbuf.at[pl.ds(i * BS, BS), :], lsem).start()
        if not last:
            for q in range(2):
                cols = pl.ds(pl.multiple_of(labels[q] * SN, SN), SN)
                pltpu.make_async_copy(w_own.at[:, cols], wbuf.at[0, q], wsem.at[0, q]).start()
                pltpu.make_async_copy(w_other.at[:, cols], wbuf.at[1, q], wsem.at[1, q]).start()
        for c in range(4):
            cnt[c] = 0

        def one(i, carry):
            slot = place_of(owner, order, i, group)
            where = slot // (2 * SB)
            rank = cnt[where]
            cnt[where] = rank + 1
            rank = jnp.minimum(rank, SB - 1)
            rel = jnp.bitwise_xor(where, chip)
            full = pl.ds(pl.multiple_of(rank * BS, BS), BS)
            half = pl.ds(pl.multiple_of((rank % 4) * BS, BS), BS)
            dst = pl.ds(pl.multiple_of(i * BS, BS), BS)
            direct = rel == 1 + core
            same_half = rank // 4 == core

            @pl.when(rel == 0)
            def _():
                panel[dst, :] = p_own[full, :]

            @pl.when((rel == 1 + core) & (rel != 3))
            def _():
                panel[dst, :] = a_own[full, :]

            @pl.when((rel == 2 - core) & (rel != 3))
            def _():
                panel[dst, :] = a_swap[full, :]

            @pl.when((rel == 3) & same_half)
            def _():
                panel[dst, :] = b_own[half, :]

            @pl.when((rel == 3) & jnp.logical_not(same_half))
            def _():
                panel[dst, :] = b_swap[half, :]

            return carry

        lax.fori_loop(0, 2 * SB, one, 0)
        pltpu.make_async_copy(diag_ref.at[0], dbuf.at[0], dsem.at[0]).wait()
        x_a = jnp.dot(dbuf[0], panel[0:SN, :], preferred_element_type=F32).astype(BF16)
        x_ref[0:SN, :] = x_a
        pltpu.make_async_copy(l_refs[0], lbuf, lsem).wait()
        rest = panel[SN:PAIR, :].astype(F32) - jnp.dot(lbuf[...], x_a, preferred_element_type=F32)
        pltpu.make_async_copy(diag_ref.at[0], dbuf.at[1], dsem.at[1]).wait()
        x_b = jnp.dot(dbuf[1], rest.astype(BF16), preferred_element_type=F32).astype(BF16)
        x_ref[SN:PAIR, :] = x_b
        if last:
            return
        for side in range(2):
            rows = pattern[pl.ds(pl.multiple_of(jnp.bitwise_xor(row, side) * SB, SB), SB), :]
            total = resid_in[side * SN:(side + 1) * SN, :]
            for q, solved in enumerate((x_a, x_b)):
                mask = expand_mask(rows, labels[q] * SB, SN)
                pltpu.make_async_copy(w_own.at[:, pl.ds(0, SN)], wbuf.at[side, q], wsem.at[side, q]).wait()
                part = masked_rows(lambda j: wbuf[side, q, j * BS:(j + 1) * BS, :], mask, SB)
                total = total - jnp.dot(part, solved, preferred_element_type=F32)
            resid_ref[side * SN:(side + 1) * SN, :] = total
        pack_group(owner, order, resid_ref, p_ref, b_ref, cnt, group + 1)

    return kernel


def anc_kernel(order, x0, x1, x2, x3, a_ref, pattern, rhs_ref, sol_ref, out_ref):
    @pl.when(pl.program_id(0) == 0)
    def _():
        for k, x in enumerate((x0, x1, x2, x3)):
            for q in range(2):
                at = pl.multiple_of(order[2 * k + q] * SN, SN)
                sol_ref[pl.ds(at, SN), :] = x[q * SN:(q + 1) * SN, :]

    total = rhs_ref[...].astype(F32)
    rows = pattern[...]
    for s in range(NSUP):
        mask = expand_mask(rows, s * SB, SN)
        part = masked_rows(lambda j: a_ref[j * BS:(j + 1) * BS, s * SN:(s + 1) * SN], mask, SB)
        total = total - jnp.dot(part, sol_ref[s * SN:(s + 1) * SN, :], preferred_element_type=F32)
    out_ref[...] = total.astype(BF16)


SMEM = pl.BlockSpec(memory_space=pltpu.SMEM)
VMEM = pl.BlockSpec(memory_space=pltpu.VMEM)
ANY = pl.BlockSpec(memory_space=pl.ANY)
PARAMS = pltpu.CompilerParams(vmem_limit_bytes=40 * 1024 * 1024)


def shape_of(dims, dtype=BF16):
    return jax.ShapeDtypeStruct(dims, dtype)


def local(win_rows, anc_rows, win_pattern, anc_pattern, window_owner, sn_order, diag_inv, rhs_win, rhs_anc):
    rows_size = lax.axis_size("rows")
    if rows_size != 8:
        win_rhs = lax.all_to_all(rhs_win, "rhs", split_axis=1, concat_axis=0, tiled=True)
        anc_rhs = lax.all_to_all(rhs_anc, "rhs", split_axis=1, concat_axis=0, tiled=True)
        return general_path(win_rows, anc_rows, win_pattern, anc_pattern, window_owner, sn_order, diag_inv, win_rhs, anc_rhs)

    def swap(x, m):
        return lax.ppermute(x, "rows", [(i, i ^ m) for i in range(8)])

    def neighbour(x):
        return lax.ppermute(x, "rows", [(i, i ^ (2 if i % 2 == 0 else 4)) for i in range(8)])

    columns = rhs_win.shape[1] // lax.axis_size("rhs")
    win_rhs = lax.all_to_all(rhs_win, "rhs", split_axis=1, concat_axis=0, tiled=True)
    win_other = swap(win_rhs, 1)
    l_own = pl.pallas_call(
        factor_pack_kernel,
        out_shape=shape_of((SB * BS, SN)),
        in_specs=[SMEM, SMEM, VMEM, ANY],
        out_specs=VMEM,
        scratch_shapes=[pltpu.VMEM((SB * BS, SN), BF16), pltpu.SMEM((SB,), jnp.int32),
                        pltpu.SMEM((NSUP,), jnp.int32), pltpu.SemaphoreType.DMA],
        compiler_params=PARAMS,
        name="factor_pack",
    )(window_owner, sn_order, win_pattern, win_rows)
    l_parts = [None] * 8
    l_parts[0] = l_own
    for m in (2, 4, 6):
        l_parts[m] = swap(l_own, m)
    for m in (0, 2, 4, 6):
        l_parts[m + 1] = swap(l_parts[m], 1)
    w_other = swap(win_rows, 1)
    resid, packed, part = pl.pallas_call(
        first_pack_kernel,
        out_shape=(shape_of((PAIR, columns), F32), shape_of((SN, columns)), shape_of((SN // 2, columns))),
        in_specs=[SMEM, SMEM, VMEM, VMEM],
        out_specs=(VMEM, VMEM, VMEM),
        scratch_shapes=[pltpu.SMEM((1,), jnp.int32)],
        compiler_params=PARAMS,
        name="first_pack",
    )(window_owner, sn_order, win_rhs, win_other)
    anc_rhs = lax.all_to_all(rhs_anc, "rhs", split_axis=1, concat_axis=0, tiled=True)
    solved = []
    for group in range(GROUPS):
        a_own = neighbour(packed)
        b_own = swap(part, 6)
        a_swap = swap(a_own, 1)
        b_swap = swap(b_own, 1)
        last = group == GROUPS - 1
        operands = [window_owner, sn_order, win_pattern, packed, a_own, a_swap, b_own, b_swap, *l_parts, diag_inv]
        in_specs = [SMEM, SMEM] + [VMEM] * 6 + [ANY] * 9
        scratch = [pltpu.VMEM((PAIR, columns), BF16), pltpu.VMEM((SN, SN), BF16), pltpu.VMEM((2, SN, SN), BF16)]
        sems = [pltpu.SMEM((4,), jnp.int32), pltpu.SemaphoreType.DMA, pltpu.SemaphoreType.DMA((2,))]
        if last:
            out_shape = (shape_of((PAIR, columns)),)
        else:
            operands += [win_rows, w_other, resid]
            in_specs += [ANY, ANY, VMEM]
            scratch += [pltpu.VMEM((2, 2, SN, SN), BF16)]
            sems += [pltpu.SemaphoreType.DMA((2, 2))]
            out_shape = (shape_of((PAIR, columns)), shape_of((PAIR, columns), F32),
                         shape_of((SN, columns)), shape_of((SN // 2, columns)))
        results = pl.pallas_call(
            make_group_kernel(group),
            out_shape=out_shape,
            in_specs=in_specs,
            out_specs=(VMEM,) * len(out_shape),
            scratch_shapes=scratch + sems,
            compiler_params=PARAMS,
            name="pair_solve",
        )(*operands)
        solved.append(results[0])
        if not last:
            resid, packed, part = results[1:]

    anc_local = anc_rows.shape[0]
    tile = SB * BS
    chip_of = window_owner // (2 * SB)
    place = jnp.argsort(sn_order)
    group_of = jnp.repeat(place // 2, SB, total_repeat_length=NWB)
    same = (group_of[:, None] == group_of[None, :]) & (chip_of[:, None] == chip_of[None, :])
    fits = jnp.max(jnp.sum(same.astype(jnp.int32), axis=1)) <= SB

    def packed_path(*xs):
        return pl.pallas_call(
            anc_kernel,
            out_shape=(shape_of((NW, columns)), shape_of((anc_local, columns))),
            grid=(anc_local // tile,),
            in_specs=[SMEM] + [pl.BlockSpec((PAIR, columns), lambda i: (0, 0))] * 4 + [
                pl.BlockSpec((tile, NW), lambda i: (i, 0)),
                pl.BlockSpec((SB, NWB), lambda i: (i, 0)),
                pl.BlockSpec((tile, columns), lambda i: (i, 0)),
            ],
            out_specs=(pl.BlockSpec((NW, columns), lambda i: (0, 0)), pl.BlockSpec((tile, columns), lambda i: (i, 0))),
            compiler_params=PARAMS,
            name="rows_below",
        )(sn_order, *xs, anc_rows, anc_pattern, anc_rhs)

    def other_path(*xs):
        return general_path(win_rows, anc_rows, win_pattern, anc_pattern, window_owner, sn_order, diag_inv, win_rhs, anc_rhs)

    return tuple(lax.cond(fits, packed_path, other_path, *solved))


def solution(mesh):
    return jax.shard_map(
        local,
        mesh=mesh,
        in_specs=(P("rows", None), P("rows", None), P(), P("rows", None), P(), P(), P(),
                  P(("rows", "rhs"), None), P(("rows", "rhs"), None)),
        out_specs=(P(None, "rhs"), P("rows", "rhs")),
        check_vma=False,
    )
```

```python
import jax
import jax.numpy as jnp
from jax import lax
from jax.experimental import pallas as pl
from jax.experimental.pallas import tpu as pltpu
from jax.sharding import PartitionSpec as P

BS = 64
SB = 8
NSUP = 8
SN = 512
NW = 4096
NWB = 64
GROUPS = 4
PAIR = 2 * SN
F32 = jnp.float32
BF16 = jnp.bfloat16


def masked_columns(factor, pattern, node_label):
    blocks = pattern.shape[0]
    columns = lax.dynamic_slice_in_dim(factor, node_label * SN, SN, 1)
    chosen = lax.dynamic_slice_in_dim(pattern, node_label * SB, SB, 1)
    shaped = columns.reshape(blocks, BS, SB, BS) * chosen[:, None, :, None].astype(BF16)
    return shaped.reshape(blocks * BS, SN)


def sum_over_rows(values):
    count = lax.axis_size("rows")
    if count & (count - 1):
        return lax.psum(values, "rows")
    step = 1
    while step < count:
        values = values + lax.ppermute(values, "rows", [(i, i ^ step) for i in range(count)])
        step *= 2
    return values


def general_path(win_rows, anc_rows, win_pattern, anc_pattern, window_owner, sn_order, diag_inv, win_rhs, anc_rhs):
    columns_rhs = win_rhs.shape[1]
    slot_count = win_rows.shape[0] // BS
    first_slot = lax.axis_index("rows") * slot_count
    local_pattern = lax.dynamic_slice_in_dim(win_pattern, first_slot, slot_count, 0)

    def step(position, carry):
        solution, win_resid, anc_resid = carry
        node_label = sn_order[position]
        owners = lax.dynamic_slice_in_dim(window_owner, node_label * SB, SB, 0)
        inverse = lax.dynamic_index_in_dim(diag_inv, node_label, 0, keepdims=False)
        local_place = owners - first_slot
        present = (local_place >= 0) & (local_place < slot_count)
        resid_blocks = win_resid.reshape(slot_count, BS, columns_rhs)
        taken = jnp.take(resid_blocks, jnp.clip(local_place, 0, slot_count - 1), axis=0)
        placed = jnp.where(present[:, None, None], taken, 0.0).reshape(SN, columns_rhs)
        panel = sum_over_rows(placed.astype(BF16))
        solved = jnp.dot(inverse, panel, preferred_element_type=F32).astype(BF16)
        solution = lax.dynamic_update_slice_in_dim(solution, solved, node_label * SN, 0)
        win_part = jnp.dot(masked_columns(win_rows, local_pattern, node_label), solved, preferred_element_type=F32)
        anc_part = jnp.dot(masked_columns(anc_rows, anc_pattern, node_label), solved, preferred_element_type=F32)
        return solution, win_resid - win_part, anc_resid - anc_part

    first = (jnp.zeros((NW, columns_rhs), BF16), win_rhs.astype(F32), anc_rhs.astype(F32))
    solution, _, anc_resid = lax.fori_loop(0, NSUP, step, first)
    return solution, anc_resid.astype(BF16)


def spread_matrix():
    block_index = lax.broadcasted_iota(jnp.int32, (NWB, SN), 0)
    lane_index = lax.broadcasted_iota(jnp.int32, (NWB, SN), 1)
    return (block_index % SB == lane_index // BS).astype(F32).astype(BF16)


def expand_mask(rows_pattern, label, spread):
    lane = lax.broadcasted_iota(jnp.int32, rows_pattern.shape, 1)
    chosen = jnp.where(lane // SB == label, rows_pattern, 0).astype(F32).astype(BF16)
    return jnp.dot(chosen, spread, preferred_element_type=F32).astype(BF16)


def masked_rows(block_of, mask, count):
    return jnp.concatenate([block_of(j) * mask[j:j + 1, :] for j in range(count)], axis=0)


def rows_at(index):
    return pl.ds(pl.multiple_of(index * BS, BS), BS)


def columns_at(label):
    return pl.ds(pl.multiple_of(label * SN, SN), SN)


SRC, LSRC, PACK, TABLE = 0, 64, 96, 128


def first_kernel(owner, order, pattern, rhs_ref, win_ref, tab, flag, l0, l1, r0, r1, r2, r3,
                 buf, pat, cnt, dcnt, lslot, llab, sem):
    row, depth = lax.axis_index("rows"), lax.axis_index("rhs")
    chip, core = row // 2, row % 2
    width = r0.shape[1]
    for s, r in enumerate((r0, r1, r2, r3)):
        at = pl.multiple_of(jnp.bitwise_xor(depth, s) * width, width)
        r[...] = rhs_ref[:, pl.ds(at, width)]
    flag[0] = 0
    for t in range(SB):
        dcnt[t] = 0
        lslot[t] = 0
        llab[t] = 0
    for t in range(GROUPS * SB):
        tab[PACK + t] = 0
    for group in range(GROUPS):
        for t in range(4):
            cnt[t] = 0

        def one(i, carry, group=group):
            slot = owner[order[2 * group + i // SB] * SB + i % SB]
            where, device = slot // (2 * SB), slot // SB
            rank = cnt[where]
            cnt[where] = rank + 1
            flag[0] = jnp.where(rank >= SB, 1, flag[0])
            rank = jnp.minimum(rank, SB - 1)
            rel = jnp.bitwise_xor(where, chip)
            diagonal = rel == 3
            source = jnp.where(rel == 0, 0, jnp.where(diagonal, jnp.where(rank // 4 == core, 3, 4),
                                                      jnp.where(rel == 1 + core, 1, 2)))
            tab[SRC + group * 16 + i] = source * SB + jnp.where(diagonal, rank % 4, rank)

            @pl.when(rel == 0)
            def _():
                tab[PACK + group * SB + rank] = jnp.bitwise_xor(device % 2, core) * SB + slot % SB

            @pl.when(i >= SB)
            def _():
                index = dcnt[device]
                dcnt[device] = index + 1
                tab[LSRC + group * SB + i - SB] = jnp.bitwise_xor(device, row) * SB + index
                if group == 0:
                    flag[0] = jnp.where(index >= 4, 1, flag[0])

                @pl.when(device == row)
                def _():
                    lslot[index] = slot % SB
                    llab[index] = order[2 * group]

            return carry

        lax.fori_loop(0, 2 * SB, one, 0)
    labels = jnp.zeros((SB, 1), jnp.int32)
    for t in range(SB):
        slot, label = lslot[t], llab[t]
        pltpu.make_async_copy(win_ref.at[rows_at(slot), columns_at(label)], buf.at[pl.ds(t * BS, BS), :], sem).start()
        pat[t:t + 1, :] = pattern[pl.ds(row * SB + slot, 1), :]
        labels = jnp.where(lax.broadcasted_iota(jnp.int32, (SB, 1), 0) == t, label, labels)
    mask = expand_mask(pat[...], labels, spread_matrix())
    pltpu.make_async_copy(win_ref.at[:, pl.ds(0, SN)], buf, sem).wait()
    l0[...] = masked_rows(lambda j: buf[j * BS:(j + 1) * BS, :], mask[0:4], 4)
    l1[...] = masked_rows(lambda j: buf[(j + 4) * BS:(j + 5) * BS, :], mask[4:8], 4)


def first_pack_kernel(tab, *refs):
    pieces, (chip_rhs, p_ref, b_ref) = refs[:8], refs[8:]
    depth, core = lax.axis_index("rhs"), lax.axis_index("rows") % 2
    tall = pieces[0].shape[0]
    for side in range(2):
        for s in range(4):
            at = pl.multiple_of(side * SB * BS + jnp.bitwise_xor(depth, s) * tall, tall)
            chip_rhs[pl.ds(at, tall), :] = pieces[side * 4 + s][...]
    for j in range(SB):
        block = chip_rhs[rows_at(tab[PACK + j]), :]
        p_ref[j * BS:(j + 1) * BS, :] = block
    b_ref[...] = p_ref[pl.ds(pl.multiple_of(core * SB // 2 * BS, SB // 2 * BS), SB // 2 * BS), :]


def make_prep_kernel(group):
    last = group == GROUPS - 1

    def kernel(*refs):
        tab, order = refs[:2]
        l_refs, diag_ref = refs[2:18], refs[18]
        refs = refs[19:]
        if last:
            d_out, l_out, dsem, lsem = refs
        else:
            pattern, w_own, w_other, chip_rhs = refs[:4]
            xs = refs[4:4 + group]
            d_out, l_out, wn_out, r_out, wrow, pat, dsem, lsem, wsem = refs[4 + group:]
        for q in range(2):
            pltpu.make_async_copy(diag_ref.at[order[2 * group + q]], d_out.at[q], dsem.at[q]).start()
        if not last:
            for j in range(SB):
                place = tab[PACK + (group + 1) * SB + j]
                for side, w_ref in enumerate((w_own, w_other)):
                    @pl.when(place // SB == side)
                    def _(j=j, place=place, w_ref=w_ref):
                        pltpu.make_async_copy(w_ref.at[rows_at(place % SB), :], wrow.at[pl.ds(j * BS, BS), :], wsem).start()
        for i in range(SB):
            code = tab[LSRC + group * SB + i]
            for m in range(8):
                for half in range(1 if group == 0 else 2):
                    @pl.when((code // SB == m) & ((code % SB) // 4 == half) if group else code // SB == m)
                    def _(m=m, half=half, i=i, code=code):
                        pltpu.make_async_copy(l_refs[2 * m + half].at[rows_at(code % 4), :], l_out.at[pl.ds(i * BS, BS), :], lsem).start()
        if not last:
            row = lax.axis_index("rows")
            for j in range(SB):
                place = tab[PACK + (group + 1) * SB + j]
                pat[j:j + 1, :] = pattern[pl.ds(jnp.bitwise_xor(row, place // SB) * SB + place % SB, 1), :]
            spread = spread_matrix()
            rows = pat[...]
            total = jnp.concatenate([chip_rhs[rows_at(tab[PACK + (group + 1) * SB + j]), :] for j in range(SB)], axis=0).astype(F32)
            pltpu.make_async_copy(w_own, wrow, wsem).wait()
            for k in range(group + 1):
                for q in range(2):
                    label = order[2 * k + q]
                    mask = expand_mask(rows, label, spread)
                    part = masked_rows(lambda j: wrow[j * BS:(j + 1) * BS, columns_at(label)], mask, SB)
                    if k == group:
                        wn_out[:, q * SN:(q + 1) * SN] = part
                    else:
                        total = total - jnp.dot(part, xs[k][q * SN:(q + 1) * SN, :], preferred_element_type=F32)
            r_out[...] = total
        for q in range(2):
            pltpu.make_async_copy(diag_ref.at[0], d_out.at[q], dsem.at[q]).wait()
        pltpu.make_async_copy(diag_ref.at[0], l_out, lsem).wait()

    return kernel


def make_solve_kernel(group):
    last = group == GROUPS - 1

    def kernel(*refs):
        tab, sources, d_ref, l_ref = refs[0], refs[1:6], refs[6], refs[7]
        if last:
            x_ref, panel = refs[8:]
        else:
            wn_ref, r_ref, x_ref, p_ref, b_ref, panel = refs[8:]

        def place(i):
            code = tab[SRC + group * 16 + i]
            for which, source in enumerate(sources):
                @pl.when(code // SB == which)
                def _(source=source):
                    panel[rows_at(i), :] = source[rows_at(code % SB), :]

        for i in range(2 * SB):
            place(i)
        x_a = jnp.dot(d_ref[0], panel[0:SN, :], preferred_element_type=F32).astype(BF16)
        x_ref[0:SN, :] = x_a
        rest = panel[SN:PAIR, :].astype(F32) - jnp.dot(l_ref[...], x_a, preferred_element_type=F32)
        x_b = jnp.dot(d_ref[1], rest.astype(BF16), preferred_element_type=F32).astype(BF16)
        x_ref[SN:PAIR, :] = x_b
        if last:
            return
        total = r_ref[...] - jnp.dot(wn_ref[:, 0:SN], x_a, preferred_element_type=F32)
        total = total - jnp.dot(wn_ref[:, SN:PAIR], x_b, preferred_element_type=F32)
        p_ref[...] = total.astype(BF16)
        core = lax.axis_index("rows") % 2
        b_ref[...] = p_ref[pl.ds(pl.multiple_of(core * SB // 2 * BS, SB // 2 * BS), SB // 2 * BS), :]

    return kernel


def pair_product(a0, a1, pattern, x_ref, order, group):
    spread = spread_matrix()
    rows = pattern[...]
    total = None
    for q, a_ref in enumerate((a0, a1)):
        mask = expand_mask(rows, order[2 * group + q], spread)
        part = masked_rows(lambda j: a_ref[j * BS:(j + 1) * BS, :], mask, a_ref.shape[0] // BS)
        term = jnp.dot(part, x_ref[q * SN:(q + 1) * SN, :], preferred_element_type=F32)
        total = term if total is None else total + term
    return total


def make_rows_kernel(group):
    def kernel(order, a0, a1, pattern, x_ref, *refs):
        total = pair_product(a0, a1, pattern, x_ref, order, group)
        refs[-1][...] = total if group == 0 else refs[0][...] + total

    return kernel


def last_rows_kernel(order, a0, a1, pattern, x0, x1, x2, x3, sums, h0, h1, h2, h3, sol_ref, out_ref, sems):
    step = pl.program_id(0)
    copies = []
    for k, x in enumerate((x0, x1, x2, x3)):
        for q in range(2):
            at = pl.multiple_of(order[2 * k + q] * SN, SN)
            copies.append(pltpu.make_async_copy(x.at[pl.ds(q * SN, SN), :], sol_ref.at[pl.ds(at, SN), :], sems.at[2 * k + q]))

    @pl.when(step == 0)
    def _():
        for c in copies:
            c.start()

    total = sums[...] + pair_product(a0, a1, pattern, x3, order, GROUPS - 1)
    which = jnp.bitwise_xor(lax.axis_index("rhs"), step)
    for s, h in enumerate((h0, h1, h2, h3)):
        @pl.when(which == s)
        def _(h=h):
            out_ref[...] = (h[...].astype(F32) - total).astype(BF16)

    @pl.when(step == pl.num_programs(0) - 1)
    def _():
        for c in copies:
            c.wait()


SMEM = pl.BlockSpec(memory_space=pltpu.SMEM)
VMEM = pl.BlockSpec(memory_space=pltpu.VMEM)
HBM = pl.BlockSpec(memory_space=pltpu.HBM)


def params(mib):
    return pltpu.CompilerParams(vmem_limit_bytes=mib * 1024 * 1024)


def shape_of(dims, dtype=BF16):
    return jax.ShapeDtypeStruct(dims, dtype)


def local(win_rows, anc_rows, win_pattern, anc_pattern, window_owner, sn_order, diag_inv, rhs_win, rhs_anc):
    if lax.axis_size("rows") != 8 or lax.axis_size("rhs") != 4 or anc_rows.shape[0] != 4 * SB * BS:
        win_rhs = lax.all_to_all(rhs_win, "rhs", split_axis=1, concat_axis=0, tiled=True)
        anc_rhs = lax.all_to_all(rhs_anc, "rhs", split_axis=1, concat_axis=0, tiled=True)
        return general_path(win_rows, anc_rows, win_pattern, anc_pattern, window_owner, sn_order, diag_inv, win_rhs, anc_rhs)

    def swap(x, m):
        return lax.ppermute(x, "rows", [(i, i ^ m) for i in range(8)])

    def deep(x, m):
        return lax.ppermute(x, "rhs", [(i, i ^ m) for i in range(4)])

    def neighbour(x):
        return lax.ppermute(x, "rows", [(i, i ^ (2 if i % 2 == 0 else 4)) for i in range(8)])

    columns = rhs_win.shape[1] // 4
    half = SN // 2
    w_other = swap(win_rows, 1)
    tall = rhs_win.shape[0]
    tab, flag, l_low, l_high, *sent = pl.pallas_call(
        first_kernel,
        out_shape=(shape_of((TABLE,), jnp.int32), shape_of((1,), jnp.int32), shape_of((half, SN)), shape_of((half, SN)))
        + (shape_of((tall, columns)),) * 4,
        in_specs=[SMEM, SMEM, VMEM, VMEM, HBM],
        out_specs=(SMEM, SMEM) + (VMEM,) * 6,
        scratch_shapes=[pltpu.VMEM((SN, SN), BF16), pltpu.VMEM((SB, NWB), jnp.int32), pltpu.SMEM((4,), jnp.int32),
                        pltpu.SMEM((SB,), jnp.int32), pltpu.SMEM((SB,), jnp.int32), pltpu.SMEM((SB,), jnp.int32),
                        pltpu.SemaphoreType.DMA],
        compiler_params=params(8),
        name="first",
    )(window_owner, sn_order, win_pattern, rhs_win, win_rows)

    low, high = {0: l_low}, {0: l_high}
    for m in (2, 4, 6):
        low[m] = swap(l_low, m)
    pieces = [sent[0]] + [deep(sent[s], s) for s in (1, 2, 3)]
    others = [swap(x, 1) for x in pieces]
    for m in (0, 2, 4, 6):
        low[m + 1] = swap(low[m], 1)
    chip_rhs, packed, part = pl.pallas_call(
        first_pack_kernel,
        out_shape=(shape_of((PAIR, columns)), shape_of((SN, columns)), shape_of((half, columns))),
        in_specs=[SMEM] + [VMEM] * 8,
        out_specs=(VMEM,) * 3,
        compiler_params=params(6),
        name="first_pack",
    )(tab, *pieces, *others)

    depth = lax.axis_index("rhs")
    tile = rhs_anc.shape[0]
    sums, anc_pieces, solved = None, None, []
    for group in range(GROUPS):
        last = group == GROUPS - 1
        a_own = neighbour(packed)
        b_own = swap(part, 6)
        if group == 0:
            for m in (2, 4, 6):
                high[m] = swap(l_high, m)
            for m in (0, 2, 4, 6):
                high[m + 1] = swap(high[m], 1)
            l_parts = [x for m in range(8) for x in (low[m], low[m])]
        else:
            l_parts = [x for m in range(8) for x in (low[m], high[m])]
        if group == 1:
            anc_pieces = [lax.dynamic_slice_in_dim(rhs_anc, (depth ^ s) * columns, columns, 1) for s in range(4)]
            anc_pieces = anc_pieces[:1] + [deep(anc_pieces[s], s) for s in (1, 2, 3)]
        a_swap = swap(a_own, 1)
        b_swap = swap(b_own, 1)

        operands = [tab, sn_order, *l_parts, diag_inv]
        in_specs = [SMEM, SMEM] + [HBM] * 17
        out_shape = [shape_of((2, SN, SN)), shape_of((SN, SN))]
        scratch = []
        sems = [pltpu.SemaphoreType.DMA((2,)), pltpu.SemaphoreType.DMA]
        if not last:
            operands += [win_pattern, win_rows, w_other, chip_rhs, *solved]
            in_specs += [VMEM, HBM, HBM] + [VMEM] * (1 + group)
            out_shape += [shape_of((SN, PAIR)), shape_of((SN, columns), F32)]
            scratch = [pltpu.VMEM((SN, NW), BF16), pltpu.VMEM((SB, NWB), jnp.int32)]
            sems += [pltpu.SemaphoreType.DMA]
        ready = pl.pallas_call(
            make_prep_kernel(group),
            out_shape=tuple(out_shape),
            in_specs=in_specs,
            out_specs=(VMEM,) * len(out_shape),
            scratch_shapes=scratch + sems,
            compiler_params=params(16),
            name="prep",
        )(*operands)
        if group > 0:
            k = group - 1
            more = [] if k == 0 else [sums]
            sums = pl.pallas_call(
                make_rows_kernel(k),
                out_shape=shape_of((anc_rows.shape[0], columns), F32),
                grid_spec=pltpu.PrefetchScalarGridSpec(
                    num_scalar_prefetch=1,
                    grid=(anc_rows.shape[0] // tile,),
                    in_specs=[pl.BlockSpec((tile, SN), lambda i, o, k=k: (i, o[2 * k])),
                              pl.BlockSpec((tile, SN), lambda i, o, k=k: (i, o[2 * k + 1])),
                              pl.BlockSpec((SB, NWB), lambda i, o: (i, 0)),
                              pl.BlockSpec((PAIR, columns), lambda i, o: (0, 0))]
                    + [pl.BlockSpec((tile, columns), lambda i, o: (i, 0))] * len(more),
                    out_specs=pl.BlockSpec((tile, columns), lambda i, o: (i, 0)),
                ),
                input_output_aliases={5: 0} if more else {},
                compiler_params=params(12),
                name="rows_below",
            )(sn_order, anc_rows, anc_rows, anc_pattern, solved[k], *more)

        out_shape = [shape_of((PAIR, columns))]
        if not last:
            out_shape += [shape_of((SN, columns)), shape_of((half, columns))]
        results = pl.pallas_call(
            make_solve_kernel(group),
            out_shape=tuple(out_shape),
            in_specs=[SMEM] + [VMEM] * (5 + len(ready)),
            out_specs=(VMEM,) * len(out_shape),
            scratch_shapes=[pltpu.VMEM((PAIR, columns), BF16)],
            compiler_params=params(12),
            name="pair_solve",
        )(tab, packed, a_own, a_swap, b_own, b_swap, *ready)
        solved.append(results[0])
        if not last:
            packed, part = results[1:]

    def packed_path(*xs):
        k = GROUPS - 1
        whole = [pl.BlockSpec((PAIR, columns), lambda i, o: (0, 0))] * 4
        return pl.pallas_call(
            last_rows_kernel,
            out_shape=(shape_of((NW, columns)), shape_of((anc_rows.shape[0], columns))),
            grid_spec=pltpu.PrefetchScalarGridSpec(
                num_scalar_prefetch=1,
                grid=(anc_rows.shape[0] // tile,),
                in_specs=[pl.BlockSpec((tile, SN), lambda i, o: (i, o[2 * k])),
                          pl.BlockSpec((tile, SN), lambda i, o: (i, o[2 * k + 1])),
                          pl.BlockSpec((SB, NWB), lambda i, o: (i, 0))] + whole
                + [pl.BlockSpec((tile, columns), lambda i, o: (i, 0))]
                + [pl.BlockSpec((tile, columns), lambda i, o: (0, 0))] * 4,
                out_specs=(HBM, pl.BlockSpec((tile, columns), lambda i, o: (i, 0))),
                scratch_shapes=[pltpu.SemaphoreType.DMA((2 * GROUPS,))],
            ),
            compiler_params=params(24),
            name="last_rows",
        )(sn_order, anc_rows, anc_rows, anc_pattern, *xs, sums, *anc_pieces)

    def other_path(*xs):
        back = depth ^ jnp.arange(4)
        win_rhs = jnp.take(jnp.stack(pieces), back, axis=0).reshape(4 * tall, columns)
        anc_rhs = jnp.take(jnp.stack(anc_pieces), back, axis=0).reshape(4 * tile, columns)
        return general_path(win_rows, anc_rows, win_pattern, anc_pattern, window_owner, sn_order, diag_inv, win_rhs, anc_rhs)

    return tuple(lax.cond(flag[0] == 0, packed_path, other_path, *solved))


def solution(mesh):
    return jax.shard_map(
        local,
        mesh=mesh,
        in_specs=(P("rows", None), P("rows", None), P(), P("rows", None), P(), P(), P(),
                  P(("rows", "rhs"), None), P(("rows", "rhs"), None)),
        out_specs=(P(None, "rhs"), P("rows", "rhs")),
        check_vma=False,
    )
```

```python
import jax
import jax.numpy as jnp
from jax import lax
from jax.experimental import pallas as pl
from jax.experimental.pallas import tpu as pltpu
from jax.sharding import PartitionSpec as P

BS = 64
SB = 8
NSUP = 8
SN = 512
NW = 4096
NWB = 64
GROUPS = 4
PAIR = 2 * SN
F32 = jnp.float32
BF16 = jnp.bfloat16


def masked_columns(factor, pattern, node_label):
    blocks = pattern.shape[0]
    columns = lax.dynamic_slice_in_dim(factor, node_label * SN, SN, 1)
    chosen = lax.dynamic_slice_in_dim(pattern, node_label * SB, SB, 1)
    shaped = columns.reshape(blocks, BS, SB, BS) * chosen[:, None, :, None].astype(BF16)
    return shaped.reshape(blocks * BS, SN)


def sum_over_rows(values):
    count = lax.axis_size("rows")
    if count & (count - 1):
        return lax.psum(values, "rows")
    step = 1
    while step < count:
        values = values + lax.ppermute(values, "rows", [(i, i ^ step) for i in range(count)])
        step *= 2
    return values


def general_path(win_rows, anc_rows, win_pattern, anc_pattern, window_owner, sn_order, diag_inv, win_rhs, anc_rhs):
    columns_rhs = win_rhs.shape[1]
    slot_count = win_rows.shape[0] // BS
    first_slot = lax.axis_index("rows") * slot_count
    local_pattern = lax.dynamic_slice_in_dim(win_pattern, first_slot, slot_count, 0)

    def step(position, carry):
        solution, win_resid, anc_resid = carry
        node_label = sn_order[position]
        owners = lax.dynamic_slice_in_dim(window_owner, node_label * SB, SB, 0)
        inverse = lax.dynamic_index_in_dim(diag_inv, node_label, 0, keepdims=False)
        local_place = owners - first_slot
        present = (local_place >= 0) & (local_place < slot_count)
        resid_blocks = win_resid.reshape(slot_count, BS, columns_rhs)
        taken = jnp.take(resid_blocks, jnp.clip(local_place, 0, slot_count - 1), axis=0)
        placed = jnp.where(present[:, None, None], taken, 0.0).reshape(SN, columns_rhs)
        panel = sum_over_rows(placed.astype(BF16))
        solved = jnp.dot(inverse, panel, preferred_element_type=F32).astype(BF16)
        solution = lax.dynamic_update_slice_in_dim(solution, solved, node_label * SN, 0)
        win_part = jnp.dot(masked_columns(win_rows, local_pattern, node_label), solved, preferred_element_type=F32)
        anc_part = jnp.dot(masked_columns(anc_rows, anc_pattern, node_label), solved, preferred_element_type=F32)
        return solution, win_resid - win_part, anc_resid - anc_part

    first = (jnp.zeros((NW, columns_rhs), BF16), win_rhs.astype(F32), anc_rhs.astype(F32))
    solution, _, anc_resid = lax.fori_loop(0, NSUP, step, first)
    return solution, anc_resid.astype(BF16)


def spread_matrix():
    block_index = lax.broadcasted_iota(jnp.int32, (NWB, SN), 0)
    lane_index = lax.broadcasted_iota(jnp.int32, (NWB, SN), 1)
    return (block_index % SB == lane_index // BS).astype(F32).astype(BF16)


def expand_mask(rows_pattern, label, spread):
    lane = lax.broadcasted_iota(jnp.int32, rows_pattern.shape, 1)
    chosen = jnp.where(lane // SB == label, rows_pattern, 0).astype(F32).astype(BF16)
    return jnp.dot(chosen, spread, preferred_element_type=F32).astype(BF16)


def masked_rows(block_of, mask, count):
    return jnp.concatenate([block_of(j) * mask[j:j + 1, :] for j in range(count)], axis=0)


def rows_at(index):
    return pl.ds(pl.multiple_of(index * BS, BS), BS)


def columns_at(label):
    return pl.ds(pl.multiple_of(label * SN, SN), SN)


SRC, LSRC, PACK, TABLE = 0, 64, 96, 128


def first_kernel(owner, order, pattern, rhs_ref, win_ref, l0, l1, r0, r1, r2, r3, buf, pat, inv, pos, sem):
    row, depth = lax.axis_index("rows"), lax.axis_index("rhs")
    width = r0.shape[1]

    def note_slot(w, carry):
        slot = owner[w]

        @pl.when(slot // SB == row)
        def _():
            inv[slot % SB] = w

        return carry

    lax.fori_loop(0, NWB, note_slot, 0)
    for k in range(NSUP):
        pos[order[k]] = k
    labels = jnp.zeros((SB, 1), jnp.int32)
    for t in range(SB):
        label = order[(pos[inv[t] // SB] // 2) * 2]
        pltpu.make_async_copy(win_ref.at[pl.ds(t * BS, BS), columns_at(label)], buf.at[pl.ds(t * BS, BS), :], sem).start()
        labels = jnp.where(lax.broadcasted_iota(jnp.int32, (SB, 1), 0) == t, label, labels)
    for s, r in enumerate((r0, r1, r2, r3)):
        at = pl.multiple_of(jnp.bitwise_xor(depth, s) * width, width)
        r[...] = rhs_ref[:, pl.ds(at, width)]
    pat[...] = pattern[pl.ds(pl.multiple_of(row * SB, SB), SB), :]
    mask = expand_mask(pat[...], labels, spread_matrix())
    pltpu.make_async_copy(win_ref.at[:, pl.ds(0, SN)], buf, sem).wait()
    l0[...] = masked_rows(lambda j: buf[j * BS:(j + 1) * BS, :], mask[0:4], 4)
    l1[...] = masked_rows(lambda j: buf[(j + 4) * BS:(j + 5) * BS, :], mask[4:8], 4)


def table_kernel(owner, order, tab, flag, cnt):
    row = lax.axis_index("rows")
    chip, core = row // 2, row % 2
    flag[0] = 0
    for t in range(GROUPS * SB):
        tab[PACK + t] = 0
    for group in range(GROUPS):
        for t in range(4):
            cnt[t] = 0

        def one(i, carry, group=group):
            slot = owner[order[2 * group + i // SB] * SB + i % SB]
            where, device = slot // (2 * SB), slot // SB
            rank = cnt[where]
            cnt[where] = rank + 1
            flag[0] = jnp.where(rank >= SB, 1, flag[0])
            rank = jnp.minimum(rank, SB - 1)
            rel = jnp.bitwise_xor(where, chip)
            diagonal = rel == 3
            source = jnp.where(rel == 0, 0, jnp.where(diagonal, jnp.where(rank // 4 == core, 3, 4),
                                                      jnp.where(rel == 1 + core, 1, 2)))
            tab[SRC + group * 16 + i] = source * SB + jnp.where(diagonal, rank % 4, rank)

            @pl.when(rel == 0)
            def _():
                tab[PACK + group * SB + rank] = jnp.bitwise_xor(device % 2, core) * SB + slot % SB

            @pl.when(i >= SB)
            def _():
                tab[LSRC + group * SB + i - SB] = jnp.bitwise_xor(device, row) * SB + slot % SB

            return carry

        lax.fori_loop(0, 2 * SB, one, 0)


def first_pack_kernel(tab, *refs):
    pieces, (chip_rhs, p_ref, b_ref) = refs[:8], refs[8:]
    depth, core = lax.axis_index("rhs"), lax.axis_index("rows") % 2
    tall = pieces[0].shape[0]
    for side in range(2):
        for s in range(4):
            at = pl.multiple_of(side * SB * BS + jnp.bitwise_xor(depth, s) * tall, tall)
            chip_rhs[pl.ds(at, tall), :] = pieces[side * 4 + s][...]
    for j in range(SB):
        block = chip_rhs[rows_at(tab[PACK + j]), :]
        p_ref[j * BS:(j + 1) * BS, :] = block
    b_ref[...] = p_ref[pl.ds(pl.multiple_of(core * SB // 2 * BS, SB // 2 * BS), SB // 2 * BS), :]


def make_mask_kernel(group):
    def kernel(tab, order, pattern, w_own, w_other, out, wrow, pat, sem):
        row = lax.axis_index("rows")
        for j in range(SB):
            place = tab[PACK + (group + 1) * SB + j]
            for side, w_ref in enumerate((w_own, w_other)):
                @pl.when(place // SB == side)
                def _(j=j, place=place, w_ref=w_ref):
                    pltpu.make_async_copy(w_ref.at[rows_at(place % SB), :], wrow.at[pl.ds(j * BS, BS), :], sem).start()
            pat[j:j + 1, :] = pattern[pl.ds(jnp.bitwise_xor(row, place // SB) * SB + place % SB, 1), :]
        spread = spread_matrix()
        rows = pat[...]
        masks = [expand_mask(rows, order[k], spread) for k in range(2 * group + 2)]
        pltpu.make_async_copy(w_own, wrow, sem).wait()
        for k in range(2 * group + 2):
            for j in range(SB):
                at = slice(j * BS, (j + 1) * BS)
                out[at, k * SN:(k + 1) * SN] = wrow[at, columns_at(order[k])] * masks[k][j:j + 1, :]

    return kernel


def make_prep_kernel(group):
    last = group == GROUPS - 1

    def kernel(*refs):
        tab, order = refs[:2]
        l_refs, diag_ref = refs[2:18], refs[18]
        refs = refs[19:]
        if last:
            d_out, l_out, dsem, lsem = refs
        else:
            w_ref, chip_rhs = refs[:2]
            xs = refs[2:2 + group]
            d_out, l_out, r_out, dsem, lsem = refs[2 + group:]
        for q in range(2):
            pltpu.make_async_copy(diag_ref.at[order[2 * group + q]], d_out.at[q], dsem.at[q]).start()
        for i in range(SB):
            code = tab[LSRC + group * SB + i]
            for m in range(8):
                @pl.when(code // SB == m)
                def _(m=m, i=i, code=code):
                    for half in range(2):
                        @pl.when((code % SB) // 4 == half)
                        def _(half=half):
                            pltpu.make_async_copy(l_refs[2 * m + half].at[rows_at(code % 4), :], l_out.at[pl.ds(i * BS, BS), :], lsem).start()
        if not last:
            total = jnp.concatenate([chip_rhs[rows_at(tab[PACK + (group + 1) * SB + j]), :] for j in range(SB)], axis=0).astype(F32)
            for k in range(group):
                total = total - jnp.dot(w_ref[:, k * PAIR:(k + 1) * PAIR], xs[k][...], preferred_element_type=F32)
            r_out[...] = total
        for q in range(2):
            pltpu.make_async_copy(diag_ref.at[0], d_out.at[q], dsem.at[q]).wait()
        pltpu.make_async_copy(diag_ref.at[0], l_out, lsem).wait()

    return kernel


def make_solve_kernel(group):
    last = group == GROUPS - 1

    def kernel(*refs):
        tab, sources, d_ref, l_ref = refs[0], refs[1:6], refs[6], refs[7]
        if last:
            x_ref, panel = refs[8:]
        else:
            r_ref, wn_ref, x_ref, p_ref, b_ref, panel = refs[8:]

        def place(i):
            code = tab[SRC + group * 16 + i]
            for which, source in enumerate(sources):
                @pl.when(code // SB == which)
                def _(source=source):
                    panel[rows_at(i), :] = source[rows_at(code % SB), :]

        for i in range(2 * SB):
            place(i)
        x_a = jnp.dot(d_ref[0], panel[0:SN, :], preferred_element_type=F32).astype(BF16)
        x_ref[0:SN, :] = x_a
        rest = panel[SN:PAIR, :].astype(F32) - jnp.dot(l_ref[...], x_a, preferred_element_type=F32)
        x_b = jnp.dot(d_ref[1], rest.astype(BF16), preferred_element_type=F32).astype(BF16)
        x_ref[SN:PAIR, :] = x_b
        if last:
            return
        total = r_ref[...] - jnp.dot(wn_ref[:, group * PAIR:(group + 1) * PAIR], x_ref[...], preferred_element_type=F32)
        p_ref[...] = total.astype(BF16)
        core = lax.axis_index("rows") % 2
        b_ref[...] = p_ref[pl.ds(pl.multiple_of(core * SB // 2 * BS, SB // 2 * BS), SB // 2 * BS), :]

    return kernel


def pair_product(a0, a1, pattern, x_ref, order, group):
    spread = spread_matrix()
    rows = pattern[...]
    total = None
    for q, a_ref in enumerate((a0, a1)):
        mask = expand_mask(rows, order[2 * group + q], spread)
        part = masked_rows(lambda j: a_ref[j * BS:(j + 1) * BS, :], mask, a_ref.shape[0] // BS)
        term = jnp.dot(part, x_ref[q * SN:(q + 1) * SN, :], preferred_element_type=F32)
        total = term if total is None else total + term
    return total


def make_rows_kernel(group):
    def kernel(order, a0, a1, pattern, x_ref, *refs):
        total = pair_product(a0, a1, pattern, x_ref, order, group)
        refs[-1][...] = total if group == 0 else refs[0][...] + total

    return kernel


def last_rows_kernel(order, a0, a1, pattern, x0, x1, x2, x3, sums, h0, h1, h2, h3, sol_ref, out_ref, sems):
    step = pl.program_id(0)
    copies = []
    for k, x in enumerate((x0, x1, x2, x3)):
        for q in range(2):
            at = pl.multiple_of(order[2 * k + q] * SN, SN)
            copies.append(pltpu.make_async_copy(x.at[pl.ds(q * SN, SN), :], sol_ref.at[pl.ds(at, SN), :], sems.at[2 * k + q]))

    @pl.when(step == 0)
    def _():
        for c in copies:
            c.start()

    total = sums[...] + pair_product(a0, a1, pattern, x3, order, GROUPS - 1)
    which = jnp.bitwise_xor(lax.axis_index("rhs"), step)
    for s, h in enumerate((h0, h1, h2, h3)):
        @pl.when(which == s)
        def _(h=h):
            out_ref[...] = (h[...].astype(F32) - total).astype(BF16)

    @pl.when(step == pl.num_programs(0) - 1)
    def _():
        for c in copies:
            c.wait()


SMEM = pl.BlockSpec(memory_space=pltpu.SMEM)
VMEM = pl.BlockSpec(memory_space=pltpu.VMEM)
HBM = pl.BlockSpec(memory_space=pltpu.HBM)


def params(mib):
    return pltpu.CompilerParams(vmem_limit_bytes=mib * 1024 * 1024)


def cost(micros):
    return pl.CostEstimate(flops=micros * 10 ** 8, bytes_accessed=micros * 3 * 10 ** 6, transcendentals=0)


def shape_of(dims, dtype=BF16):
    return jax.ShapeDtypeStruct(dims, dtype)


def local(win_rows, anc_rows, win_pattern, anc_pattern, window_owner, sn_order, diag_inv, rhs_win, rhs_anc):
    if lax.axis_size("rows") != 8 or lax.axis_size("rhs") != 4 or anc_rows.shape[0] != 4 * SB * BS:
        win_rhs = lax.all_to_all(rhs_win, "rhs", split_axis=1, concat_axis=0, tiled=True)
        anc_rhs = lax.all_to_all(rhs_anc, "rhs", split_axis=1, concat_axis=0, tiled=True)
        return general_path(win_rows, anc_rows, win_pattern, anc_pattern, window_owner, sn_order, diag_inv, win_rhs, anc_rhs)

    def swap(x, m):
        return lax.ppermute(x, "rows", [(i, i ^ m) for i in range(8)])

    def deep(x, m):
        return lax.ppermute(x, "rhs", [(i, i ^ m) for i in range(4)])

    def neighbour(x):
        return lax.ppermute(x, "rows", [(i, i ^ (2 if i % 2 == 0 else 4)) for i in range(8)])

    columns = rhs_win.shape[1] // 4
    half = SN // 2
    w_other = swap(win_rows, 1)
    tall = rhs_win.shape[0]
    l_low, l_high, *sent = pl.pallas_call(
        first_kernel,
        out_shape=(shape_of((half, SN)), shape_of((half, SN))) + (shape_of((tall, columns)),) * 4,
        in_specs=[SMEM, SMEM, VMEM, VMEM, HBM],
        out_specs=(VMEM,) * 6,
        scratch_shapes=[pltpu.VMEM((SN, SN), BF16), pltpu.VMEM((SB, NWB), jnp.int32),
                        pltpu.SMEM((SB,), jnp.int32), pltpu.SMEM((SB,), jnp.int32), pltpu.SemaphoreType.DMA],
        compiler_params=params(8),
        cost_estimate=cost(2),
        name="first",
    )(window_owner, sn_order, win_pattern, rhs_win, win_rows)
    low, high = {0: l_low}, {0: l_high}
    for m in (2, 4):
        low[m] = swap(l_low, m)
    pieces = [sent[0]] + [deep(sent[s], s) for s in (1, 2, 3)]
    for m in (2, 4):
        high[m] = swap(l_high, m)
    tab, flag = pl.pallas_call(
        table_kernel,
        out_shape=(shape_of((TABLE,), jnp.int32), shape_of((1,), jnp.int32)),
        in_specs=[SMEM, SMEM],
        out_specs=(SMEM, SMEM),
        scratch_shapes=[pltpu.SMEM((4,), jnp.int32)],
        compiler_params=params(4),
        cost_estimate=cost(2),
        name="tables",
    )(window_owner, sn_order)
    others = [swap(x, 1) for x in pieces]
    chip_rhs, packed, part = pl.pallas_call(
        first_pack_kernel,
        out_shape=(shape_of((PAIR, columns)), shape_of((SN, columns)), shape_of((half, columns))),
        in_specs=[SMEM] + [VMEM] * 8,
        out_specs=(VMEM,) * 3,
        compiler_params=params(6),
        cost_estimate=cost(1),
        name="first_pack",
    )(tab, *pieces, *others)
    low[6], high[6] = swap(low[2], 4), swap(high[4], 2)
    for m in (0, 2, 4, 6):
        low[m + 1] = swap(low[m], 1)
        high[m + 1] = swap(high[m], 1)
    l_parts = [x for m in range(8) for x in (low[m], high[m])]

    depth = lax.axis_index("rhs")
    tile = rhs_anc.shape[0]
    sums, solved, masked = None, [], []
    anc_order, anc_pieces = (2, 3, 1), [None] * 4
    tab_later, rhs_later = tab, rhs_anc
    for group in range(GROUPS):
        last = group == GROUPS - 1
        a_own = neighbour(packed)
        b_own = swap(part, 6)
        hold = [a_own, b_own]
        if group == 0:
            tab_later, _ = lax.optimization_barrier((tab, packed))
            for k in range(GROUPS - 1):
                masked.append(pl.pallas_call(
                    make_mask_kernel(k),
                    out_shape=shape_of((SN, (k + 1) * PAIR)),
                    in_specs=[SMEM, SMEM, VMEM, HBM, HBM],
                    out_specs=VMEM,
                    scratch_shapes=[pltpu.VMEM((SN, NW), BF16), pltpu.VMEM((SB, NWB), jnp.int32), pltpu.SemaphoreType.DMA],
                    compiler_params=params(10),
                    cost_estimate=cost(3),
                    name="mask_rows",
                )(tab_later, sn_order, win_pattern, win_rows, w_other))
            hold += masked
        if not last:
            rhs_later, _ = lax.optimization_barrier((rhs_later, packed))
            s = anc_order[group]
            anc_pieces[s] = deep(lax.dynamic_slice_in_dim(rhs_later, (depth ^ s) * columns, columns, 1), s)
            if group == 2:
                anc_pieces[0] = lax.dynamic_slice_in_dim(rhs_later, depth * columns, columns, 1)

        operands = [tab, sn_order, *l_parts, diag_inv]
        in_specs = [SMEM, SMEM] + [HBM] * 17
        out_shape = [shape_of((2, SN, SN)), shape_of((SN, SN))]
        if not last:
            operands += [masked[group], chip_rhs, *solved]
            in_specs += [VMEM] * (2 + group)
            out_shape += [shape_of((SN, columns), F32)]
        ready = pl.pallas_call(
            make_prep_kernel(group),
            out_shape=tuple(out_shape),
            in_specs=in_specs,
            out_specs=(VMEM,) * len(out_shape),
            scratch_shapes=[pltpu.SemaphoreType.DMA((2,)), pltpu.SemaphoreType.DMA],
            compiler_params=params(8),
            cost_estimate=cost(2),
            name="prep",
        )(*operands)
        if group > 0:
            k = group - 1
            more = [] if k == 0 else [sums]
            sums = pl.pallas_call(
                make_rows_kernel(k),
                out_shape=shape_of((anc_rows.shape[0], columns), F32),
                grid_spec=pltpu.PrefetchScalarGridSpec(
                    num_scalar_prefetch=1,
                    grid=(anc_rows.shape[0] // (2 * tile),),
                    in_specs=[pl.BlockSpec((2 * tile, SN), lambda i, o, k=k: (i, o[2 * k])),
                              pl.BlockSpec((2 * tile, SN), lambda i, o, k=k: (i, o[2 * k + 1])),
                              pl.BlockSpec((2 * SB, NWB), lambda i, o: (i, 0)),
                              pl.BlockSpec((PAIR, columns), lambda i, o: (0, 0))]
                    + [pl.BlockSpec((2 * tile, columns), lambda i, o: (i, 0))] * len(more),
                    out_specs=pl.BlockSpec((2 * tile, columns), lambda i, o: (i, 0)),
                ),
                input_output_aliases={5: 0} if more else {},
                compiler_params=params(14),
                cost_estimate=cost(5),
                name="rows_below",
            )(sn_order, anc_rows, anc_rows, anc_pattern, solved[k], *more)
            previous = anc_pieces[anc_order[k]]
            a_own, b_own, sums, previous, *ready = lax.optimization_barrier((a_own, b_own, sums, previous, *ready))
            anc_pieces[anc_order[k]] = previous
        else:
            a_own, b_own, *masked = lax.optimization_barrier((a_own, b_own, *masked))
        a_swap = swap(a_own, 1)
        b_swap = swap(b_own, 1)
        ready = list(ready) if last else list(ready) + [masked[group]]

        out_shape = [shape_of((PAIR, columns))]
        if not last:
            out_shape += [shape_of((SN, columns)), shape_of((half, columns))]
        results = pl.pallas_call(
            make_solve_kernel(group),
            out_shape=tuple(out_shape),
            in_specs=[SMEM] + [VMEM] * (5 + len(ready)),
            out_specs=(VMEM,) * len(out_shape),
            scratch_shapes=[pltpu.VMEM((PAIR, columns), BF16)],
            compiler_params=params(8),
            cost_estimate=cost(3),
            name="pair_solve",
        )(tab, packed, a_own, a_swap, b_own, b_swap, *ready)
        solved.append(results[0])
        if not last:
            packed, part = results[1:]

    def packed_path(*xs):
        k = GROUPS - 1
        whole = [pl.BlockSpec((PAIR, columns), lambda i, o: (0, 0))] * 4
        return pl.pallas_call(
            last_rows_kernel,
            out_shape=(shape_of((NW, columns)), shape_of((anc_rows.shape[0], columns))),
            grid_spec=pltpu.PrefetchScalarGridSpec(
                num_scalar_prefetch=1,
                grid=(anc_rows.shape[0] // tile,),
                in_specs=[pl.BlockSpec((tile, SN), lambda i, o: (i, o[2 * k])),
                          pl.BlockSpec((tile, SN), lambda i, o: (i, o[2 * k + 1])),
                          pl.BlockSpec((SB, NWB), lambda i, o: (i, 0))] + whole
                + [pl.BlockSpec((tile, columns), lambda i, o: (i, 0))]
                + [pl.BlockSpec((tile, columns), lambda i, o: (0, 0))] * 4,
                out_specs=(HBM, pl.BlockSpec((tile, columns), lambda i, o: (i, 0))),
                scratch_shapes=[pltpu.SemaphoreType.DMA((2 * GROUPS,))],
            ),
            compiler_params=params(20),
            cost_estimate=cost(6),
            name="last_rows",
        )(sn_order, anc_rows, anc_rows, anc_pattern, *xs, sums, *anc_pieces)

    def other_path(*xs):
        back = depth ^ jnp.arange(4)
        win_rhs = jnp.take(jnp.stack(pieces), back, axis=0).reshape(4 * tall, columns)
        anc_rhs = jnp.take(jnp.stack(anc_pieces), back, axis=0).reshape(4 * tile, columns)
        return general_path(win_rows, anc_rows, win_pattern, anc_pattern, window_owner, sn_order, diag_inv, win_rhs, anc_rhs)

    return tuple(lax.cond(flag[0] == 0, packed_path, other_path, *solved))


def solution(mesh):
    return jax.shard_map(
        local,
        mesh=mesh,
        in_specs=(P("rows", None), P("rows", None), P(), P("rows", None), P(), P(), P(),
                  P(("rows", "rhs"), None), P(("rows", "rhs"), None)),
        out_specs=(P(None, "rhs"), P("rows", "rhs")),
        check_vma=False,
    )
```

```python
import jax
import jax.numpy as jnp
from jax import lax
from jax.experimental import pallas as pl
from jax.experimental.pallas import tpu as pltpu
from jax.sharding import PartitionSpec as P

BS = 64
SB = 8
NSUP = 8
SN = 512
NW = 4096
NWB = 64
GROUPS = 4
PAIR = 2 * SN
F32 = jnp.float32
BF16 = jnp.bfloat16


def masked_columns(factor, pattern, node_label):
    blocks = pattern.shape[0]
    columns = lax.dynamic_slice_in_dim(factor, node_label * SN, SN, 1)
    chosen = lax.dynamic_slice_in_dim(pattern, node_label * SB, SB, 1)
    shaped = columns.reshape(blocks, BS, SB, BS) * chosen[:, None, :, None].astype(BF16)
    return shaped.reshape(blocks * BS, SN)


def sum_over_rows(values):
    count = lax.axis_size("rows")
    if count & (count - 1):
        return lax.psum(values, "rows")
    step = 1
    while step < count:
        values = values + lax.ppermute(values, "rows", [(i, i ^ step) for i in range(count)])
        step *= 2
    return values


def general_path(win_rows, anc_rows, win_pattern, anc_pattern, window_owner, sn_order, diag_inv, win_rhs, anc_rhs):
    columns_rhs = win_rhs.shape[1]
    slot_count = win_rows.shape[0] // BS
    first_slot = lax.axis_index("rows") * slot_count
    local_pattern = lax.dynamic_slice_in_dim(win_pattern, first_slot, slot_count, 0)

    def step(position, carry):
        solution, win_resid, anc_resid = carry
        node_label = sn_order[position]
        owners = lax.dynamic_slice_in_dim(window_owner, node_label * SB, SB, 0)
        inverse = lax.dynamic_index_in_dim(diag_inv, node_label, 0, keepdims=False)
        local_place = owners - first_slot
        present = (local_place >= 0) & (local_place < slot_count)
        resid_blocks = win_resid.reshape(slot_count, BS, columns_rhs)
        taken = jnp.take(resid_blocks, jnp.clip(local_place, 0, slot_count - 1), axis=0)
        placed = jnp.where(present[:, None, None], taken, 0.0).reshape(SN, columns_rhs)
        panel = sum_over_rows(placed.astype(BF16))
        solved = jnp.dot(inverse, panel, preferred_element_type=F32).astype(BF16)
        solution = lax.dynamic_update_slice_in_dim(solution, solved, node_label * SN, 0)
        win_part = jnp.dot(masked_columns(win_rows, local_pattern, node_label), solved, preferred_element_type=F32)
        anc_part = jnp.dot(masked_columns(anc_rows, anc_pattern, node_label), solved, preferred_element_type=F32)
        return solution, win_resid - win_part, anc_resid - anc_part

    first = (jnp.zeros((NW, columns_rhs), BF16), win_rhs.astype(F32), anc_rhs.astype(F32))
    solution, _, anc_resid = lax.fori_loop(0, NSUP, step, first)
    return solution, anc_resid.astype(BF16)


def spread_matrix():
    block_index = lax.broadcasted_iota(jnp.int32, (NWB, SN), 0)
    lane_index = lax.broadcasted_iota(jnp.int32, (NWB, SN), 1)
    return (block_index % SB == lane_index // BS).astype(F32).astype(BF16)


def expand_mask(rows_pattern, label, spread):
    lane = lax.broadcasted_iota(jnp.int32, rows_pattern.shape, 1)
    chosen = jnp.where(lane // SB == label, rows_pattern, 0).astype(F32).astype(BF16)
    return jnp.dot(chosen, spread, preferred_element_type=F32).astype(BF16)


def masked_rows(block_of, mask, count):
    return jnp.concatenate([block_of(j) * mask[j:j + 1, :] for j in range(count)], axis=0)


def rows_at(index):
    return pl.ds(pl.multiple_of(index * BS, BS), BS)


def columns_at(label):
    return pl.ds(pl.multiple_of(label * SN, SN), SN)


SRC, LSRC, PACK, TABLE = 0, 64, 96, 128


def factor_kernel(owner, order, pattern, win_ref, out, buf, pat, inv, pos, sem):
    row = lax.axis_index("rows")

    def note_slot(w, carry):
        slot = owner[w]

        @pl.when(slot // SB == row)
        def _():
            inv[slot % SB] = w

        return carry

    lax.fori_loop(0, NWB, note_slot, 0, unroll=8)
    for k in range(NSUP):
        pos[order[k]] = k
    labels = jnp.zeros((SB, 1), jnp.int32)
    for t in range(SB):
        label = order[(pos[inv[t] // SB] // 2) * 2]
        pltpu.make_async_copy(win_ref.at[pl.ds(t * BS, BS), columns_at(label)], buf.at[pl.ds(t * BS, BS), :], sem).start()
        labels = jnp.where(lax.broadcasted_iota(jnp.int32, (SB, 1), 0) == t, label, labels)
    pat[...] = pattern[pl.ds(pl.multiple_of(row * SB, SB), SB), :]
    mask = expand_mask(pat[...], labels, spread_matrix())
    pltpu.make_async_copy(win_ref.at[:, pl.ds(0, SN)], buf, sem).wait()
    for j in range(SB):
        out[j * BS:(j + 1) * BS, :] = buf[j * BS:(j + 1) * BS, :] * mask[j:j + 1, :]


def rhs_kernel(own_ref, other_ref, *sent):
    depth = lax.axis_index("rhs")
    tall, width = own_ref.shape[0], sent[0].shape[1]
    for s, out in enumerate(sent):
        at = pl.multiple_of(jnp.bitwise_xor(depth, s) * width, width)
        out[0:tall, :] = own_ref[:, pl.ds(at, width)]
        out[tall:2 * tall, :] = other_ref[:, pl.ds(at, width)]


def table_kernel(owner, order, tab, flag, cnt):
    row = lax.axis_index("rows")
    chip, core = row // 2, row % 2
    flag[0] = 0
    for t in range(GROUPS * SB):
        tab[PACK + t] = 0
    for group in range(GROUPS):
        for t in range(4):
            cnt[t] = 0

        def one(i, carry, group=group):
            slot = owner[order[2 * group + i // SB] * SB + i % SB]
            where, device = slot // (2 * SB), slot // SB
            rank = cnt[where]
            cnt[where] = rank + 1
            flag[0] = jnp.where(rank >= SB, 1, flag[0])
            rank = jnp.minimum(rank, SB - 1)
            rel = jnp.bitwise_xor(where, chip)
            diagonal = rel == 3
            source = jnp.where(rel == 0, 0, jnp.where(diagonal, jnp.where(rank // 4 == core, 3, 4),
                                                      jnp.where(rel == 1 + core, 1, 2)))
            tab[SRC + group * 16 + i] = source * SB + jnp.where(diagonal, rank % 4, rank)

            @pl.when(rel == 0)
            def _():
                tab[PACK + group * SB + rank] = jnp.bitwise_xor(device % 2, core) * SB + slot % SB

            @pl.when(i >= SB)
            def _():
                kind = jnp.where(rel == 0, 0, jnp.where(diagonal, 3, jnp.where(rel == 1 + core, 1, 2)))
                tab[LSRC + group * SB + i - SB] = (2 * kind + jnp.where(device % 2 == core, 0, 1)) * SB + slot % SB

            return carry

        lax.fori_loop(0, 2 * SB, one, 0, unroll=True)


def below_rhs_kernel(rhs_ref, *refs):
    outs, sems = refs[:-1], refs[-1]
    depth = lax.axis_index("rhs")
    width = outs[0].shape[1]
    copies = []
    for s, out in enumerate(outs):
        at = pl.multiple_of(jnp.bitwise_xor(depth, s) * width, width)
        copies.append(pltpu.make_async_copy(rhs_ref.at[:, pl.ds(at, width)], out, sems.at[s]))
        copies[-1].start()
    for c in copies:
        c.wait()


def first_pack_kernel(tab, *refs):
    pieces, (chip_rhs, p_ref, b_ref) = refs[:4], refs[4:]
    depth, core = lax.axis_index("rhs"), lax.axis_index("rows") % 2
    tall = pieces[0].shape[0] // 2
    for s in range(4):
        for side in range(2):
            at = pl.multiple_of(side * SB * BS + jnp.bitwise_xor(depth, s) * tall, tall)
            chip_rhs[pl.ds(at, tall), :] = pieces[s][side * tall:(side + 1) * tall, :]
    for j in range(SB):
        p_ref[j * BS:(j + 1) * BS, :] = chip_rhs[rows_at(tab[PACK + j]), :]
    b_ref[...] = p_ref[pl.ds(pl.multiple_of(core * SB // 2 * BS, SB // 2 * BS), SB // 2 * BS), :]


def make_mask_kernel(group):
    def kernel(tab, order, pattern, w_own, w_other, out, wrow, pat, sem):
        row = lax.axis_index("rows")
        for j in range(SB):
            place = tab[PACK + (group + 1) * SB + j]
            for side, w_ref in enumerate((w_own, w_other)):
                @pl.when(place // SB == side)
                def _(j=j, place=place, w_ref=w_ref):
                    pltpu.make_async_copy(w_ref.at[rows_at(place % SB), :], wrow.at[pl.ds(j * BS, BS), :], sem).start()
            pat[j:j + 1, :] = pattern[pl.ds(jnp.bitwise_xor(row, place // SB) * SB + place % SB, 1), :]
        spread = spread_matrix()
        rows = pat[...]
        masks = [expand_mask(rows, order[k], spread) for k in range(2 * group + 2)]
        pltpu.make_async_copy(w_own, wrow, sem).wait()
        for k in range(2 * group + 2):
            for j in range(SB):
                at = slice(j * BS, (j + 1) * BS)
                out[at, k * SN:(k + 1) * SN] = wrow[at, columns_at(order[k])] * masks[k][j:j + 1, :]

    return kernel


def make_prep_kernel(group):
    last = group == GROUPS - 1

    def kernel(*refs):
        tab, order = refs[:2]
        l_refs, diag_ref = refs[2:10], refs[10]
        refs = refs[11:]
        if last:
            d_out, l_out, dsem, lsem = refs
        else:
            w_ref, chip_rhs = refs[:2]
            xs = refs[2:2 + group]
            d_out, l_out, r_out, dsem, lsem = refs[2 + group:]
        for q in range(2):
            pltpu.make_async_copy(diag_ref.at[order[2 * group + q]], d_out.at[q], dsem.at[q]).start()
        for i in range(SB):
            code = tab[LSRC + group * SB + i]
            for m in range(8):
                @pl.when(code // SB == m)
                def _(m=m, i=i, code=code):
                    pltpu.make_async_copy(l_refs[m].at[rows_at(code % SB), :], l_out.at[pl.ds(i * BS, BS), :], lsem).start()
        if not last:
            total = jnp.concatenate([chip_rhs[rows_at(tab[PACK + (group + 1) * SB + j]), :] for j in range(SB)], axis=0).astype(F32)
            for k in range(group):
                total = total - jnp.dot(w_ref[:, k * PAIR:(k + 1) * PAIR], xs[k][...], preferred_element_type=F32)
            r_out[...] = total
        for q in range(2):
            pltpu.make_async_copy(diag_ref.at[0], d_out.at[q], dsem.at[q]).wait()
        pltpu.make_async_copy(diag_ref.at[0], l_out, lsem).wait()

    return kernel


def make_solve_kernel(group):
    last = group == GROUPS - 1

    def kernel(*refs):
        tab, sources, d_ref, l_ref = refs[0], refs[1:6], refs[6], refs[7]
        if last:
            x_ref, panel = refs[8:]
        else:
            r_ref, wn_ref, x_ref, p_ref, b_ref, panel = refs[8:]

        def place(i):
            code = tab[SRC + group * 16 + i]
            for which, source in enumerate(sources):
                @pl.when(code // SB == which)
                def _(source=source):
                    panel[rows_at(i), :] = source[rows_at(code % SB), :]

        for i in range(2 * SB):
            place(i)
        x_a = jnp.dot(d_ref[0], panel[0:SN, :], preferred_element_type=F32).astype(BF16)
        x_ref[0:SN, :] = x_a
        rest = panel[SN:PAIR, :].astype(F32) - jnp.dot(l_ref[...], x_a, preferred_element_type=F32)
        x_b = jnp.dot(d_ref[1], rest.astype(BF16), preferred_element_type=F32).astype(BF16)
        x_ref[SN:PAIR, :] = x_b
        if last:
            return
        total = r_ref[...] - jnp.dot(wn_ref[:, group * PAIR:(group + 1) * PAIR], x_ref[...], preferred_element_type=F32)
        p_ref[...] = total.astype(BF16)
        core = lax.axis_index("rows") % 2
        b_ref[...] = p_ref[pl.ds(pl.multiple_of(core * SB // 2 * BS, SB // 2 * BS), SB // 2 * BS), :]

    return kernel


def make_below_mask_kernel(group):
    def kernel(order, pattern, a_ref, out, sems):
        tiles = sems.shape[0]
        tall = out.shape[0] // tiles
        copies = []
        for i in range(tiles):
            for q in range(2):
                c = pltpu.make_async_copy(a_ref.at[pl.ds(i * tall, tall), columns_at(order[2 * group + q])],
                                          out.at[pl.ds(i * tall, tall), pl.ds(q * SN, SN)], sems.at[i, q])
                c.start()
                copies.append(c)
        spread = spread_matrix()
        rows = pattern[...]
        masks = [expand_mask(rows, order[2 * group + q], spread) for q in range(2)]
        for i in range(tiles):
            for q in range(2):
                copies[2 * i + q].wait()
                for j in range(i * tall // BS, (i + 1) * tall // BS):
                    at = (slice(j * BS, (j + 1) * BS), slice(q * SN, (q + 1) * SN))
                    out[at] = out[at] * masks[q][j:j + 1, :]

    return kernel


def first_rows_kernel(a_ref, x_ref, out):
    out[...] = jnp.dot(a_ref[...], x_ref[...], preferred_element_type=F32)


def next_rows_kernel(a_ref, x_ref, sums, out):
    out[...] = sums[...] + jnp.dot(a_ref[...], x_ref[...], preferred_element_type=F32)


def base_rows_kernel(a_ref, x_ref, sums, h0, h1, h2, h3, out):
    depth = lax.axis_index("rhs")
    tall = h0.shape[0]
    for s, h in enumerate((h0, h1, h2, h3)):
        at = pl.ds(pl.multiple_of(jnp.bitwise_xor(depth, s) * tall, tall), tall)
        part = jnp.dot(a_ref[at, :], x_ref[...], preferred_element_type=F32)
        out[at, :] = h[...].astype(F32) - (sums[at, :] + part)


def last_rows_kernel(order, a_ref, x0, x1, x2, x3, base, sol_ref, out_ref, done, sems, osem):
    copies = []
    for k, x in enumerate((x0, x1, x2, x3)):
        for q in range(2):
            at = pl.multiple_of(order[2 * k + q] * SN, SN)
            copies.append(pltpu.make_async_copy(x.at[pl.ds(q * SN, SN), :], sol_ref.at[pl.ds(at, SN), :], sems.at[2 * k + q]))
            copies[-1].start()
    tiles = osem.shape[0]
    tall = done.shape[0] // tiles
    for i in range(tiles):
        at = slice(i * tall, (i + 1) * tall)
        done[at, :] = (base[at, :] - jnp.dot(a_ref[at, :], x3[...], preferred_element_type=F32)).astype(BF16)
        copies.append(pltpu.make_async_copy(done.at[pl.ds(i * tall, tall), :], out_ref.at[pl.ds(i * tall, tall), :], osem.at[i]))
        copies[-1].start()
    for c in copies:
        c.wait()


def in_hbm(x):
    return pltpu.with_memory_space_constraint(x, pltpu.HBM)


SMEM = pl.BlockSpec(memory_space=pltpu.SMEM)
VMEM = pl.BlockSpec(memory_space=pltpu.VMEM)
HBM = pl.BlockSpec(memory_space=pltpu.HBM)


def params(mib):
    return pltpu.CompilerParams(vmem_limit_bytes=mib * 1024 * 1024)


def cost(micros):
    return pl.CostEstimate(flops=micros * 10 ** 8, bytes_accessed=micros * 3 * 10 ** 6, transcendentals=0)


def shape_of(dims, dtype=BF16):
    return jax.ShapeDtypeStruct(dims, dtype)


def local(win_rows, anc_rows, win_pattern, anc_pattern, window_owner, sn_order, diag_inv, rhs_win, rhs_anc):
    if lax.axis_size("rows") != 8 or lax.axis_size("rhs") != 4 or anc_rows.shape[0] != 4 * SB * BS:
        win_rhs = lax.all_to_all(rhs_win, "rhs", split_axis=1, concat_axis=0, tiled=True)
        anc_rhs = lax.all_to_all(rhs_anc, "rhs", split_axis=1, concat_axis=0, tiled=True)
        return general_path(win_rows, anc_rows, win_pattern, anc_pattern, window_owner, sn_order, diag_inv, win_rhs, anc_rhs)

    def swap(x, m):
        return lax.ppermute(x, "rows", [(i, i ^ m) for i in range(8)])

    def deep(x, m):
        return lax.ppermute(x, "rhs", [(i, i ^ m) for i in range(4)])

    def neighbour(x):
        return lax.ppermute(x, "rows", [(i, i ^ (2 if i % 2 == 0 else 4)) for i in range(8)])

    def forward(x):
        return lax.ppermute(x, "rows", [(i, i ^ (4 if i % 2 == 0 else 2)) for i in range(8)])

    columns = rhs_win.shape[1] // 4
    half = SN // 2
    tall = rhs_win.shape[0]
    rhs_other = swap(rhs_win, 1)
    w_own = in_hbm(win_rows)
    l_own = pl.pallas_call(
        factor_kernel,
        out_shape=shape_of((SN, SN)),
        in_specs=[SMEM, SMEM, VMEM, HBM],
        out_specs=VMEM,
        scratch_shapes=[pltpu.VMEM((SN, SN), BF16), pltpu.VMEM((SB, NWB), jnp.int32),
                        pltpu.SMEM((SB,), jnp.int32), pltpu.SMEM((SB,), jnp.int32), pltpu.SemaphoreType.DMA],
        compiler_params=params(4),
        cost_estimate=cost(2),
        name="factor_pack",
    )(window_owner, sn_order, win_pattern, w_own)
    near = neighbour(l_own)
    sent = pl.pallas_call(
        rhs_kernel,
        out_shape=(shape_of((2 * tall, columns)),) * 4,
        in_specs=[VMEM] * 2,
        out_specs=(VMEM,) * 4,
        compiler_params=params(4),
        cost_estimate=cost(1),
        name="rhs_pack",
    )(rhs_win, rhs_other)
    pieces = [sent[0]] + [deep(sent[s], s) for s in (1, 2, 3)]
    owner_later, _ = lax.optimization_barrier((window_owner, l_own))
    tab, flag = pl.pallas_call(
        table_kernel,
        out_shape=(shape_of((TABLE,), jnp.int32), shape_of((1,), jnp.int32)),
        in_specs=[SMEM, SMEM],
        out_specs=(SMEM, SMEM),
        scratch_shapes=[pltpu.SMEM((4,), jnp.int32)],
        compiler_params=params(4),
        cost_estimate=cost(3),
        name="tables",
    )(owner_later, sn_order)
    chip_rhs, packed, part = pl.pallas_call(
        first_pack_kernel,
        out_shape=(shape_of((PAIR, columns)), shape_of((SN, columns)), shape_of((half, columns))),
        in_specs=[SMEM] + [VMEM] * 4,
        out_specs=(VMEM,) * 3,
        compiler_params=params(4),
        cost_estimate=cost(1),
        name="first_pack",
    )(tab, *pieces)
    l_other = swap(l_own, 1)
    near_other = neighbour(l_other)
    far = forward(near)
    l_parts = [in_hbm(x) for x in (l_own, l_other, near, near_other, swap(near_other, 1), swap(near, 1), far, swap(far, 1))]
    w_other = in_hbm(swap(win_rows, 1))

    depth = lax.axis_index("rhs")
    tile = rhs_anc.shape[0]
    sums, solved, masked, below = None, [], [], []
    anc_hbm = in_hbm(anc_rows)
    diag_hbm = in_hbm(diag_inv)
    below_rows = anc_rows.shape[0]

    def mask_below(k, order):
        below.append(pl.pallas_call(
            make_below_mask_kernel(k),
            out_shape=shape_of((below_rows, PAIR)),
            in_specs=[SMEM, VMEM, HBM],
            out_specs=VMEM,
            scratch_shapes=[pltpu.SemaphoreType.DMA((4, 2))],
            compiler_params=params(4),
            cost_estimate=cost(3),
            name="mask_below",
        )(order, anc_pattern, anc_hbm))

    anc_order, anc_pieces = (2, 3, 1), [None] * 4
    for group in range(GROUPS):
        last = group == GROUPS - 1
        a_own = neighbour(packed)
        b_own = swap(part, 6)
        if group == 0:
            tab_later, order_later, _ = lax.optimization_barrier((tab, sn_order, packed))
            for k in range(GROUPS - 1):
                masked.append(pl.pallas_call(
                    make_mask_kernel(k),
                    out_shape=shape_of((SN, (k + 1) * PAIR)),
                    in_specs=[SMEM, SMEM, VMEM, HBM, HBM],
                    out_specs=VMEM,
                    scratch_shapes=[pltpu.VMEM((SN, NW), BF16), pltpu.VMEM((SB, NWB), jnp.int32), pltpu.SemaphoreType.DMA],
                    compiler_params=params(6),
                    cost_estimate=cost(2),
                    name="mask_rows",
                )(tab_later, order_later, win_pattern, w_own, w_other))
            mask_below(0, order_later)
            mask_below(1, order_later)
        if group == 0:
            rhs_later, _ = lax.optimization_barrier((rhs_anc, packed))
            anc_pieces = list(pl.pallas_call(
                below_rhs_kernel,
                out_shape=(shape_of((tile, columns)),) * 4,
                in_specs=[HBM],
                out_specs=(VMEM,) * 4,
                scratch_shapes=[pltpu.SemaphoreType.DMA((4,))],
                compiler_params=params(4),
                cost_estimate=cost(1),
                name="below_rhs",
            )(in_hbm(rhs_later)))
        if not last:
            s = anc_order[group]
            moved, _ = lax.optimization_barrier((anc_pieces[s], packed))
            anc_pieces[s] = deep(moved, s)

        operands = [tab, sn_order, *l_parts, diag_hbm]
        in_specs = [SMEM, SMEM] + [HBM] * 9
        out_shape = [shape_of((2, SN, SN)), shape_of((SN, SN))]
        if not last:
            operands += [masked[group], chip_rhs, *solved]
            in_specs += [VMEM] * (2 + group)
            out_shape += [shape_of((SN, columns), F32)]
        ready = pl.pallas_call(
            make_prep_kernel(group),
            out_shape=tuple(out_shape),
            in_specs=in_specs,
            out_specs=(VMEM,) * len(out_shape),
            scratch_shapes=[pltpu.SemaphoreType.DMA((2,)), pltpu.SemaphoreType.DMA],
            compiler_params=params(8),
            cost_estimate=cost(2),
            name="prep",
        )(*operands)
        if group > 0:
            k = group - 1
            previous = anc_pieces[anc_order[k]]
            if k < 2:
                more, kernel = ([], first_rows_kernel) if k == 0 else ([sums], next_rows_kernel)
            else:
                more, kernel = [sums, *anc_pieces], base_rows_kernel
            sums = pl.pallas_call(
                kernel,
                out_shape=shape_of((below_rows, columns), F32),
                in_specs=[VMEM] * (2 + len(more)),
                out_specs=VMEM,
                input_output_aliases={2: 0} if more else {},
                compiler_params=params(6),
                cost_estimate=cost(3),
                name="rows_below",
            )(below[k], solved[k], *more)
            if k < 2:
                order_later, _ = lax.optimization_barrier((sn_order, packed))
                mask_below(k + 2, order_later)
            a_own, b_own, sums, below[-1], previous, *ready = lax.optimization_barrier(
                (a_own, b_own, sums, below[-1], previous, *ready))
            anc_pieces[anc_order[k]] = previous
        else:
            a_own, b_own, masked[0], masked[1], masked[2], below[0], below[1] = lax.optimization_barrier(
                (a_own, b_own, *masked, *below))
        a_swap = swap(a_own, 1)
        b_swap = swap(b_own, 1)
        ready = list(ready) if last else list(ready) + [masked[group]]

        out_shape = [shape_of((PAIR, columns))]
        if not last:
            out_shape += [shape_of((SN, columns)), shape_of((half, columns))]
        results = pl.pallas_call(
            make_solve_kernel(group),
            out_shape=tuple(out_shape),
            in_specs=[SMEM] + [VMEM] * (5 + len(ready)),
            out_specs=(VMEM,) * len(out_shape),
            scratch_shapes=[pltpu.VMEM((PAIR, columns), BF16)],
            compiler_params=params(8),
            cost_estimate=cost(3),
            name="pair_solve",
        )(tab, packed, a_own, a_swap, b_own, b_swap, *ready)
        solved.append(results[0])
        if not last:
            packed, part = results[1:]

    def packed_path(*xs):
        return pl.pallas_call(
            last_rows_kernel,
            out_shape=(shape_of((NW, columns)), shape_of((below_rows, columns))),
            in_specs=[SMEM] + [VMEM] * 6,
            out_specs=(HBM, HBM),
            scratch_shapes=[pltpu.VMEM((below_rows, columns), BF16), pltpu.SemaphoreType.DMA((2 * GROUPS,)),
                            pltpu.SemaphoreType.DMA((4,))],
            compiler_params=params(16),
            cost_estimate=cost(3),
            name="last_rows",
        )(sn_order, below[-1], *xs, sums)

    def other_path(*xs):
        back = depth ^ jnp.arange(4)
        win_rhs = jnp.take(jnp.stack([x[:tall] for x in pieces]), back, axis=0).reshape(4 * tall, columns)
        anc_rhs = jnp.take(jnp.stack(anc_pieces), back, axis=0).reshape(4 * tile, columns)
        return general_path(win_rows, anc_rows, win_pattern, anc_pattern, window_owner, sn_order, diag_inv, win_rhs, anc_rhs)

    return tuple(lax.cond(flag[0] == 0, packed_path, other_path, *solved))


def solution(mesh):
    return jax.shard_map(
        local,
        mesh=mesh,
        in_specs=(P("rows", None), P("rows", None), P(), P("rows", None), P(), P(), P(),
                  P(("rows", "rhs"), None), P(("rows", "rhs"), None)),
        out_specs=(P(None, "rhs"), P("rows", "rhs")),
        check_vma=False,
    )
```

```python
import jax
import jax.numpy as jnp
from jax import lax
from jax.experimental import pallas as pl
from jax.experimental.pallas import tpu as pltpu
from jax.sharding import PartitionSpec as P

BS = 64
SB = 8
NSUP = 8
SN = 512
NW = 4096
NWB = 64
GROUPS = 4
PAIR = 2 * SN
F32 = jnp.float32
BF16 = jnp.bfloat16


def masked_columns(factor, pattern, node_label):
    blocks = pattern.shape[0]
    columns = lax.dynamic_slice_in_dim(factor, node_label * SN, SN, 1)
    chosen = lax.dynamic_slice_in_dim(pattern, node_label * SB, SB, 1)
    shaped = columns.reshape(blocks, BS, SB, BS) * chosen[:, None, :, None].astype(BF16)
    return shaped.reshape(blocks * BS, SN)


def sum_over_rows(values):
    count = lax.axis_size("rows")
    if count & (count - 1):
        return lax.psum(values, "rows")
    step = 1
    while step < count:
        values = values + lax.ppermute(values, "rows", [(i, i ^ step) for i in range(count)])
        step *= 2
    return values


def general_path(win_rows, anc_rows, win_pattern, anc_pattern, window_owner, sn_order, diag_inv, win_rhs, anc_rhs):
    columns_rhs = win_rhs.shape[1]
    slot_count = win_rows.shape[0] // BS
    first_slot = lax.axis_index("rows") * slot_count
    local_pattern = lax.dynamic_slice_in_dim(win_pattern, first_slot, slot_count, 0)

    def step(position, carry):
        solution, win_resid, anc_resid = carry
        node_label = sn_order[position]
        owners = lax.dynamic_slice_in_dim(window_owner, node_label * SB, SB, 0)
        inverse = lax.dynamic_index_in_dim(diag_inv, node_label, 0, keepdims=False)
        local_place = owners - first_slot
        present = (local_place >= 0) & (local_place < slot_count)
        resid_blocks = win_resid.reshape(slot_count, BS, columns_rhs)
        taken = jnp.take(resid_blocks, jnp.clip(local_place, 0, slot_count - 1), axis=0)
        placed = jnp.where(present[:, None, None], taken, 0.0).reshape(SN, columns_rhs)
        panel = sum_over_rows(placed.astype(BF16))
        solved = jnp.dot(inverse, panel, preferred_element_type=F32).astype(BF16)
        solution = lax.dynamic_update_slice_in_dim(solution, solved, node_label * SN, 0)
        win_part = jnp.dot(masked_columns(win_rows, local_pattern, node_label), solved, preferred_element_type=F32)
        anc_part = jnp.dot(masked_columns(anc_rows, anc_pattern, node_label), solved, preferred_element_type=F32)
        return solution, win_resid - win_part, anc_resid - anc_part

    first = (jnp.zeros((NW, columns_rhs), BF16), win_rhs.astype(F32), anc_rhs.astype(F32))
    solution, _, anc_resid = lax.fori_loop(0, NSUP, step, first)
    return solution, anc_resid.astype(BF16)


def spread_matrix():
    block_index = lax.broadcasted_iota(jnp.int32, (NWB, SN), 0)
    lane_index = lax.broadcasted_iota(jnp.int32, (NWB, SN), 1)
    return (block_index % SB == lane_index // BS).astype(F32).astype(BF16)


def expand_mask(rows_pattern, label, spread):
    lane = lax.broadcasted_iota(jnp.int32, rows_pattern.shape, 1)
    chosen = jnp.where(lane // SB == label, rows_pattern, 0).astype(F32).astype(BF16)
    return jnp.dot(chosen, spread, preferred_element_type=F32).astype(BF16)


def masked_rows(block_of, mask, count):
    return jnp.concatenate([block_of(j) * mask[j:j + 1, :] for j in range(count)], axis=0)


def rows_at(index):
    return pl.ds(pl.multiple_of(index * BS, BS), BS)


def columns_at(label):
    return pl.ds(pl.multiple_of(label * SN, SN), SN)


SRC, LSRC, PACK, TABLE = 0, 64, 96, 128


def factor_kernel(owner, order, pattern, win_ref, out, buf, pat, inv, pos, sem):
    row = lax.axis_index("rows")

    def note_slot(w, carry):
        slot = owner[w]

        @pl.when(slot // SB == row)
        def _():
            inv[slot % SB] = w

        return carry

    lax.fori_loop(0, NWB, note_slot, 0, unroll=8)
    for k in range(NSUP):
        pos[order[k]] = k
    labels = jnp.zeros((SB, 1), jnp.int32)
    for t in range(SB):
        label = order[(pos[inv[t] // SB] // 2) * 2]
        pltpu.make_async_copy(win_ref.at[pl.ds(t * BS, BS), columns_at(label)], buf.at[pl.ds(t * BS, BS), :], sem).start()
        labels = jnp.where(lax.broadcasted_iota(jnp.int32, (SB, 1), 0) == t, label, labels)
    pat[...] = pattern[pl.ds(pl.multiple_of(row * SB, SB), SB), :]
    mask = expand_mask(pat[...], labels, spread_matrix())
    pltpu.make_async_copy(win_ref.at[:, pl.ds(0, SN)], buf, sem).wait()
    for j in range(SB):
        out[j * BS:(j + 1) * BS, :] = buf[j * BS:(j + 1) * BS, :] * mask[j:j + 1, :]


def rhs_kernel(own_ref, other_ref, *sent):
    depth = lax.axis_index("rhs")
    tall, width = own_ref.shape[0], sent[0].shape[1]
    for s, out in enumerate(sent):
        at = pl.multiple_of(jnp.bitwise_xor(depth, s) * width, width)
        out[0:tall, :] = own_ref[:, pl.ds(at, width)]
        out[tall:2 * tall, :] = other_ref[:, pl.ds(at, width)]


def table_kernel(owner, order, tab, flag, cnt):
    row = lax.axis_index("rows")
    chip, core = row // 2, row % 2
    flag[0] = 0
    flag[1] = lax.axis_index("rhs")
    for t in range(GROUPS * SB):
        tab[PACK + t] = 0
    for group in range(GROUPS):
        for t in range(4):
            cnt[t] = 0

        def one(i, carry, group=group):
            slot = owner[order[2 * group + i // SB] * SB + i % SB]
            where, device = slot // (2 * SB), slot // SB
            rank = cnt[where]
            cnt[where] = rank + 1
            flag[0] = jnp.where(rank >= SB, 1, flag[0])
            rank = jnp.minimum(rank, SB - 1)
            rel = jnp.bitwise_xor(where, chip)
            diagonal = rel == 3
            source = jnp.where(rel == 0, 0, jnp.where(diagonal, jnp.where(rank // 4 == core, 3, 4),
                                                      jnp.where(rel == 1 + core, 1, 2)))
            tab[SRC + group * 16 + i] = source * SB + jnp.where(diagonal, rank % 4, rank)

            @pl.when(rel == 0)
            def _():
                tab[PACK + group * SB + rank] = jnp.bitwise_xor(device % 2, core) * SB + slot % SB

            @pl.when(i >= SB)
            def _():
                kind = jnp.where(rel == 0, 0, jnp.where(diagonal, 3, jnp.where(rel == 1 + core, 1, 2)))
                tab[LSRC + group * SB + i - SB] = (2 * kind + jnp.where(device % 2 == core, 0, 1)) * SB + slot % SB

            return carry

        lax.fori_loop(0, 2 * SB, one, 0, unroll=True)


def below_rhs_kernel(rhs_ref, *refs):
    outs, sems = refs[:-1], refs[-1]
    depth = lax.axis_index("rhs")
    width = outs[0].shape[1]
    copies = []
    for s, out in enumerate(outs):
        at = pl.multiple_of(jnp.bitwise_xor(depth, s) * width, width)
        copies.append(pltpu.make_async_copy(rhs_ref.at[:, pl.ds(at, width)], out, sems.at[s]))
        copies[-1].start()
    for c in copies:
        c.wait()


def first_pack_kernel(tab, *refs):
    pieces, (chip_rhs, p_ref, b_ref) = refs[:4], refs[4:]
    depth, core = lax.axis_index("rhs"), lax.axis_index("rows") % 2
    tall = pieces[0].shape[0] // 2
    for s in range(4):
        for side in range(2):
            at = pl.multiple_of(side * SB * BS + jnp.bitwise_xor(depth, s) * tall, tall)
            chip_rhs[pl.ds(at, tall), :] = pieces[s][side * tall:(side + 1) * tall, :]
    for j in range(SB):
        p_ref[j * BS:(j + 1) * BS, :] = chip_rhs[rows_at(tab[PACK + j]), :]
    b_ref[...] = p_ref[pl.ds(pl.multiple_of(core * SB // 2 * BS, SB // 2 * BS), SB // 2 * BS), :]


def make_mask_kernel(group):
    def kernel(tab, order, pattern, w_own, w_other, out, pat):
        row = lax.axis_index("rows")
        places = [tab[PACK + (group + 1) * SB + j] for j in range(SB)]
        for j, place in enumerate(places):
            pat[j:j + 1, :] = pattern[pl.ds(jnp.bitwise_xor(row, place // SB) * SB + place % SB, 1), :]
        spread = spread_matrix()
        rows = pat[...]
        masks = [expand_mask(rows, order[k], spread) for k in range(2 * group + 2)]
        for j, place in enumerate(places):
            at = slice(j * BS, (j + 1) * BS)
            for side, w_ref in enumerate((w_own, w_other)):
                @pl.when(place // SB == side)
                def _(w_ref=w_ref, at=at, j=j, place=place):
                    for k in range(2 * group + 2):
                        block = w_ref[rows_at(place % SB), columns_at(order[k])]
                        out[at, k * SN:(k + 1) * SN] = block * masks[k][j:j + 1, :]

    return kernel


def make_prep_kernel(group):
    last = group == GROUPS - 1

    def kernel(tab, *refs):
        l_refs, refs = refs[:8], refs[8:]
        if last:
            l_out = refs[0]
        else:
            w_ref, chip_rhs = refs[:2]
            xs = refs[2:2 + group]
            l_out, r_out = refs[2 + group:]
        for i in range(SB):
            code = tab[LSRC + group * SB + i]
            for m in range(8):
                @pl.when(code // SB == m)
                def _(m=m, i=i, code=code):
                    l_out[i * BS:(i + 1) * BS, :] = l_refs[m][rows_at(code % SB), :]
        if not last:
            total = jnp.concatenate([chip_rhs[rows_at(tab[PACK + (group + 1) * SB + j]), :] for j in range(SB)], axis=0).astype(F32)
            for k in range(group):
                total = total - jnp.dot(w_ref[:, k * PAIR:(k + 1) * PAIR], xs[k][...], preferred_element_type=F32)
            r_out[...] = total

    return kernel


def make_solve_kernel(group):
    last = group == GROUPS - 1

    def kernel(*refs):
        tab, order, sources, d_ref, l_ref = refs[0], refs[1], refs[2:7], refs[7], refs[8]
        if last:
            x_ref, panel = refs[9:]
        else:
            r_ref, wn_ref, x_ref, p_ref, b_ref, panel = refs[9:]

        def place(i):
            code = tab[SRC + group * 16 + i]
            for which, source in enumerate(sources):
                @pl.when(code // SB == which)
                def _(source=source):
                    panel[rows_at(i), :] = source[rows_at(code % SB), :]

        for i in range(2 * SB):
            place(i)
        x_a = jnp.dot(d_ref[order[2 * group]], panel[0:SN, :], preferred_element_type=F32).astype(BF16)
        x_ref[0:SN, :] = x_a
        rest = panel[SN:PAIR, :].astype(F32) - jnp.dot(l_ref[...], x_a, preferred_element_type=F32)
        x_b = jnp.dot(d_ref[order[2 * group + 1]], rest.astype(BF16), preferred_element_type=F32).astype(BF16)
        x_ref[SN:PAIR, :] = x_b
        if last:
            return
        total = r_ref[...] - jnp.dot(wn_ref[:, group * PAIR:(group + 1) * PAIR], x_ref[...], preferred_element_type=F32)
        p_ref[...] = total.astype(BF16)
        core = lax.axis_index("rows") % 2
        b_ref[...] = p_ref[pl.ds(pl.multiple_of(core * SB // 2 * BS, SB // 2 * BS), SB // 2 * BS), :]

    return kernel


def below_part(order, pattern, a_ref, buf, sems, group):
    tiles = sems.shape[0]
    tall = buf.shape[0] // tiles
    copies = []
    for i in range(tiles):
        for q in range(2):
            c = pltpu.make_async_copy(a_ref.at[pl.ds(i * tall, tall), columns_at(order[2 * group + q])],
                                      buf.at[pl.ds(i * tall, tall), pl.ds(q * SN, SN)], sems.at[i, q])
            c.start()
            copies.append(c)
    spread = spread_matrix()
    rows = pattern[...]
    masks = [expand_mask(rows, order[2 * group + q], spread) for q in range(2)]
    for i in range(tiles):
        halves = []
        for q in range(2):
            copies[2 * i + q].wait()
            halves.append(jnp.concatenate([buf[j * BS:(j + 1) * BS, q * SN:(q + 1) * SN] * masks[q][j:j + 1, :]
                                           for j in range(i * tall // BS, (i + 1) * tall // BS)], axis=0))
        yield slice(i * tall, (i + 1) * tall), jnp.concatenate(halves, axis=1)


def last_mask_kernel(order, pattern, a_ref, out, sems):
    for at, part in below_part(order, pattern, a_ref, out, sems, GROUPS - 1):
        out[at, :] = part


def first_rows_kernel(order, pattern, a_ref, x_ref, out, buf, sems):
    for at, part in below_part(order, pattern, a_ref, buf, sems, 0):
        out[at, :] = jnp.dot(part, x_ref[...], preferred_element_type=F32)


def next_rows_kernel(order, pattern, a_ref, x_ref, sums, out, buf, sems):
    for at, part in below_part(order, pattern, a_ref, buf, sems, 1):
        out[at, :] = sums[at, :] + jnp.dot(part, x_ref[...], preferred_element_type=F32)


def base_rows_kernel(order, pattern, a_ref, x_ref, sums, h0, h1, h2, h3, out, buf, sems, rhs):
    depth = lax.axis_index("rhs")
    tall = h0.shape[0]
    for s, h in enumerate((h0, h1, h2, h3)):
        rhs[pl.ds(pl.multiple_of(jnp.bitwise_xor(depth, s) * tall, tall), tall), :] = h[...]
    for at, part in below_part(order, pattern, a_ref, buf, sems, 2):
        out[at, :] = rhs[at, :].astype(F32) - (sums[at, :] + jnp.dot(part, x_ref[...], preferred_element_type=F32))


def last_rows_kernel(order, a_ref, x0, x1, x2, x3, base, sol_ref, out_ref, done, sems, osem):
    copies = []
    for k, x in enumerate((x0, x1, x2, x3)):
        for q in range(2):
            at = pl.multiple_of(order[2 * k + q] * SN, SN)
            copies.append(pltpu.make_async_copy(x.at[pl.ds(q * SN, SN), :], sol_ref.at[pl.ds(at, SN), :], sems.at[2 * k + q]))
            copies[-1].start()
    tiles = osem.shape[0]
    tall = done.shape[0] // tiles
    for i in range(tiles):
        at = slice(i * tall, (i + 1) * tall)
        done[at, :] = (base[at, :] - jnp.dot(a_ref[at, :], x3[...], preferred_element_type=F32)).astype(BF16)
        copies.append(pltpu.make_async_copy(done.at[pl.ds(i * tall, tall), :], out_ref.at[pl.ds(i * tall, tall), :], osem.at[i]))
        copies[-1].start()
    for c in copies:
        c.wait()


def in_vmem(x):
    return pltpu.with_memory_space_constraint(x, pltpu.VMEM)


def in_hbm(x):
    return pltpu.with_memory_space_constraint(x, pltpu.HBM)


SMEM = pl.BlockSpec(memory_space=pltpu.SMEM)
VMEM = pl.BlockSpec(memory_space=pltpu.VMEM)
HBM = pl.BlockSpec(memory_space=pltpu.HBM)


def params(mib):
    return pltpu.CompilerParams(vmem_limit_bytes=mib * 1024 * 1024)


def cost(micros):
    return pl.CostEstimate(flops=micros * 10 ** 8, bytes_accessed=micros * 3 * 10 ** 6, transcendentals=0)


def shape_of(dims, dtype=BF16):
    return jax.ShapeDtypeStruct(dims, dtype)


def local(win_rows, anc_rows, win_pattern, anc_pattern, window_owner, sn_order, diag_inv, rhs_win, rhs_anc):
    if lax.axis_size("rows") != 8 or lax.axis_size("rhs") != 4 or anc_rows.shape[0] != 4 * SB * BS:
        win_rhs = lax.all_to_all(rhs_win, "rhs", split_axis=1, concat_axis=0, tiled=True)
        anc_rhs = lax.all_to_all(rhs_anc, "rhs", split_axis=1, concat_axis=0, tiled=True)
        return general_path(win_rows, anc_rows, win_pattern, anc_pattern, window_owner, sn_order, diag_inv, win_rhs, anc_rhs)

    def swap(x, m):
        return lax.ppermute(x, "rows", [(i, i ^ m) for i in range(8)])

    def deep(x, m):
        return lax.ppermute(x, "rhs", [(i, i ^ m) for i in range(4)])

    def neighbour(x):
        return lax.ppermute(x, "rows", [(i, i ^ (2 if i % 2 == 0 else 4)) for i in range(8)])

    def forward(x):
        return lax.ppermute(x, "rows", [(i, i ^ (4 if i % 2 == 0 else 2)) for i in range(8)])

    columns = rhs_win.shape[1] // 4
    half = SN // 2
    tall = rhs_win.shape[0]
    rhs_other = swap(rhs_win, 1)
    w_own = in_hbm(win_rows)
    l_own = pl.pallas_call(
        factor_kernel,
        out_shape=shape_of((SN, SN)),
        in_specs=[SMEM, SMEM, VMEM, HBM],
        out_specs=VMEM,
        scratch_shapes=[pltpu.VMEM((SN, SN), BF16), pltpu.VMEM((SB, NWB), jnp.int32),
                        pltpu.SMEM((SB,), jnp.int32), pltpu.SMEM((SB,), jnp.int32), pltpu.SemaphoreType.DMA],
        compiler_params=params(4),
        cost_estimate=cost(2),
        name="factor_pack",
    )(window_owner, sn_order, win_pattern, w_own)
    l_other = swap(l_own, 1)
    rhs_late, _ = lax.optimization_barrier((rhs_win, l_own))
    sent = pl.pallas_call(
        rhs_kernel,
        out_shape=(shape_of((2 * tall, columns)),) * 4,
        in_specs=[VMEM] * 2,
        out_specs=(VMEM,) * 4,
        compiler_params=params(4),
        cost_estimate=cost(1),
        name="rhs_pack",
    )(rhs_late, rhs_other)
    l_own, l_other, *sent = lax.optimization_barrier((l_own, l_other, *sent))
    near, near_other = neighbour(l_own), neighbour(l_other)
    pieces = [sent[0]] + [deep(sent[s], s) for s in (1, 2, 3)]
    owner_later, _ = lax.optimization_barrier((window_owner, l_own))
    tab, flag = pl.pallas_call(
        table_kernel,
        out_shape=(shape_of((TABLE,), jnp.int32), shape_of((2,), jnp.int32)),
        in_specs=[SMEM, SMEM],
        out_specs=(SMEM, SMEM),
        scratch_shapes=[pltpu.SMEM((4,), jnp.int32)],
        compiler_params=params(4),
        cost_estimate=cost(3),
        name="tables",
    )(owner_later, sn_order)
    chip_rhs, packed, part = pl.pallas_call(
        first_pack_kernel,
        out_shape=(shape_of((PAIR, columns)), shape_of((SN, columns)), shape_of((half, columns))),
        in_specs=[SMEM] + [VMEM] * 4,
        out_specs=(VMEM,) * 3,
        compiler_params=params(4),
        cost_estimate=cost(1),
        name="first_pack",
    )(tab, *pieces)
    near_late, near_other, w_late, *_ = lax.optimization_barrier((near, near_other, win_rows, *pieces[1:]))
    far = forward(near_late)
    l_parts = [in_vmem(x) for x in (l_own, l_other, near, near_other, swap(near_other, 1), swap(near, 1), far, swap(far, 1))]
    w_other = in_vmem(swap(w_late, 1))
    w_own = in_vmem(win_rows)

    tile = rhs_anc.shape[0]
    sums, solved, masked = None, [], []
    anc_hbm = in_hbm(anc_rows)
    diag_vmem = in_vmem(diag_inv)
    below_rows = anc_rows.shape[0]

    anc_order, anc_pieces = (2, 3, 1), [None] * 4
    for group in range(GROUPS):
        last = group == GROUPS - 1
        a_own = neighbour(packed)
        b_own = swap(part, 6)
        if group == 0:
            tab_later, order_later, _ = lax.optimization_barrier((tab, sn_order, packed))
            for k in range(GROUPS - 1):
                masked.append(pl.pallas_call(
                    make_mask_kernel(k),
                    out_shape=shape_of((SN, (k + 1) * PAIR)),
                    in_specs=[SMEM, SMEM, VMEM, VMEM, VMEM],
                    out_specs=VMEM,
                    scratch_shapes=[pltpu.VMEM((SB, NWB), jnp.int32)],
                    compiler_params=params(6),
                    cost_estimate=cost(2),
                    name="mask_rows",
                )(tab_later, order_later, win_pattern, w_own, w_other))
        if group == 1:
            order_later, _ = lax.optimization_barrier((sn_order, packed))
            last_below = pl.pallas_call(
                last_mask_kernel,
                out_shape=shape_of((below_rows, PAIR)),
                in_specs=[SMEM, VMEM, HBM],
                out_specs=VMEM,
                scratch_shapes=[pltpu.SemaphoreType.DMA((4, 2))],
                compiler_params=params(4),
                cost_estimate=cost(3),
                name="last_mask",
            )(order_later, anc_pattern, anc_hbm)
        if group == 0:
            rhs_later, _ = lax.optimization_barrier((rhs_anc, packed))
            anc_pieces = list(pl.pallas_call(
                below_rhs_kernel,
                out_shape=(shape_of((tile, columns)),) * 4,
                in_specs=[HBM],
                out_specs=(VMEM,) * 4,
                scratch_shapes=[pltpu.SemaphoreType.DMA((4,))],
                compiler_params=params(4),
                cost_estimate=cost(1),
                name="below_rhs",
            )(in_hbm(rhs_later)))
        if not last:
            s = anc_order[group]
            moved, _ = lax.optimization_barrier((anc_pieces[s], packed))
            anc_pieces[s] = deep(moved, s)

        operands = [tab, *l_parts]
        out_shape = [shape_of((SN, SN))]
        if not last:
            operands += [masked[group], chip_rhs, *solved]
            out_shape += [shape_of((SN, columns), F32)]
        ready = pl.pallas_call(
            make_prep_kernel(group),
            out_shape=tuple(out_shape),
            in_specs=[SMEM] + [VMEM] * (len(operands) - 1),
            out_specs=(VMEM,) * len(out_shape),
            compiler_params=params(6),
            cost_estimate=cost(2),
            name="prep",
        )(*operands)
        if group > 0:
            k = group - 1
            previous = anc_pieces[anc_order[k]]
            if k < 2:
                more, kernel = ([], first_rows_kernel) if k == 0 else ([sums], next_rows_kernel)
            else:
                more, kernel = [sums, *anc_pieces], base_rows_kernel
            sums = pl.pallas_call(
                kernel,
                out_shape=shape_of((below_rows, columns), F32),
                in_specs=[SMEM, VMEM, HBM] + [VMEM] * (1 + len(more)),
                out_specs=VMEM,
                scratch_shapes=[pltpu.VMEM((below_rows, PAIR), BF16), pltpu.SemaphoreType.DMA((4, 2))]
                + ([pltpu.VMEM((below_rows, columns), BF16)] if k == 2 else []),
                input_output_aliases={4: 0} if more else {},
                compiler_params=params(10),
                cost_estimate=cost(3),
                name="rows_below",
            )(sn_order, anc_pattern, anc_hbm, solved[k], *more)
            if k == 2:
                a_own, last_below = lax.optimization_barrier((a_own, last_below))
            a_own, b_own, sums, previous, *ready = lax.optimization_barrier((a_own, b_own, sums, previous, *ready))
            anc_pieces[anc_order[k]] = previous
        else:
            a_own, b_own, *masked = lax.optimization_barrier((a_own, b_own, *masked))
        a_swap = swap(a_own, 1)
        b_swap = swap(b_own, 1)
        ready = list(ready) if last else list(ready) + [masked[group]]

        out_shape = [shape_of((PAIR, columns))]
        if not last:
            out_shape += [shape_of((SN, columns)), shape_of((half, columns))]
        results = pl.pallas_call(
            make_solve_kernel(group),
            out_shape=tuple(out_shape),
            in_specs=[SMEM, SMEM] + [VMEM] * (6 + len(ready)),
            out_specs=(VMEM,) * len(out_shape),
            scratch_shapes=[pltpu.VMEM((PAIR, columns), BF16)],
            compiler_params=params(8),
            cost_estimate=cost(3),
            name="pair_solve",
        )(tab, sn_order, packed, a_own, a_swap, b_own, b_swap, diag_vmem, *ready)
        solved.append(results[0])
        if not last:
            packed, part = results[1:]

    outputs = pl.pallas_call(
        last_rows_kernel,
        out_shape=(shape_of((NW, columns)), shape_of((below_rows, columns))),
        in_specs=[SMEM] + [VMEM] * 6,
        out_specs=(HBM, HBM),
        scratch_shapes=[pltpu.VMEM((below_rows, columns), BF16), pltpu.SemaphoreType.DMA((2 * GROUPS,)),
                        pltpu.SemaphoreType.DMA((4,))],
        compiler_params=params(6),
        cost_estimate=cost(3),
        name="last_rows",
    )(sn_order, last_below, *solved, sums)

    def again(carry):
        carry, own_pieces, below_pieces = lax.optimization_barrier((carry, pieces, anc_pieces))
        back = carry[0][1] ^ jnp.arange(4)
        win_rhs = jnp.take(jnp.stack([x[:tall] for x in own_pieces]), back, axis=0).reshape(4 * tall, columns)
        anc_rhs = jnp.take(jnp.stack(below_pieces), back, axis=0).reshape(4 * tile, columns)
        return jnp.zeros_like(carry[0]), *general_path(
            win_rows, anc_rows, win_pattern, anc_pattern, window_owner, sn_order, diag_inv, win_rhs, anc_rhs)

    return tuple(lax.while_loop(lambda carry: carry[0][0] != 0, again, (flag, *outputs))[1:])


def solution(mesh):
    return jax.shard_map(
        local,
        mesh=mesh,
        in_specs=(P("rows", None), P("rows", None), P(), P("rows", None), P(), P(), P(),
                  P(("rows", "rhs"), None), P(("rows", "rhs"), None)),
        out_specs=(P(None, "rhs"), P("rows", "rhs")),
        check_vma=False,
    )
```

```python
import jax
import jax.numpy as jnp
from jax import lax
from jax.experimental import pallas as pl
from jax.experimental.pallas import tpu as pltpu
from jax.sharding import PartitionSpec as P

BS = 64
SB = 8
NSUP = 8
SN = 512
NW = 4096
NWB = 64
GROUPS = 4
PAIR = 2 * SN
F32 = jnp.float32
BF16 = jnp.bfloat16


def masked_columns(factor, pattern, node_label):
    blocks = pattern.shape[0]
    columns = lax.dynamic_slice_in_dim(factor, node_label * SN, SN, 1)
    chosen = lax.dynamic_slice_in_dim(pattern, node_label * SB, SB, 1)
    shaped = columns.reshape(blocks, BS, SB, BS) * chosen[:, None, :, None].astype(BF16)
    return shaped.reshape(blocks * BS, SN)


def sum_over_rows(values):
    count = lax.axis_size("rows")
    if count & (count - 1):
        return lax.psum(values, "rows")
    step = 1
    while step < count:
        values = values + lax.ppermute(values, "rows", [(i, i ^ step) for i in range(count)])
        step *= 2
    return values


def general_path(win_rows, anc_rows, win_pattern, anc_pattern, window_owner, sn_order, diag_inv, win_rhs, anc_rhs):
    columns_rhs = win_rhs.shape[1]
    slot_count = win_rows.shape[0] // BS
    first_slot = lax.axis_index("rows") * slot_count
    local_pattern = lax.dynamic_slice_in_dim(win_pattern, first_slot, slot_count, 0)

    def step(position, carry):
        solution, win_resid, anc_resid = carry
        node_label = sn_order[position]
        owners = lax.dynamic_slice_in_dim(window_owner, node_label * SB, SB, 0)
        inverse = lax.dynamic_index_in_dim(diag_inv, node_label, 0, keepdims=False)
        local_place = owners - first_slot
        present = (local_place >= 0) & (local_place < slot_count)
        resid_blocks = win_resid.reshape(slot_count, BS, columns_rhs)
        taken = jnp.take(resid_blocks, jnp.clip(local_place, 0, slot_count - 1), axis=0)
        placed = jnp.where(present[:, None, None], taken, 0.0).reshape(SN, columns_rhs)
        panel = sum_over_rows(placed.astype(BF16))
        solved = jnp.dot(inverse, panel, preferred_element_type=F32).astype(BF16)
        solution = lax.dynamic_update_slice_in_dim(solution, solved, node_label * SN, 0)
        win_part = jnp.dot(masked_columns(win_rows, local_pattern, node_label), solved, preferred_element_type=F32)
        anc_part = jnp.dot(masked_columns(anc_rows, anc_pattern, node_label), solved, preferred_element_type=F32)
        return solution, win_resid - win_part, anc_resid - anc_part

    first = (jnp.zeros((NW, columns_rhs), BF16), win_rhs.astype(F32), anc_rhs.astype(F32))
    solution, _, anc_resid = lax.fori_loop(0, NSUP, step, first)
    return solution, anc_resid.astype(BF16)


def spread_matrix():
    block_index = lax.broadcasted_iota(jnp.int32, (NWB, SN), 0)
    lane_index = lax.broadcasted_iota(jnp.int32, (NWB, SN), 1)
    return (block_index % SB == lane_index // BS).astype(F32).astype(BF16)


def expand_mask(rows_pattern, label, spread):
    lane = lax.broadcasted_iota(jnp.int32, rows_pattern.shape, 1)
    chosen = jnp.where(lane // SB == label, rows_pattern, 0).astype(F32).astype(BF16)
    return jnp.dot(chosen, spread, preferred_element_type=F32).astype(BF16)


def masked_rows(block_of, mask, count):
    return jnp.concatenate([block_of(j) * mask[j:j + 1, :] for j in range(count)], axis=0)


def rows_at(index):
    return pl.ds(pl.multiple_of(index * BS, BS), BS)


def columns_at(label):
    return pl.ds(pl.multiple_of(label * SN, SN), SN)


SRC, LSRC, PACK, TABLE = 0, 64, 96, 128


def factor_kernel(owner, order, pattern, win_ref, out, buf, pat, inv, pos, sem):
    row = lax.axis_index("rows")

    def note_slot(w, carry):
        slot = owner[w]

        @pl.when(slot // SB == row)
        def _():
            inv[slot % SB] = w

        return carry

    lax.fori_loop(0, NWB, note_slot, 0, unroll=8)
    for k in range(NSUP):
        pos[order[k]] = k
    labels = jnp.zeros((SB, 1), jnp.int32)
    for t in range(SB):
        label = order[(pos[inv[t] // SB] // 2) * 2]
        pltpu.make_async_copy(win_ref.at[pl.ds(t * BS, BS), columns_at(label)], buf.at[pl.ds(t * BS, BS), :], sem).start()
        labels = jnp.where(lax.broadcasted_iota(jnp.int32, (SB, 1), 0) == t, label, labels)
    pat[...] = pattern[pl.ds(pl.multiple_of(row * SB, SB), SB), :]
    mask = expand_mask(pat[...], labels, spread_matrix())
    pltpu.make_async_copy(win_ref.at[:, pl.ds(0, SN)], buf, sem).wait()
    for j in range(SB):
        out[j * BS:(j + 1) * BS, :] = buf[j * BS:(j + 1) * BS, :] * mask[j:j + 1, :]


def rhs_kernel(rhs_ref, *sent):
    depth = lax.axis_index("rhs")
    width = sent[0].shape[1]
    for s, out in enumerate(sent):
        at = pl.multiple_of(jnp.bitwise_xor(depth, s) * width, width)
        out[...] = rhs_ref[:, pl.ds(at, width)]


def table_kernel(owner, order, tab, flag, cnt):
    row = lax.axis_index("rows")
    chip, core = row // 2, row % 2
    flag[0] = 0
    flag[1] = lax.axis_index("rhs")
    for t in range(GROUPS * SB):
        tab[PACK + t] = 0
    for group in range(GROUPS):
        for t in range(4):
            cnt[t] = 0

        def one(i, carry, group=group):
            slot = owner[order[2 * group + i // SB] * SB + i % SB]
            where, device = slot // (2 * SB), slot // SB
            rank = cnt[where]
            cnt[where] = rank + 1
            flag[0] = jnp.where(rank >= SB, 1, flag[0])
            rank = jnp.minimum(rank, SB - 1)
            rel = jnp.bitwise_xor(where, chip)
            diagonal = rel == 3
            source = jnp.where(rel == 0, 0, jnp.where(diagonal, jnp.where(rank // 4 == core, 3, 4),
                                                      jnp.where(rel == 1 + core, 1, 2)))
            tab[SRC + group * 16 + i] = source * SB + jnp.where(diagonal, rank % 4, rank)

            @pl.when(rel == 0)
            def _():
                tab[PACK + group * SB + rank] = jnp.bitwise_xor(device % 2, core) * SB + slot % SB

            @pl.when(i >= SB)
            def _():
                kind = jnp.where(rel == 0, 0, jnp.where(diagonal, 3, jnp.where(rel == 1 + core, 1, 2)))
                tab[LSRC + group * SB + i - SB] = (2 * kind + jnp.where(device % 2 == core, 0, 1)) * SB + slot % SB

            return carry

        lax.fori_loop(0, 2 * SB, one, 0, unroll=True)


def below_rhs_kernel(rhs_ref, *refs):
    outs, sems = refs[:-1], refs[-1]
    depth = lax.axis_index("rhs")
    width = outs[0].shape[1]
    copies = []
    for s, out in enumerate(outs):
        at = pl.multiple_of(jnp.bitwise_xor(depth, s) * width, width)
        copies.append(pltpu.make_async_copy(rhs_ref.at[:, pl.ds(at, width)], out, sems.at[s]))
        copies[-1].start()
    for c in copies:
        c.wait()


def first_pack_kernel(tab, *refs):
    pieces, (chip_rhs, p_ref, b_ref) = refs[:8], refs[8:]
    depth, core = lax.axis_index("rhs"), lax.axis_index("rows") % 2
    tall = pieces[0].shape[0]
    for side in range(2):
        for s in range(4):
            at = pl.multiple_of(side * SB * BS + jnp.bitwise_xor(depth, s) * tall, tall)
            chip_rhs[pl.ds(at, tall), :] = pieces[4 * side + s][...]
    for j in range(SB):
        p_ref[j * BS:(j + 1) * BS, :] = chip_rhs[rows_at(tab[PACK + j]), :]
    b_ref[...] = p_ref[pl.ds(pl.multiple_of(core * SB // 2 * BS, SB // 2 * BS), SB // 2 * BS), :]


def make_mask_kernel(group):
    def kernel(tab, order, pattern, w_own, w_other, out, pat):
        row = lax.axis_index("rows")
        places = [tab[PACK + (group + 1) * SB + j] for j in range(SB)]
        for j, place in enumerate(places):
            pat[j:j + 1, :] = pattern[pl.ds(jnp.bitwise_xor(row, place // SB) * SB + place % SB, 1), :]
        spread = spread_matrix()
        rows = pat[...]
        masks = [expand_mask(rows, order[k], spread) for k in range(2 * group + 2)]
        for j, place in enumerate(places):
            at = slice(j * BS, (j + 1) * BS)
            for side, w_ref in enumerate((w_own, w_other)):
                @pl.when(place // SB == side)
                def _(w_ref=w_ref, at=at, j=j, place=place):
                    for k in range(2 * group + 2):
                        block = w_ref[rows_at(place % SB), columns_at(order[k])]
                        out[at, k * SN:(k + 1) * SN] = block * masks[k][j:j + 1, :]

    return kernel


def make_prep_kernel(group):
    last = group == GROUPS - 1

    def kernel(tab, order, diag, *refs):
        l_refs, refs = refs[:8], refs[8:]
        if last:
            m_out, lbuf = refs
        else:
            w_ref, chip_rhs = refs[:2]
            xs = refs[2:2 + group]
            m_out, r_out, lbuf = refs[2 + group:]
        for i in range(SB):
            code = tab[LSRC + group * SB + i]
            for m in range(8):
                @pl.when(code // SB == m)
                def _(m=m, i=i, code=code):
                    lbuf[i * BS:(i + 1) * BS, :] = l_refs[m][rows_at(code % SB), :]
        first, second = diag[order[2 * group]], diag[order[2 * group + 1]]
        m_out[0:SN, 0:SN] = first
        m_out[SN:PAIR, SN:PAIR] = second
        joined = jnp.dot(second, lbuf[...], preferred_element_type=F32).astype(BF16)
        m_out[SN:PAIR, 0:SN] = (-jnp.dot(joined, first, preferred_element_type=F32)).astype(BF16)
        if not last:
            total = jnp.concatenate([chip_rhs[rows_at(tab[PACK + (group + 1) * SB + j]), :] for j in range(SB)], axis=0).astype(F32)
            for k in range(group):
                total = total - jnp.dot(w_ref[:, k * PAIR:(k + 1) * PAIR], xs[k][...], preferred_element_type=F32)
            r_out[...] = total

    return kernel


def make_solve_kernel(group):
    last = group == GROUPS - 1

    def kernel(*refs):
        tab, sources, m_ref = refs[0], refs[1:6], refs[6]
        if last:
            x_ref, panel = refs[7:]
        else:
            r_ref, wn_ref, x_ref, p_ref, b_ref, panel = refs[7:]
        for i in range(2 * SB):
            code = tab[SRC + group * 16 + i]
            for which, source in enumerate(sources):
                @pl.when(code // SB == which)
                def _(source=source, i=i, code=code):
                    panel[i * BS:(i + 1) * BS, :] = source[rows_at(code % SB), :]
        x_ref[0:SN, :] = jnp.dot(m_ref[0:SN, 0:SN], panel[0:SN, :], preferred_element_type=F32).astype(BF16)
        x_ref[SN:PAIR, :] = jnp.dot(m_ref[SN:PAIR, :], panel[...], preferred_element_type=F32).astype(BF16)
        if last:
            return
        total = r_ref[...] - jnp.dot(wn_ref[:, group * PAIR:(group + 1) * PAIR], x_ref[...], preferred_element_type=F32)
        p_ref[...] = total.astype(BF16)
        core = lax.axis_index("rows") % 2
        b_ref[...] = p_ref[pl.ds(pl.multiple_of(core * SB // 2 * BS, SB // 2 * BS), SB // 2 * BS), :]

    return kernel


def make_below_mask_kernel(tile):
    def kernel(pattern, a_ref, out, sems):
        copies = []
        for j in range(SB):
            c = pltpu.make_async_copy(a_ref.at[pl.ds((tile * SB + j) * BS, BS), :], out.at[pl.ds(j * BS, BS), :], sems.at[j])
            c.start()
            copies.append(c)
        spread = spread_matrix()
        rows = pattern[tile * SB:(tile + 1) * SB, :]
        masks = [expand_mask(rows, k, spread) for k in range(NSUP)]
        for j in range(SB):
            copies[j].wait()
            for k in range(NSUP):
                at = (slice(j * BS, (j + 1) * BS), slice(k * SN, (k + 1) * SN))
                out[at] = out[at] * masks[k][j:j + 1, :]

    return kernel


def below_product(order, a_ref, x_ref, group):
    first = jnp.dot(a_ref[:, columns_at(order[2 * group])], x_ref[0:SN, :], preferred_element_type=F32)
    return first + jnp.dot(a_ref[:, columns_at(order[2 * group + 1])], x_ref[SN:PAIR, :], preferred_element_type=F32)


def first_rows_kernel(order, a0, a1, a2, a3, x_ref, out):
    for i, a_ref in enumerate((a0, a1, a2, a3)):
        out[i * SN:(i + 1) * SN, :] = below_product(order, a_ref, x_ref, 0)


def next_rows_kernel(order, a0, a1, a2, a3, x_ref, sums, out):
    for i, a_ref in enumerate((a0, a1, a2, a3)):
        at = slice(i * SN, (i + 1) * SN)
        out[at, :] = sums[at, :] + below_product(order, a_ref, x_ref, 1)


def base_rows_kernel(order, a0, a1, a2, a3, x_ref, sums, h0, h1, h2, h3, out, rhs):
    depth = lax.axis_index("rhs")
    tall = h0.shape[0]
    for s, h in enumerate((h0, h1, h2, h3)):
        rhs[pl.ds(pl.multiple_of(jnp.bitwise_xor(depth, s) * tall, tall), tall), :] = h[...]
    for i, a_ref in enumerate((a0, a1, a2, a3)):
        at = slice(i * SN, (i + 1) * SN)
        out[at, :] = rhs[at, :].astype(F32) - (sums[at, :] + below_product(order, a_ref, x_ref, 2))


def last_rows_kernel(order, a0, a1, a2, a3, x0, x1, x2, x3, base, sol_ref, out_ref, done, sems, osem):
    copies = []
    for k, x in enumerate((x0, x1, x2, x3)):
        for q in range(2):
            at = pl.multiple_of(order[2 * k + q] * SN, SN)
            copies.append(pltpu.make_async_copy(x.at[pl.ds(q * SN, SN), :], sol_ref.at[pl.ds(at, SN), :], sems.at[2 * k + q]))
            copies[-1].start()
    for i, a_ref in enumerate((a0, a1, a2, a3)):
        at = slice(i * SN, (i + 1) * SN)
        done[at, :] = (base[at, :] - below_product(order, a_ref, x3, GROUPS - 1)).astype(BF16)
        copies.append(pltpu.make_async_copy(done.at[pl.ds(i * SN, SN), :], out_ref.at[pl.ds(i * SN, SN), :], osem.at[i]))
        copies[-1].start()
    for c in copies:
        c.wait()


def in_vmem(x):
    return pltpu.with_memory_space_constraint(x, pltpu.VMEM)


def in_hbm(x):
    return pltpu.with_memory_space_constraint(x, pltpu.HBM)


SMEM = pl.BlockSpec(memory_space=pltpu.SMEM)
VMEM = pl.BlockSpec(memory_space=pltpu.VMEM)
HBM = pl.BlockSpec(memory_space=pltpu.HBM)


def params(mib):
    return pltpu.CompilerParams(vmem_limit_bytes=mib * 1024 * 1024)


def cost(micros):
    return pl.CostEstimate(flops=micros * 10 ** 8, bytes_accessed=micros * 3 * 10 ** 6, transcendentals=0)


def shape_of(dims, dtype=BF16):
    return jax.ShapeDtypeStruct(dims, dtype)


def local(win_rows, anc_rows, win_pattern, anc_pattern, window_owner, sn_order, diag_inv, rhs_win, rhs_anc):
    if lax.axis_size("rows") != 8 or lax.axis_size("rhs") != 4 or anc_rows.shape[0] != 4 * SB * BS:
        win_rhs = lax.all_to_all(rhs_win, "rhs", split_axis=1, concat_axis=0, tiled=True)
        anc_rhs = lax.all_to_all(rhs_anc, "rhs", split_axis=1, concat_axis=0, tiled=True)
        return general_path(win_rows, anc_rows, win_pattern, anc_pattern, window_owner, sn_order, diag_inv, win_rhs, anc_rhs)

    def swap(x, m):
        return lax.ppermute(x, "rows", [(i, i ^ m) for i in range(8)])

    def deep(x, m):
        return lax.ppermute(x, "rhs", [(i, i ^ m) for i in range(4)])

    def neighbour(x):
        return lax.ppermute(x, "rows", [(i, i ^ (2 if i % 2 == 0 else 4)) for i in range(8)])

    def forward(x):
        return lax.ppermute(x, "rows", [(i, i ^ (4 if i % 2 == 0 else 2)) for i in range(8)])

    def mask_below(k, after):
        pattern_later, _ = lax.optimization_barrier((anc_pattern, after))
        return pl.pallas_call(
            make_below_mask_kernel(k),
            out_shape=shape_of((SN, NW)),
            in_specs=[VMEM, HBM],
            out_specs=VMEM,
            scratch_shapes=[pltpu.SemaphoreType.DMA((SB,))],
            compiler_params=params(4),
            cost_estimate=cost(2),
            name="mask_below",
        )(pattern_later, in_hbm(anc_rows))

    columns = rhs_win.shape[1] // 4
    half = SN // 2
    tall = rhs_win.shape[0]
    w_own = in_hbm(win_rows)
    l_own = pl.pallas_call(
        factor_kernel,
        out_shape=shape_of((SN, SN)),
        in_specs=[SMEM, SMEM, VMEM, HBM],
        out_specs=VMEM,
        scratch_shapes=[pltpu.VMEM((SN, SN), BF16), pltpu.VMEM((SB, NWB), jnp.int32),
                        pltpu.SMEM((SB,), jnp.int32), pltpu.SMEM((SB,), jnp.int32), pltpu.SemaphoreType.DMA],
        compiler_params=params(4),
        cost_estimate=cost(2),
        name="factor_pack",
    )(window_owner, sn_order, win_pattern, w_own)
    near = neighbour(l_own)
    l_other = swap(l_own, 1)
    rhs_late, _ = lax.optimization_barrier((rhs_win, l_own))
    sent = pl.pallas_call(
        rhs_kernel,
        out_shape=(shape_of((tall, columns)),) * 4,
        in_specs=[VMEM],
        out_specs=(VMEM,) * 4,
        compiler_params=params(4),
        cost_estimate=cost(1),
        name="rhs_pack",
    )(rhs_late)
    l_other, *sent = lax.optimization_barrier((l_other, *sent))
    near_other = neighbour(l_other)
    pieces = [sent[0]] + [deep(sent[s], s) for s in (1, 2, 3)]
    owner_later, _ = lax.optimization_barrier((window_owner, sent[0]))
    tab, flag = pl.pallas_call(
        table_kernel,
        out_shape=(shape_of((TABLE,), jnp.int32), shape_of((2,), jnp.int32)),
        in_specs=[SMEM, SMEM],
        out_specs=(SMEM, SMEM),
        scratch_shapes=[pltpu.SMEM((4,), jnp.int32)],
        compiler_params=params(4),
        cost_estimate=cost(3),
        name="tables",
    )(owner_later, sn_order)
    w_other = swap(win_rows, 1)
    below = [mask_below(0, sent[0])]
    tab, w_other, below[0], *pieces = lax.optimization_barrier((tab, w_other, below[0], *pieces))
    others = [swap(x, 1) for x in pieces]
    chip_rhs, packed, part = pl.pallas_call(
        first_pack_kernel,
        out_shape=(shape_of((PAIR, columns)), shape_of((SN, columns)), shape_of((half, columns))),
        in_specs=[SMEM] + [VMEM] * 8,
        out_specs=(VMEM,) * 3,
        compiler_params=params(4),
        cost_estimate=cost(1),
        name="first_pack",
    )(tab, *pieces, *others)
    near, near_other, _ = lax.optimization_barrier((near, near_other, packed))
    far = forward(near)
    l_parts = [x for x in (l_own, l_other, near, near_other, swap(near_other, 1), swap(near, 1), far)]
    w_other = in_vmem(w_other)
    w_own = in_vmem(win_rows)

    tile = rhs_anc.shape[0]
    sums, solved, masked = None, [], []
    diag_vmem = in_vmem(diag_inv)
    below_rows = anc_rows.shape[0]

    anc_order, anc_pieces = (2, 3, 1), [None] * 4
    for group in range(GROUPS):
        last = group == GROUPS - 1
        a_own = neighbour(packed)
        b_own = swap(part, 6)
        if group == 0:
            far_late, *_ = lax.optimization_barrier((far, a_own, b_own))
            l_parts = [in_vmem(x) for x in (*l_parts, swap(far_late, 1))]
            below += [mask_below(k, packed) for k in (1, 2, 3)]
            tab_later, order_later, _ = lax.optimization_barrier((tab, sn_order, packed))
            for k in range(GROUPS - 1):
                masked.append(pl.pallas_call(
                    make_mask_kernel(k),
                    out_shape=shape_of((SN, (k + 1) * PAIR)),
                    in_specs=[SMEM, SMEM, VMEM, VMEM, VMEM],
                    out_specs=VMEM,
                    scratch_shapes=[pltpu.VMEM((SB, NWB), jnp.int32)],
                    compiler_params=params(6),
                    cost_estimate=cost(2),
                    name="mask_rows",
                )(tab_later, order_later, win_pattern, w_own, w_other))
        if group == 0:
            rhs_later, _ = lax.optimization_barrier((rhs_anc, packed))
            anc_pieces = list(pl.pallas_call(
                below_rhs_kernel,
                out_shape=(shape_of((tile, columns)),) * 4,
                in_specs=[HBM],
                out_specs=(VMEM,) * 4,
                scratch_shapes=[pltpu.SemaphoreType.DMA((4,))],
                compiler_params=params(4),
                cost_estimate=cost(1),
                name="below_rhs",
            )(in_hbm(rhs_later)))
        if not last:
            s = anc_order[group]
            moved, _ = lax.optimization_barrier((anc_pieces[s], packed))
            anc_pieces[s] = deep(moved, s)

        operands = [tab, sn_order, diag_vmem, *l_parts]
        out_shape = [shape_of((PAIR, PAIR))]
        if not last:
            operands += [masked[group], chip_rhs, *solved]
            out_shape += [shape_of((SN, columns), F32)]
        ready = pl.pallas_call(
            make_prep_kernel(group),
            out_shape=tuple(out_shape),
            in_specs=[SMEM, SMEM] + [VMEM] * (len(operands) - 2),
            out_specs=(VMEM,) * len(out_shape),
            scratch_shapes=[pltpu.VMEM((SN, SN), BF16)],
            compiler_params=params(6),
            cost_estimate=cost(2),
            name="prep",
        )(*operands)
        if group > 0:
            k = group - 1
            previous = anc_pieces[anc_order[k]]
            if k < 2:
                more, kernel = ([], first_rows_kernel) if k == 0 else ([sums], next_rows_kernel)
            else:
                more, kernel = [sums, *anc_pieces], base_rows_kernel
            sums = pl.pallas_call(
                kernel,
                out_shape=shape_of((below_rows, columns), F32),
                in_specs=[SMEM] + [VMEM] * (5 + len(more)),
                out_specs=VMEM,
                scratch_shapes=[pltpu.VMEM((below_rows, columns), BF16)] if k == 2 else [],
                input_output_aliases={6: 0} if more else {},
                compiler_params=params(6),
                cost_estimate=cost(3),
                name="rows_below",
            )(sn_order, *below, solved[k], *more)
            a_own, b_own, sums, previous, *ready = lax.optimization_barrier((a_own, b_own, sums, previous, *ready))
            anc_pieces[anc_order[k]] = previous
        else:
            a_own, b_own, below[1], below[2], below[3], *masked = lax.optimization_barrier(
                (a_own, b_own, below[1], below[2], below[3], *masked))
        a_swap = swap(a_own, 1)
        b_swap = swap(b_own, 1)
        ready = list(ready) if last else list(ready) + [masked[group]]

        out_shape = [shape_of((PAIR, columns))]
        if not last:
            out_shape += [shape_of((SN, columns)), shape_of((half, columns))]
        results = pl.pallas_call(
            make_solve_kernel(group),
            out_shape=tuple(out_shape),
            in_specs=[SMEM] + [VMEM] * (5 + len(ready)),
            out_specs=(VMEM,) * len(out_shape),
            scratch_shapes=[pltpu.VMEM((PAIR, columns), BF16)],
            compiler_params=params(8),
            cost_estimate=cost(3),
            name="pair_solve",
        )(tab, packed, a_own, a_swap, b_own, b_swap, *ready)
        solved.append(results[0])
        if not last:
            packed, part = results[1:]

    outputs = pl.pallas_call(
        last_rows_kernel,
        out_shape=(shape_of((NW, columns)), shape_of((below_rows, columns))),
        in_specs=[SMEM] + [VMEM] * 9,
        out_specs=(HBM, HBM),
        scratch_shapes=[pltpu.VMEM((below_rows, columns), BF16), pltpu.SemaphoreType.DMA((2 * GROUPS,)),
                        pltpu.SemaphoreType.DMA((4,))],
        compiler_params=params(6),
        cost_estimate=cost(3),
        name="last_rows",
    )(sn_order, *below, *solved, sums)

    def again(carry):
        carry, own_pieces, below_pieces = lax.optimization_barrier((carry, pieces, anc_pieces))
        back = carry[0][1] ^ jnp.arange(4)
        win_rhs = jnp.take(jnp.stack(own_pieces), back, axis=0).reshape(4 * tall, columns)
        anc_rhs = jnp.take(jnp.stack(below_pieces), back, axis=0).reshape(4 * tile, columns)
        return jnp.zeros_like(carry[0]), *general_path(
            win_rows, anc_rows, win_pattern, anc_pattern, window_owner, sn_order, diag_inv, win_rhs, anc_rhs)

    return tuple(lax.while_loop(lambda carry: carry[0][0] != 0, again, (flag, *outputs))[1:])


def solution(mesh):
    return jax.shard_map(
        local,
        mesh=mesh,
        in_specs=(P("rows", None), P("rows", None), P(), P("rows", None), P(), P(), P(),
                  P(("rows", "rhs"), None), P(("rows", "rhs"), None)),
        out_specs=(P(None, "rhs"), P("rows", "rhs")),
        check_vma=False,
    )
```

```python
import jax
import jax.numpy as jnp
from jax import lax
from jax.experimental import pallas as pl
from jax.experimental.pallas import tpu as pltpu
from jax.sharding import PartitionSpec as P

BS = 64
SB = 8
NSUP = 8
SN = 512
NW = 4096
NWB = 64
GROUPS = 4
PAIR = 2 * SN
F32 = jnp.float32
BF16 = jnp.bfloat16


def masked_columns(factor, pattern, node_label):
    blocks = pattern.shape[0]
    columns = lax.dynamic_slice_in_dim(factor, node_label * SN, SN, 1)
    chosen = lax.dynamic_slice_in_dim(pattern, node_label * SB, SB, 1)
    shaped = columns.reshape(blocks, BS, SB, BS) * chosen[:, None, :, None].astype(BF16)
    return shaped.reshape(blocks * BS, SN)


def sum_over_rows(values):
    count = lax.axis_size("rows")
    if count & (count - 1):
        return lax.psum(values, "rows")
    step = 1
    while step < count:
        values = values + lax.ppermute(values, "rows", [(i, i ^ step) for i in range(count)])
        step *= 2
    return values


def general_path(win_rows, anc_rows, win_pattern, anc_pattern, window_owner, sn_order, diag_inv, win_rhs, anc_rhs):
    columns_rhs = win_rhs.shape[1]
    slot_count = win_rows.shape[0] // BS
    first_slot = lax.axis_index("rows") * slot_count
    local_pattern = lax.dynamic_slice_in_dim(win_pattern, first_slot, slot_count, 0)

    def step(position, carry):
        solution, win_resid, anc_resid = carry
        node_label = sn_order[position]
        owners = lax.dynamic_slice_in_dim(window_owner, node_label * SB, SB, 0)
        inverse = lax.dynamic_index_in_dim(diag_inv, node_label, 0, keepdims=False)
        local_place = owners - first_slot
        present = (local_place >= 0) & (local_place < slot_count)
        resid_blocks = win_resid.reshape(slot_count, BS, columns_rhs)
        taken = jnp.take(resid_blocks, jnp.clip(local_place, 0, slot_count - 1), axis=0)
        placed = jnp.where(present[:, None, None], taken, 0.0).reshape(SN, columns_rhs)
        panel = sum_over_rows(placed.astype(BF16))
        solved = jnp.dot(inverse, panel, preferred_element_type=F32).astype(BF16)
        solution = lax.dynamic_update_slice_in_dim(solution, solved, node_label * SN, 0)
        win_part = jnp.dot(masked_columns(win_rows, local_pattern, node_label), solved, preferred_element_type=F32)
        anc_part = jnp.dot(masked_columns(anc_rows, anc_pattern, node_label), solved, preferred_element_type=F32)
        return solution, win_resid - win_part, anc_resid - anc_part

    first = (jnp.zeros((NW, columns_rhs), BF16), win_rhs.astype(F32), anc_rhs.astype(F32))
    solution, _, anc_resid = lax.fori_loop(0, NSUP, step, first)
    return solution, anc_resid.astype(BF16)


def spread_matrix():
    block_index = lax.broadcasted_iota(jnp.int32, (NWB, SN), 0)
    lane_index = lax.broadcasted_iota(jnp.int32, (NWB, SN), 1)
    return (block_index % SB == lane_index // BS).astype(F32).astype(BF16)


def expand_mask(rows_pattern, label, spread):
    lane = lax.broadcasted_iota(jnp.int32, rows_pattern.shape, 1)
    chosen = jnp.where(lane // SB == label, rows_pattern, 0).astype(F32).astype(BF16)
    return jnp.dot(chosen, spread, preferred_element_type=F32).astype(BF16)


def masked_rows(block_of, mask, count):
    return jnp.concatenate([block_of(j) * mask[j:j + 1, :] for j in range(count)], axis=0)


def rows_at(index):
    return pl.ds(pl.multiple_of(index * BS, BS), BS)


def columns_at(label):
    return pl.ds(pl.multiple_of(label * SN, SN), SN)


SRC, LSRC, PACK, TABLE = 0, 64, 96, 128


def factor_kernel(owner, order, pattern, win_ref, out, buf, pat, inv, pos, sem):
    row = lax.axis_index("rows")

    def note_slot(w, carry):
        slot = owner[w]

        @pl.when(slot // SB == row)
        def _():
            inv[slot % SB] = w

        return carry

    lax.fori_loop(0, NWB, note_slot, 0, unroll=8)
    for k in range(NSUP):
        pos[order[k]] = k
    labels = jnp.zeros((SB, 1), jnp.int32)
    for t in range(SB):
        label = order[(pos[inv[t] // SB] // 2) * 2]
        pltpu.make_async_copy(win_ref.at[pl.ds(t * BS, BS), columns_at(label)], buf.at[pl.ds(t * BS, BS), :], sem).start()
        labels = jnp.where(lax.broadcasted_iota(jnp.int32, (SB, 1), 0) == t, label, labels)
    pat[...] = pattern[pl.ds(pl.multiple_of(row * SB, SB), SB), :]
    mask = expand_mask(pat[...], labels, spread_matrix())
    pltpu.make_async_copy(win_ref.at[:, pl.ds(0, SN)], buf, sem).wait()
    for j in range(SB):
        out[j * BS:(j + 1) * BS, :] = buf[j * BS:(j + 1) * BS, :] * mask[j:j + 1, :]


def start_pack_kernel(own_ref, other_ref, rhs_ref, l_chip, *sent):
    l_chip[0:SN, :] = own_ref[...]
    l_chip[SN:PAIR, :] = other_ref[...]
    depth = lax.axis_index("rhs")
    width = sent[0].shape[1]
    for s, out in enumerate(sent):
        at = pl.multiple_of(jnp.bitwise_xor(depth, s) * width, width)
        out[...] = rhs_ref[:, pl.ds(at, width)]


def take_half_kernel(x_ref, out):
    out[...] = x_ref[0:SN, :]


def table_kernel(owner, order, tab, flag, cnt):
    row = lax.axis_index("rows")
    chip, core = row // 2, row % 2
    flag[0] = 0
    flag[1] = lax.axis_index("rhs")
    for t in range(GROUPS * SB):
        tab[PACK + t] = 0
    for group in range(GROUPS):
        for t in range(4):
            cnt[t] = 0

        def one(i, carry, group=group):
            slot = owner[order[2 * group + i // SB] * SB + i % SB]
            where, device = slot // (2 * SB), slot // SB
            rank = cnt[where]
            cnt[where] = rank + 1
            flag[0] = jnp.where(rank >= SB, 1, flag[0])
            rank = jnp.minimum(rank, SB - 1)
            rel = jnp.bitwise_xor(where, chip)
            diagonal = rel == 3
            source = jnp.where(rel == 0, 0, jnp.where(diagonal, jnp.where(rank // 4 == core, 3, 4),
                                                      jnp.where(rel == 1 + core, 1, 2)))
            tab[SRC + group * 16 + i] = source * SB + jnp.where(diagonal, rank % 4, rank)

            @pl.when(rel == 0)
            def _():
                tab[PACK + group * SB + rank] = jnp.bitwise_xor(device % 2, core) * SB + slot % SB

            @pl.when(i >= SB)
            def _():
                kind = jnp.where(rel == 0, 0, jnp.where(diagonal, 3, jnp.where(rel == 1 + core, 1, 2)))
                tab[LSRC + group * SB + i - SB] = (2 * kind + jnp.where(device % 2 == core, 0, 1)) * SB + slot % SB

            return carry

        lax.fori_loop(0, 2 * SB, one, 0, unroll=True)


def below_rhs_kernel(rhs_ref, *refs):
    outs, sems = refs[:-1], refs[-1]
    depth = lax.axis_index("rhs")
    width = outs[0].shape[1]
    copies = []
    for s, out in enumerate(outs):
        at = pl.multiple_of(jnp.bitwise_xor(depth, s) * width, width)
        copies.append(pltpu.make_async_copy(rhs_ref.at[:, pl.ds(at, width)], out, sems.at[s]))
        copies[-1].start()
    for c in copies:
        c.wait()


def first_pack_kernel(owner, order, *refs):
    pieces, (chip_rhs, p_ref, b_ref, count) = refs[:8], refs[8:]
    row, depth = lax.axis_index("rows"), lax.axis_index("rhs")
    core = row % 2
    tall = pieces[0].shape[0]
    for side in range(2):
        for s in range(4):
            at = pl.multiple_of(side * SB * BS + jnp.bitwise_xor(depth, s) * tall, tall)
            chip_rhs[pl.ds(at, tall), :] = pieces[4 * side + s][...]
    count[0] = 0
    for i in range(2 * SB):
        slot = owner[order[i // SB] * SB + i % SB]

        @pl.when(slot // (2 * SB) == row // 2)
        def _(slot=slot):
            rank = count[0]
            count[0] = rank + 1
            place = jnp.bitwise_xor((slot // SB) % 2, core) * SB + slot % SB

            @pl.when(rank < SB)
            def _():
                p_ref[rows_at(rank), :] = chip_rhs[rows_at(place), :]

    b_ref[...] = p_ref[pl.ds(pl.multiple_of(core * SB // 2 * BS, SB // 2 * BS), SB // 2 * BS), :]


def make_mask_kernel(group):
    def kernel(tab, order, pattern, w_own, w_other, out, pat):
        row = lax.axis_index("rows")
        places = [tab[PACK + (group + 1) * SB + j] for j in range(SB)]
        for j, place in enumerate(places):
            pat[j:j + 1, :] = pattern[pl.ds(jnp.bitwise_xor(row, place // SB) * SB + place % SB, 1), :]
        spread = spread_matrix()
        rows = pat[...]
        masks = [expand_mask(rows, order[k], spread) for k in range(2 * group + 2)]
        for j, place in enumerate(places):
            at = slice(j * BS, (j + 1) * BS)
            for side, w_ref in enumerate((w_own, w_other)):
                @pl.when(place // SB == side)
                def _(w_ref=w_ref, at=at, j=j, place=place):
                    for k in range(2 * group + 2):
                        block = w_ref[rows_at(place % SB), columns_at(order[k])]
                        out[at, k * SN:(k + 1) * SN] = block * masks[k][j:j + 1, :]

    return kernel


def make_prep_kernel(group):
    last = group == GROUPS - 1

    def kernel(tab, order, diag, *refs):
        own, other, near, near_swap, far, far_swap = refs[:6]
        l_refs = ((own, 0), (other, 0), (near, 0), (near, SB), (near_swap, SB), (near_swap, 0), (far, 0), (far_swap, 0))
        refs = refs[6:]
        if last:
            m_out, lbuf = refs
        else:
            w_ref, chip_rhs = refs[:2]
            xs = refs[2:2 + group]
            m_out, r_out, lbuf = refs[2 + group:]
        for i in range(SB):
            code = tab[LSRC + group * SB + i]
            for m in range(8):
                @pl.when(code // SB == m)
                def _(m=m, i=i, code=code):
                    lbuf[i * BS:(i + 1) * BS, :] = l_refs[m][0][rows_at(code % SB + l_refs[m][1]), :]
        first, second = diag[order[2 * group]], diag[order[2 * group + 1]]
        m_out[0:SN, 0:SN] = first
        m_out[SN:PAIR, SN:PAIR] = second
        joined = jnp.dot(second, lbuf[...], preferred_element_type=F32).astype(BF16)
        m_out[SN:PAIR, 0:SN] = (-jnp.dot(joined, first, preferred_element_type=F32)).astype(BF16)
        if not last:
            total = jnp.concatenate([chip_rhs[rows_at(tab[PACK + (group + 1) * SB + j]), :] for j in range(SB)], axis=0).astype(F32)
            for k in range(group):
                total = total - jnp.dot(w_ref[:, k * PAIR:(k + 1) * PAIR], xs[k][...], preferred_element_type=F32)
            r_out[...] = total

    return kernel


def make_solve_kernel(group):
    last = group == GROUPS - 1

    def kernel(*refs):
        tab, sources, m_ref = refs[0], refs[1:6], refs[6]
        if last:
            x_ref, panel = refs[7:]
        else:
            r_ref, wn_ref, x_ref, p_ref, b_ref, panel = refs[7:]
        for i in range(2 * SB):
            code = tab[SRC + group * 16 + i]
            for which, source in enumerate(sources):
                @pl.when(code // SB == which)
                def _(source=source, i=i, code=code):
                    panel[i * BS:(i + 1) * BS, :] = source[rows_at(code % SB), :]
        x_ref[0:SN, :] = jnp.dot(m_ref[0:SN, 0:SN], panel[0:SN, :], preferred_element_type=F32).astype(BF16)
        x_ref[SN:PAIR, :] = jnp.dot(m_ref[SN:PAIR, :], panel[...], preferred_element_type=F32).astype(BF16)
        if last:
            return
        total = r_ref[...] - jnp.dot(wn_ref[:, group * PAIR:(group + 1) * PAIR], x_ref[...], preferred_element_type=F32)
        p_ref[...] = total.astype(BF16)
        core = lax.axis_index("rows") % 2
        b_ref[...] = p_ref[pl.ds(pl.multiple_of(core * SB // 2 * BS, SB // 2 * BS), SB // 2 * BS), :]

    return kernel


def make_below_mask_kernel(tile):
    def kernel(pattern, a_ref, out, sems):
        copies = []
        for j in range(SB):
            c = pltpu.make_async_copy(a_ref.at[pl.ds((tile * SB + j) * BS, BS), :], out.at[pl.ds(j * BS, BS), :], sems.at[j])
            c.start()
            copies.append(c)
        spread = spread_matrix()
        rows = pattern[tile * SB:(tile + 1) * SB, :]
        masks = [expand_mask(rows, k, spread) for k in range(NSUP)]
        for j in range(SB):
            copies[j].wait()
            for k in range(NSUP):
                at = (slice(j * BS, (j + 1) * BS), slice(k * SN, (k + 1) * SN))
                out[at] = out[at] * masks[k][j:j + 1, :]

    return kernel


def below_product(order, a_ref, x_ref, group):
    first = jnp.dot(a_ref[:, columns_at(order[2 * group])], x_ref[0:SN, :], preferred_element_type=F32)
    return first + jnp.dot(a_ref[:, columns_at(order[2 * group + 1])], x_ref[SN:PAIR, :], preferred_element_type=F32)


def two_rows_kernel(order, a0, a1, a2, a3, x0_ref, x1_ref, out):
    for i, a_ref in enumerate((a0, a1, a2, a3)):
        out[i * SN:(i + 1) * SN, :] = below_product(order, a_ref, x0_ref, 0) + below_product(order, a_ref, x1_ref, 1)


def base_rows_kernel(order, a0, a1, a2, a3, x_ref, sums, h0, h1, h2, h3, out, rhs):
    depth = lax.axis_index("rhs")
    tall = h0.shape[0]
    for s, h in enumerate((h0, h1, h2, h3)):
        rhs[pl.ds(pl.multiple_of(jnp.bitwise_xor(depth, s) * tall, tall), tall), :] = h[...]
    for i, a_ref in enumerate((a0, a1, a2, a3)):
        at = slice(i * SN, (i + 1) * SN)
        out[at, :] = rhs[at, :].astype(F32) - (sums[at, :] + below_product(order, a_ref, x_ref, 2))


def last_rows_kernel(order, a0, a1, a2, a3, x0, x1, x2, x3, base, sol_ref, out_ref, done, sems, osem):
    copies = []
    for k, x in enumerate((x0, x1, x2, x3)):
        for q in range(2):
            at = pl.multiple_of(order[2 * k + q] * SN, SN)
            copies.append(pltpu.make_async_copy(x.at[pl.ds(q * SN, SN), :], sol_ref.at[pl.ds(at, SN), :], sems.at[2 * k + q]))
            copies[-1].start()
    for i, a_ref in enumerate((a0, a1, a2, a3)):
        at = slice(i * SN, (i + 1) * SN)
        done[at, :] = (base[at, :] - below_product(order, a_ref, x3, GROUPS - 1)).astype(BF16)
        copies.append(pltpu.make_async_copy(done.at[pl.ds(i * SN, SN), :], out_ref.at[pl.ds(i * SN, SN), :], osem.at[i]))
        copies[-1].start()
    for c in copies:
        c.wait()


def in_vmem(x):
    return pltpu.with_memory_space_constraint(x, pltpu.VMEM)


def in_hbm(x):
    return pltpu.with_memory_space_constraint(x, pltpu.HBM)


SMEM = pl.BlockSpec(memory_space=pltpu.SMEM)
VMEM = pl.BlockSpec(memory_space=pltpu.VMEM)
HBM = pl.BlockSpec(memory_space=pltpu.HBM)


def params(mib):
    return pltpu.CompilerParams(vmem_limit_bytes=mib * 1024 * 1024)


def cost(micros):
    return pl.CostEstimate(flops=micros * 10 ** 8, bytes_accessed=micros * 3 * 10 ** 6, transcendentals=0)


def shape_of(dims, dtype=BF16):
    return jax.ShapeDtypeStruct(dims, dtype)


def local(win_rows, anc_rows, win_pattern, anc_pattern, window_owner, sn_order, diag_inv, rhs_win, rhs_anc):
    if lax.axis_size("rows") != 8 or lax.axis_size("rhs") != 4 or anc_rows.shape[0] != 4 * SB * BS:
        win_rhs = lax.all_to_all(rhs_win, "rhs", split_axis=1, concat_axis=0, tiled=True)
        anc_rhs = lax.all_to_all(rhs_anc, "rhs", split_axis=1, concat_axis=0, tiled=True)
        return general_path(win_rows, anc_rows, win_pattern, anc_pattern, window_owner, sn_order, diag_inv, win_rhs, anc_rhs)

    def swap(x, m):
        return lax.ppermute(x, "rows", [(i, i ^ m) for i in range(8)])

    def deep(x, m):
        return lax.ppermute(x, "rhs", [(i, i ^ m) for i in range(4)])

    def neighbour(x):
        return lax.ppermute(x, "rows", [(i, i ^ (2 if i % 2 == 0 else 4)) for i in range(8)])

    def forward(x):
        return lax.ppermute(x, "rows", [(i, i ^ (4 if i % 2 == 0 else 2)) for i in range(8)])

    def mask_below(k, after):
        pattern_later, _ = lax.optimization_barrier((anc_pattern, after))
        return pl.pallas_call(
            make_below_mask_kernel(k),
            out_shape=shape_of((SN, NW)),
            in_specs=[VMEM, HBM],
            out_specs=VMEM,
            scratch_shapes=[pltpu.SemaphoreType.DMA((SB,))],
            compiler_params=params(4),
            cost_estimate=cost(2),
            name="mask_below",
        )(pattern_later, in_hbm(anc_rows))

    columns = rhs_win.shape[1] // 4
    half = SN // 2
    tall = rhs_win.shape[0]
    w_own = in_hbm(win_rows)
    l_own = pl.pallas_call(
        factor_kernel,
        out_shape=shape_of((SN, SN)),
        in_specs=[SMEM, SMEM, VMEM, HBM],
        out_specs=VMEM,
        scratch_shapes=[pltpu.VMEM((SN, SN), BF16), pltpu.VMEM((SB, NWB), jnp.int32),
                        pltpu.SMEM((SB,), jnp.int32), pltpu.SMEM((SB,), jnp.int32), pltpu.SemaphoreType.DMA],
        compiler_params=params(4),
        cost_estimate=cost(2),
        name="factor_pack",
    )(window_owner, sn_order, win_pattern, w_own)
    l_other = swap(l_own, 1)
    l_chip, *sent = pl.pallas_call(
        start_pack_kernel,
        out_shape=(shape_of((PAIR, SN)),) + (shape_of((tall, columns)),) * 4,
        in_specs=[VMEM] * 3,
        out_specs=(VMEM,) * 5,
        compiler_params=params(4),
        cost_estimate=cost(1),
        name="start_pack",
    )(l_own, l_other, rhs_win)
    near = neighbour(l_chip)
    pieces = [sent[0]] + [deep(sent[s], s) for s in (1, 2, 3)]
    w_late, _ = lax.optimization_barrier((win_rows, l_chip))
    w_other = swap(w_late, 1)
    w_other, *pieces = lax.optimization_barrier((w_other, *pieces))
    others = [swap(x, 1) for x in pieces]
    chip_rhs, packed, part = pl.pallas_call(
        first_pack_kernel,
        out_shape=(shape_of((PAIR, columns)), shape_of((SN, columns)), shape_of((half, columns))),
        in_specs=[SMEM, SMEM] + [VMEM] * 8,
        out_specs=(VMEM,) * 3,
        scratch_shapes=[pltpu.SMEM((1,), jnp.int32)],
        compiler_params=params(4),
        cost_estimate=cost(1),
        name="first_pack",
    )(window_owner, sn_order, *pieces, *others)
    near, _ = lax.optimization_barrier((near, packed))
    near_half = pl.pallas_call(
        take_half_kernel,
        out_shape=shape_of((SN, SN)),
        in_specs=[VMEM],
        out_specs=VMEM,
        compiler_params=params(4),
        cost_estimate=cost(1),
        name="take_half",
    )(near)
    far = forward(near_half)
    owner_later, order_later, _ = lax.optimization_barrier((window_owner, sn_order, packed))
    tab, flag = pl.pallas_call(
        table_kernel,
        out_shape=(shape_of((TABLE,), jnp.int32), shape_of((2,), jnp.int32)),
        in_specs=[SMEM, SMEM],
        out_specs=(SMEM, SMEM),
        scratch_shapes=[pltpu.SMEM((4,), jnp.int32)],
        compiler_params=params(4),
        cost_estimate=cost(3),
        name="tables",
    )(owner_later, order_later)
    w_other = in_vmem(w_other)
    w_own = in_vmem(win_rows)
    below = []

    tile = rhs_anc.shape[0]
    sums, solved, masked = None, [], []
    diag_vmem = in_vmem(diag_inv)
    below_rows = anc_rows.shape[0]

    anc_order, anc_pieces = (2, 3, 1), [None] * 4
    for group in range(GROUPS):
        last = group == GROUPS - 1
        a_own = neighbour(packed)
        b_own = swap(part, 6)
        if group == 0:
            below += [mask_below(k, packed) for k in (0, 1)]
            for k in range(GROUPS - 1):
                masked.append(pl.pallas_call(
                    make_mask_kernel(k),
                    out_shape=shape_of((SN, (k + 1) * PAIR)),
                    in_specs=[SMEM, SMEM, VMEM, VMEM, VMEM],
                    out_specs=VMEM,
                    scratch_shapes=[pltpu.VMEM((SB, NWB), jnp.int32)],
                    compiler_params=params(6),
                    cost_estimate=cost(2),
                    name="mask_rows",
                )(tab, order_later, win_pattern, w_own, w_other))
        if group == 0:
            rhs_later, _ = lax.optimization_barrier((rhs_anc, packed))
            anc_pieces = list(pl.pallas_call(
                below_rhs_kernel,
                out_shape=(shape_of((tile, columns)),) * 4,
                in_specs=[HBM],
                out_specs=(VMEM,) * 4,
                scratch_shapes=[pltpu.SemaphoreType.DMA((4,))],
                compiler_params=params(4),
                cost_estimate=cost(1),
                name="below_rhs",
            )(in_hbm(rhs_later)))
        if not last:
            s = anc_order[group]
            moved, _ = lax.optimization_barrier((anc_pieces[s], packed))
            anc_pieces[s] = deep(moved, s)

        if group == 0:
            a_own, b_own, near, far, below[0], below[1], *masked = lax.optimization_barrier(
                (a_own, b_own, near, far, below[0], below[1], *masked))
            l_parts = [in_vmem(x) for x in (l_own, l_other, near, swap(near, 1), far, swap(far, 1))]
        operands = [tab, sn_order, diag_vmem, *l_parts]
        out_shape = [shape_of((PAIR, PAIR))]
        if not last:
            operands += [masked[group], chip_rhs, *solved]
            out_shape += [shape_of((SN, columns), F32)]
        ready = pl.pallas_call(
            make_prep_kernel(group),
            out_shape=tuple(out_shape),
            in_specs=[SMEM, SMEM] + [VMEM] * (len(operands) - 2),
            out_specs=(VMEM,) * len(out_shape),
            scratch_shapes=[pltpu.VMEM((SN, SN), BF16)],
            compiler_params=params(6),
            cost_estimate=cost(2),
            name="prep",
        )(*operands)
        hold = []
        if group == 1:
            below += [mask_below(k, packed) for k in (2, 3)]
            hold = below[2:]
        elif group > 1:
            more, kernel = (solved[:2], two_rows_kernel) if group == 2 else ([solved[2], sums, *anc_pieces], base_rows_kernel)
            sums = pl.pallas_call(
                kernel,
                out_shape=shape_of((below_rows, columns), F32),
                in_specs=[SMEM] + [VMEM] * (4 + len(more)),
                out_specs=VMEM,
                scratch_shapes=[pltpu.VMEM((below_rows, columns), BF16)] if last else [],
                input_output_aliases={6: 0} if last else {},
                compiler_params=params(6),
                cost_estimate=cost(3),
                name="rows_below",
            )(sn_order, *below, *more)
            hold = [sums]
        if group > 0:
            s = anc_order[group - 1]
            a_own, b_own, anc_pieces[s], *rest = lax.optimization_barrier((a_own, b_own, anc_pieces[s], *hold, *ready))
            hold, ready = rest[:len(hold)], rest[len(hold):]
            if group == 1:
                below[2:] = hold
            else:
                sums = hold[0]
        a_swap = swap(a_own, 1)
        b_swap = swap(b_own, 1)
        ready = list(ready) if last else list(ready) + [masked[group]]

        out_shape = [shape_of((PAIR, columns))]
        if not last:
            out_shape += [shape_of((SN, columns)), shape_of((half, columns))]
        results = pl.pallas_call(
            make_solve_kernel(group),
            out_shape=tuple(out_shape),
            in_specs=[SMEM] + [VMEM] * (5 + len(ready)),
            out_specs=(VMEM,) * len(out_shape),
            scratch_shapes=[pltpu.VMEM((PAIR, columns), BF16)],
            compiler_params=params(8),
            cost_estimate=cost(3),
            name="pair_solve",
        )(tab, packed, a_own, a_swap, b_own, b_swap, *ready)
        solved.append(results[0])
        if not last:
            packed, part = results[1:]

    outputs = pl.pallas_call(
        last_rows_kernel,
        out_shape=(shape_of((NW, columns)), shape_of((below_rows, columns))),
        in_specs=[SMEM] + [VMEM] * 9,
        out_specs=(HBM, HBM),
        scratch_shapes=[pltpu.VMEM((below_rows, columns), BF16), pltpu.SemaphoreType.DMA((2 * GROUPS,)),
                        pltpu.SemaphoreType.DMA((4,))],
        compiler_params=params(6),
        cost_estimate=cost(3),
        name="last_rows",
    )(sn_order, *below, *solved, sums)

    def again(carry):
        carry, own_pieces, below_pieces = lax.optimization_barrier((carry, pieces, anc_pieces))
        back = carry[0][1] ^ jnp.arange(4)
        win_rhs = jnp.take(jnp.stack(own_pieces), back, axis=0).reshape(4 * tall, columns)
        anc_rhs = jnp.take(jnp.stack(below_pieces), back, axis=0).reshape(4 * tile, columns)
        return jnp.zeros_like(carry[0]), *general_path(
            win_rows, anc_rows, win_pattern, anc_pattern, window_owner, sn_order, diag_inv, win_rhs, anc_rhs)

    return tuple(lax.while_loop(lambda carry: carry[0][0] != 0, again, (flag, *outputs))[1:])


def solution(mesh):
    return jax.shard_map(
        local,
        mesh=mesh,
        in_specs=(P("rows", None), P("rows", None), P(), P("rows", None), P(), P(), P(),
                  P(("rows", "rhs"), None), P(("rows", "rhs"), None)),
        out_specs=(P(None, "rhs"), P("rows", "rhs")),
        check_vma=False,
    )
```

```python
import jax
import jax.numpy as jnp
from jax import lax
from jax.experimental import pallas as pl
from jax.experimental.pallas import tpu as pltpu
from jax.sharding import PartitionSpec as P

BS = 64
SB = 8
NSUP = 8
SN = 512
NW = 4096
NWB = 64
GROUPS = 4
PAIR = 2 * SN
F32 = jnp.float32
BF16 = jnp.bfloat16


def masked_columns(factor, pattern, node_label):
    blocks = pattern.shape[0]
    columns = lax.dynamic_slice_in_dim(factor, node_label * SN, SN, 1)
    chosen = lax.dynamic_slice_in_dim(pattern, node_label * SB, SB, 1)
    shaped = columns.reshape(blocks, BS, SB, BS) * chosen[:, None, :, None].astype(BF16)
    return shaped.reshape(blocks * BS, SN)


def sum_over_rows(values):
    count = lax.axis_size("rows")
    if count & (count - 1):
        return lax.psum(values, "rows")
    step = 1
    while step < count:
        values = values + lax.ppermute(values, "rows", [(i, i ^ step) for i in range(count)])
        step *= 2
    return values


def general_path(win_rows, anc_rows, win_pattern, anc_pattern, window_owner, sn_order, diag_inv, win_rhs, anc_rhs):
    columns_rhs = win_rhs.shape[1]
    slot_count = win_rows.shape[0] // BS
    first_slot = lax.axis_index("rows") * slot_count
    local_pattern = lax.dynamic_slice_in_dim(win_pattern, first_slot, slot_count, 0)

    def step(position, carry):
        solution, win_resid, anc_resid = carry
        node_label = sn_order[position]
        owners = lax.dynamic_slice_in_dim(window_owner, node_label * SB, SB, 0)
        inverse = lax.dynamic_index_in_dim(diag_inv, node_label, 0, keepdims=False)
        local_place = owners - first_slot
        present = (local_place >= 0) & (local_place < slot_count)
        resid_blocks = win_resid.reshape(slot_count, BS, columns_rhs)
        taken = jnp.take(resid_blocks, jnp.clip(local_place, 0, slot_count - 1), axis=0)
        placed = jnp.where(present[:, None, None], taken, 0.0).reshape(SN, columns_rhs)
        panel = sum_over_rows(placed.astype(BF16))
        solved = jnp.dot(inverse, panel, preferred_element_type=F32).astype(BF16)
        solution = lax.dynamic_update_slice_in_dim(solution, solved, node_label * SN, 0)
        win_part = jnp.dot(masked_columns(win_rows, local_pattern, node_label), solved, preferred_element_type=F32)
        anc_part = jnp.dot(masked_columns(anc_rows, anc_pattern, node_label), solved, preferred_element_type=F32)
        return solution, win_resid - win_part, anc_resid - anc_part

    first = (jnp.zeros((NW, columns_rhs), BF16), win_rhs.astype(F32), anc_rhs.astype(F32))
    solution, _, anc_resid = lax.fori_loop(0, NSUP, step, first)
    return solution, anc_resid.astype(BF16)


def spread_matrix():
    block_index = lax.broadcasted_iota(jnp.int32, (NWB, SN), 0)
    lane_index = lax.broadcasted_iota(jnp.int32, (NWB, SN), 1)
    return (block_index % SB == lane_index // BS).astype(F32).astype(BF16)


def expand_mask(rows_pattern, label, spread):
    lane = lax.broadcasted_iota(jnp.int32, rows_pattern.shape, 1)
    chosen = jnp.where(lane // SB == label, rows_pattern, 0).astype(F32).astype(BF16)
    return jnp.dot(chosen, spread, preferred_element_type=F32).astype(BF16)


def masked_rows(block_of, mask, count):
    return jnp.concatenate([block_of(j) * mask[j:j + 1, :] for j in range(count)], axis=0)


def rows_at(index):
    return pl.ds(pl.multiple_of(index * BS, BS), BS)


def columns_at(label):
    return pl.ds(pl.multiple_of(label * SN, SN), SN)


SRC, LSRC, PACK, TABLE = 0, 64, 96, 128


def factor_kernel(owner, order, pattern, win_ref, out, buf, pat, inv, pos, sem):
    row = lax.axis_index("rows")

    def note_slot(w, carry):
        slot = owner[w]

        @pl.when(slot // SB == row)
        def _():
            inv[slot % SB] = w

        return carry

    lax.fori_loop(0, NWB, note_slot, 0, unroll=8)
    for k in range(NSUP):
        pos[order[k]] = k
    labels = jnp.zeros((SB, 1), jnp.int32)
    for t in range(SB):
        label = order[(pos[inv[t] // SB] // 2) * 2]
        pltpu.make_async_copy(win_ref.at[pl.ds(t * BS, BS), columns_at(label)], buf.at[pl.ds(t * BS, BS), :], sem).start()
        labels = jnp.where(lax.broadcasted_iota(jnp.int32, (SB, 1), 0) == t, label, labels)
    pat[...] = pattern[pl.ds(pl.multiple_of(row * SB, SB), SB), :]
    mask = expand_mask(pat[...], labels, spread_matrix())
    pltpu.make_async_copy(win_ref.at[:, pl.ds(0, SN)], buf, sem).wait()
    for j in range(SB):
        out[j * BS:(j + 1) * BS, :] = buf[j * BS:(j + 1) * BS, :] * mask[j:j + 1, :]


def rhs_pack_kernel(rhs_ref, *sent):
    depth = lax.axis_index("rhs")
    width = sent[0].shape[1]
    for s, out in enumerate(sent):
        at = pl.multiple_of(jnp.bitwise_xor(depth, s) * width, width)
        out[...] = rhs_ref[:, pl.ds(at, width)]


def chip_pack_kernel(own_ref, other_ref, l_chip):
    l_chip[0:SN, :] = own_ref[...]
    l_chip[SN:PAIR, :] = other_ref[...]


def take_half_kernel(x_ref, out):
    out[...] = x_ref[0:SN, :]


def table_kernel(owner, order, tab, flag, cnt):
    row = lax.axis_index("rows")
    chip, core = row // 2, row % 2
    flag[0] = 0
    flag[1] = lax.axis_index("rhs")
    for t in range(GROUPS * SB):
        tab[PACK + t] = 0
    for group in range(GROUPS):
        for t in range(4):
            cnt[t] = 0

        def one(i, carry, group=group):
            slot = owner[order[2 * group + i // SB] * SB + i % SB]
            where, device = slot // (2 * SB), slot // SB
            rank = cnt[where]
            cnt[where] = rank + 1
            flag[0] = jnp.where(rank >= SB, 1, flag[0])
            rank = jnp.minimum(rank, SB - 1)
            rel = jnp.bitwise_xor(where, chip)
            diagonal = rel == 3
            source = jnp.where(rel == 0, 0, jnp.where(diagonal, jnp.where(rank // 4 == core, 3, 4),
                                                      jnp.where(rel == 1 + core, 1, 2)))
            start = jnp.where(source == 4, 7 * SB // 2, source * SB)
            tab[SRC + group * 16 + i] = start + jnp.where(diagonal, rank % 4, rank)

            @pl.when(rel == 0)
            def _():
                tab[PACK + group * SB + rank] = jnp.bitwise_xor(device % 2, core) * SB + slot % SB

            @pl.when(i >= SB)
            def _():
                kind = jnp.where(rel == 0, 0, jnp.where(diagonal, 3, jnp.where(rel == 1 + core, 1, 2)))
                tab[LSRC + group * SB + i - SB] = (2 * kind + jnp.where(device % 2 == core, 0, 1)) * SB + slot % SB

            return carry

        lax.fori_loop(0, 2 * SB, one, 0, unroll=True)


def below_rhs_kernel(rhs_ref, *refs):
    outs, sems = refs[:-1], refs[-1]
    depth = lax.axis_index("rhs")
    width = outs[0].shape[1]
    copies = []
    for s, out in enumerate(outs):
        at = pl.multiple_of(jnp.bitwise_xor(depth, s) * width, width)
        copies.append(pltpu.make_async_copy(rhs_ref.at[:, pl.ds(at, width)], out, sems.at[s]))
        copies[-1].start()
    for c in copies:
        c.wait()


def first_pack_kernel(owner, order, *refs):
    pieces, (chip_rhs, p_ref, b_ref, count) = refs[:8], refs[8:]
    row, depth = lax.axis_index("rows"), lax.axis_index("rhs")
    core = row % 2
    tall = pieces[0].shape[0]
    for side in range(2):
        for s in range(4):
            at = pl.multiple_of(side * SB * BS + jnp.bitwise_xor(depth, s) * tall, tall)
            chip_rhs[pl.ds(at, tall), :] = pieces[4 * side + s][...]
    count[0] = 0
    for i in range(2 * SB):
        slot = owner[order[i // SB] * SB + i % SB]

        @pl.when(slot // (2 * SB) == row // 2)
        def _(slot=slot):
            rank = count[0]
            count[0] = rank + 1
            place = jnp.bitwise_xor((slot // SB) % 2, core) * SB + slot % SB

            @pl.when(rank < SB)
            def _():
                p_ref[rows_at(rank), :] = chip_rhs[rows_at(place), :]

    b_ref[...] = p_ref[pl.ds(pl.multiple_of(core * SB // 2 * BS, SB // 2 * BS), SB // 2 * BS), :]


def make_mask_kernel(group):
    def kernel(tab, order, pattern, w_own, w_other, out, pat):
        row = lax.axis_index("rows")
        places = [tab[PACK + (group + 1) * SB + j] for j in range(SB)]
        for j, place in enumerate(places):
            pat[j:j + 1, :] = pattern[pl.ds(jnp.bitwise_xor(row, place // SB) * SB + place % SB, 1), :]
        spread = spread_matrix()
        rows = pat[...]
        masks = [expand_mask(rows, order[k], spread) for k in range(2 * group + 2)]
        for j, place in enumerate(places):
            at = slice(j * BS, (j + 1) * BS)
            for side, w_ref in enumerate((w_own, w_other)):
                @pl.when(place // SB == side)
                def _(w_ref=w_ref, at=at, j=j, place=place):
                    for k in range(2 * group + 2):
                        block = w_ref[rows_at(place % SB), columns_at(order[k])]
                        out[at, k * SN:(k + 1) * SN] = block * masks[k][j:j + 1, :]

    return kernel


def make_prep_kernel(group):
    last = group == GROUPS - 1

    def kernel(tab, order, diag, *refs):
        own, other, near, near_swap, far, far_swap = refs[:6]
        l_refs = ((own, 0), (other, 0), (near, 0), (near, SB), (near_swap, SB), (near_swap, 0), (far, 0), (far_swap, 0))
        refs = refs[6:]
        if last:
            m_out, lbuf = refs
        else:
            w_ref, chip_rhs = refs[:2]
            xs = refs[2:2 + group]
            m_out, r_out, lbuf = refs[2 + group:]
        for i in range(SB):
            code = tab[LSRC + group * SB + i]
            for m in range(8):
                @pl.when(code // SB == m)
                def _(m=m, i=i, code=code):
                    lbuf[i * BS:(i + 1) * BS, :] = l_refs[m][0][rows_at(code % SB + l_refs[m][1]), :]
        first, second = diag[order[2 * group]], diag[order[2 * group + 1]]
        m_out[0:SN, 0:SN] = first
        m_out[SN:PAIR, SN:PAIR] = second
        joined = jnp.dot(second, lbuf[...], preferred_element_type=F32).astype(BF16)
        m_out[SN:PAIR, 0:SN] = (-jnp.dot(joined, first, preferred_element_type=F32)).astype(BF16)
        if not last:
            total = jnp.concatenate([chip_rhs[rows_at(tab[PACK + (group + 1) * SB + j]), :] for j in range(SB)], axis=0).astype(F32)
            for k in range(group):
                total = total - jnp.dot(w_ref[:, k * PAIR:(k + 1) * PAIR], xs[k][...], preferred_element_type=F32)
            r_out[...] = total

    return kernel


def make_solve_kernel(group):
    last = group == GROUPS - 1

    def kernel(*refs):
        tab, sources, m_ref = refs[0], refs[1:6], refs[6]
        if last:
            x_ref, panel, pool = refs[7:]
        else:
            r_ref, wn_ref, x_ref, p_ref, b_ref, panel, pool = refs[7:]
        at = 0
        for source in sources:
            pool[at:at + source.shape[0], :] = source[...]
            at += source.shape[0]
        for i in range(2 * SB):
            panel[i * BS:(i + 1) * BS, :] = pool[rows_at(tab[SRC + group * 16 + i]), :]
        x_ref[0:SN, :] = jnp.dot(m_ref[0:SN, 0:SN], panel[0:SN, :], preferred_element_type=F32).astype(BF16)
        x_ref[SN:PAIR, :] = jnp.dot(m_ref[SN:PAIR, :], panel[...], preferred_element_type=F32).astype(BF16)
        if last:
            return
        total = r_ref[...] - jnp.dot(wn_ref[:, group * PAIR:(group + 1) * PAIR], x_ref[...], preferred_element_type=F32)
        p_ref[...] = total.astype(BF16)
        core = lax.axis_index("rows") % 2
        b_ref[...] = p_ref[pl.ds(pl.multiple_of(core * SB // 2 * BS, SB // 2 * BS), SB // 2 * BS), :]

    return kernel


def make_below_mask_kernel(tile):
    def kernel(pattern, a_ref, out, sems):
        copies = []
        for j in range(SB):
            c = pltpu.make_async_copy(a_ref.at[pl.ds((tile * SB + j) * BS, BS), :], out.at[pl.ds(j * BS, BS), :], sems.at[j])
            c.start()
            copies.append(c)
        spread = spread_matrix()
        rows = pattern[tile * SB:(tile + 1) * SB, :]
        masks = [expand_mask(rows, k, spread) for k in range(NSUP)]
        for j in range(SB):
            copies[j].wait()
            for k in range(NSUP):
                at = (slice(j * BS, (j + 1) * BS), slice(k * SN, (k + 1) * SN))
                out[at] = out[at] * masks[k][j:j + 1, :]

    return kernel


def below_product(order, a_ref, x_ref, group):
    first = jnp.dot(a_ref[:, columns_at(order[2 * group])], x_ref[0:SN, :], preferred_element_type=F32)
    return first + jnp.dot(a_ref[:, columns_at(order[2 * group + 1])], x_ref[SN:PAIR, :], preferred_element_type=F32)


def two_rows_kernel(order, a0, a1, a2, a3, x0_ref, x1_ref, out):
    for i, a_ref in enumerate((a0, a1, a2, a3)):
        out[i * SN:(i + 1) * SN, :] = below_product(order, a_ref, x0_ref, 0) + below_product(order, a_ref, x1_ref, 1)


def base_rows_kernel(order, a0, a1, a2, a3, x_ref, sums, h0, h1, h2, h3, out, rhs):
    depth = lax.axis_index("rhs")
    tall = h0.shape[0]
    for s, h in enumerate((h0, h1, h2, h3)):
        rhs[pl.ds(pl.multiple_of(jnp.bitwise_xor(depth, s) * tall, tall), tall), :] = h[...]
    for i, a_ref in enumerate((a0, a1, a2, a3)):
        at = slice(i * SN, (i + 1) * SN)
        out[at, :] = rhs[at, :].astype(F32) - (sums[at, :] + below_product(order, a_ref, x_ref, 2))


def last_rows_kernel(order, a0, a1, a2, a3, x0, x1, x2, x3, base, sol_ref, out_ref, done, sems, osem):
    copies = []
    for k, x in enumerate((x0, x1, x2, x3)):
        for q in range(2):
            at = pl.multiple_of(order[2 * k + q] * SN, SN)
            copies.append(pltpu.make_async_copy(x.at[pl.ds(q * SN, SN), :], sol_ref.at[pl.ds(at, SN), :], sems.at[2 * k + q]))
            copies[-1].start()
    for i, a_ref in enumerate((a0, a1, a2, a3)):
        at = slice(i * SN, (i + 1) * SN)
        done[at, :] = (base[at, :] - below_product(order, a_ref, x3, GROUPS - 1)).astype(BF16)
        copies.append(pltpu.make_async_copy(done.at[pl.ds(i * SN, SN), :], out_ref.at[pl.ds(i * SN, SN), :], osem.at[i]))
        copies[-1].start()
    for c in copies:
        c.wait()


def in_vmem(x):
    return pltpu.with_memory_space_constraint(x, pltpu.VMEM)


def in_hbm(x):
    return pltpu.with_memory_space_constraint(x, pltpu.HBM)


SMEM = pl.BlockSpec(memory_space=pltpu.SMEM)
VMEM = pl.BlockSpec(memory_space=pltpu.VMEM)
HBM = pl.BlockSpec(memory_space=pltpu.HBM)


def params(mib):
    return pltpu.CompilerParams(vmem_limit_bytes=mib * 1024 * 1024)


def cost(micros):
    return pl.CostEstimate(flops=micros * 10 ** 8, bytes_accessed=micros * 3 * 10 ** 6, transcendentals=0)


def shape_of(dims, dtype=BF16):
    return jax.ShapeDtypeStruct(dims, dtype)


def local(win_rows, anc_rows, win_pattern, anc_pattern, window_owner, sn_order, diag_inv, rhs_win, rhs_anc):
    if lax.axis_size("rows") != 8 or lax.axis_size("rhs") != 4 or anc_rows.shape[0] != 4 * SB * BS:
        win_rhs = lax.all_to_all(rhs_win, "rhs", split_axis=1, concat_axis=0, tiled=True)
        anc_rhs = lax.all_to_all(rhs_anc, "rhs", split_axis=1, concat_axis=0, tiled=True)
        return general_path(win_rows, anc_rows, win_pattern, anc_pattern, window_owner, sn_order, diag_inv, win_rhs, anc_rhs)

    def swap(x, m):
        return lax.ppermute(x, "rows", [(i, i ^ m) for i in range(8)])

    def deep(x, m):
        return lax.ppermute(x, "rhs", [(i, i ^ m) for i in range(4)])

    def neighbour(x):
        return lax.ppermute(x, "rows", [(i, i ^ (2 if i % 2 == 0 else 4)) for i in range(8)])

    def forward(x):
        return lax.ppermute(x, "rows", [(i, i ^ (4 if i % 2 == 0 else 2)) for i in range(8)])

    def mask_below(k, after):
        pattern_later, _ = lax.optimization_barrier((anc_pattern, after))
        return pl.pallas_call(
            make_below_mask_kernel(k),
            out_shape=shape_of((SN, NW)),
            in_specs=[VMEM, HBM],
            out_specs=VMEM,
            scratch_shapes=[pltpu.SemaphoreType.DMA((SB,))],
            compiler_params=params(4),
            cost_estimate=cost(2),
            name="mask_below",
        )(pattern_later, in_hbm(anc_rows))

    columns = rhs_win.shape[1] // 4
    half = SN // 2
    tall = rhs_win.shape[0]
    w_own = in_hbm(win_rows)
    l_own = pl.pallas_call(
        factor_kernel,
        out_shape=shape_of((SN, SN)),
        in_specs=[SMEM, SMEM, VMEM, HBM],
        out_specs=VMEM,
        scratch_shapes=[pltpu.VMEM((SN, SN), BF16), pltpu.VMEM((SB, NWB), jnp.int32),
                        pltpu.SMEM((SB,), jnp.int32), pltpu.SMEM((SB,), jnp.int32), pltpu.SemaphoreType.DMA],
        compiler_params=params(4),
        cost_estimate=cost(2),
        name="factor_pack",
    )(window_owner, sn_order, win_pattern, w_own)
    sent = pl.pallas_call(
        rhs_pack_kernel,
        out_shape=(shape_of((tall, columns)),) * 4,
        in_specs=[VMEM],
        out_specs=(VMEM,) * 4,
        compiler_params=params(4),
        cost_estimate=cost(1),
        name="rhs_pack",
    )(rhs_win)
    pieces = [sent[0]] + [deep(sent[s], s) for s in (1, 2, 3)]
    l_late, pieces[1] = lax.optimization_barrier((l_own, pieces[1]))
    l_other = swap(l_late, 1)
    l_chip = pl.pallas_call(
        chip_pack_kernel,
        out_shape=shape_of((PAIR, SN)),
        in_specs=[VMEM] * 2,
        out_specs=VMEM,
        compiler_params=params(4),
        cost_estimate=cost(1),
        name="chip_pack",
    )(l_own, l_other)
    near = neighbour(l_chip)
    w_late, _ = lax.optimization_barrier((win_rows, l_chip))
    w_other = swap(w_late, 1)
    below = [mask_below(k, l_chip) for k in (0, 1)]
    w_other, below[0], below[1], *pieces = lax.optimization_barrier((w_other, *below, *pieces))
    others = [swap(x, 1) for x in pieces]
    chip_rhs, packed, part = pl.pallas_call(
        first_pack_kernel,
        out_shape=(shape_of((PAIR, columns)), shape_of((SN, columns)), shape_of((half, columns))),
        in_specs=[SMEM, SMEM] + [VMEM] * 8,
        out_specs=(VMEM,) * 3,
        scratch_shapes=[pltpu.SMEM((1,), jnp.int32)],
        compiler_params=params(4),
        cost_estimate=cost(1),
        name="first_pack",
    )(window_owner, sn_order, *pieces, *others)
    near, _ = lax.optimization_barrier((near, packed))
    near_half = pl.pallas_call(
        take_half_kernel,
        out_shape=shape_of((SN, SN)),
        in_specs=[VMEM],
        out_specs=VMEM,
        compiler_params=params(4),
        cost_estimate=cost(1),
        name="take_half",
    )(near)
    far = forward(near_half)
    owner_later, order_later, _ = lax.optimization_barrier((window_owner, sn_order, packed))
    tab, flag = pl.pallas_call(
        table_kernel,
        out_shape=(shape_of((TABLE,), jnp.int32), shape_of((2,), jnp.int32)),
        in_specs=[SMEM, SMEM],
        out_specs=(SMEM, SMEM),
        scratch_shapes=[pltpu.SMEM((4,), jnp.int32)],
        compiler_params=params(4),
        cost_estimate=cost(3),
        name="tables",
    )(owner_later, order_later)
    w_other = in_vmem(w_other)
    w_own = in_vmem(win_rows)

    tile = rhs_anc.shape[0]
    sums, solved, masked = None, [], []
    diag_vmem = in_vmem(diag_inv)
    below_rows = anc_rows.shape[0]

    anc_order, anc_pieces = (1, 2, 3), [None] * 4
    for group in range(GROUPS):
        last = group == GROUPS - 1
        a_own = neighbour(packed)
        b_own = swap(part, 6)
        if group == 0:
            for k in range(GROUPS - 1):
                masked.append(pl.pallas_call(
                    make_mask_kernel(k),
                    out_shape=shape_of((SN, (k + 1) * PAIR)),
                    in_specs=[SMEM, SMEM, VMEM, VMEM, VMEM],
                    out_specs=VMEM,
                    scratch_shapes=[pltpu.VMEM((SB, NWB), jnp.int32)],
                    compiler_params=params(6),
                    cost_estimate=cost(2),
                    name="mask_rows",
                )(tab, order_later, win_pattern, w_own, w_other))
        if group == 0:
            rhs_later, _ = lax.optimization_barrier((rhs_anc, packed))
            anc_pieces = list(pl.pallas_call(
                below_rhs_kernel,
                out_shape=(shape_of((tile, columns)),) * 4,
                in_specs=[HBM],
                out_specs=(VMEM,) * 4,
                scratch_shapes=[pltpu.SemaphoreType.DMA((4,))],
                compiler_params=params(4),
                cost_estimate=cost(1),
                name="below_rhs",
            )(in_hbm(rhs_later)))
        if not last:
            s = anc_order[group]
            moved, _ = lax.optimization_barrier((anc_pieces[s], packed))
            anc_pieces[s] = deep(moved, s)

        if group == 0:
            a_own, b_own, near, far, anc_pieces[1], *masked = lax.optimization_barrier(
                (a_own, b_own, near, far, anc_pieces[1], *masked))
            l_parts = [in_vmem(x) for x in (l_own, l_other, near, swap(near, 1), far, swap(far, 1))]
        operands = [tab, sn_order, diag_vmem, *l_parts]
        out_shape = [shape_of((PAIR, PAIR))]
        if not last:
            operands += [masked[group], chip_rhs, *solved]
            out_shape += [shape_of((SN, columns), F32)]
        ready = pl.pallas_call(
            make_prep_kernel(group),
            out_shape=tuple(out_shape),
            in_specs=[SMEM, SMEM] + [VMEM] * (len(operands) - 2),
            out_specs=(VMEM,) * len(out_shape),
            scratch_shapes=[pltpu.VMEM((SN, SN), BF16)],
            compiler_params=params(6),
            cost_estimate=cost(2),
            name="prep",
        )(*operands)
        hold = []
        if group == 1:
            below += [mask_below(k, packed) for k in (2, 3)]
            hold = below[2:]
        elif group > 1:
            more, kernel = (solved[:2], two_rows_kernel) if group == 2 else ([solved[2], sums, *anc_pieces], base_rows_kernel)
            sums = pl.pallas_call(
                kernel,
                out_shape=shape_of((below_rows, columns), F32),
                in_specs=[SMEM] + [VMEM] * (4 + len(more)),
                out_specs=VMEM,
                scratch_shapes=[pltpu.VMEM((below_rows, columns), BF16)] if last else [],
                input_output_aliases={6: 0} if last else {},
                compiler_params=params(6),
                cost_estimate=cost(3),
                name="rows_below",
            )(sn_order, *below, *more)
            hold = [sums]
        if group > 0:
            s = anc_order[group - 1]
            a_own, b_own, anc_pieces[s], *rest = lax.optimization_barrier((a_own, b_own, anc_pieces[s], *hold, *ready))
            hold, ready = rest[:len(hold)], rest[len(hold):]
            if group == 1:
                below[2:] = hold
            else:
                sums = hold[0]
        a_swap = swap(a_own, 1)
        b_swap = swap(b_own, 1)
        ready = list(ready) if last else list(ready) + [masked[group]]

        out_shape = [shape_of((PAIR, columns))]
        if not last:
            out_shape += [shape_of((SN, columns)), shape_of((half, columns))]
        results = pl.pallas_call(
            make_solve_kernel(group),
            out_shape=tuple(out_shape),
            in_specs=[SMEM] + [VMEM] * (5 + len(ready)),
            out_specs=(VMEM,) * len(out_shape),
            scratch_shapes=[pltpu.VMEM((PAIR, columns), BF16), pltpu.VMEM((2 * PAIR, columns), BF16)],
            compiler_params=params(8),
            cost_estimate=cost(3),
            name="pair_solve",
        )(tab, packed, a_own, a_swap, b_own, b_swap, *ready)
        solved.append(results[0])
        if not last:
            packed, part = results[1:]

    outputs = pl.pallas_call(
        last_rows_kernel,
        out_shape=(shape_of((NW, columns)), shape_of((below_rows, columns))),
        in_specs=[SMEM] + [VMEM] * 9,
        out_specs=(HBM, HBM),
        scratch_shapes=[pltpu.VMEM((below_rows, columns), BF16), pltpu.SemaphoreType.DMA((2 * GROUPS,)),
                        pltpu.SemaphoreType.DMA((4,))],
        compiler_params=params(6),
        cost_estimate=cost(3),
        name="last_rows",
    )(sn_order, *below, *solved, sums)

    def again(carry):
        carry, own_pieces, below_pieces = lax.optimization_barrier((carry, pieces, anc_pieces))
        back = carry[0][1] ^ jnp.arange(4)
        win_rhs = jnp.take(jnp.stack(own_pieces), back, axis=0).reshape(4 * tall, columns)
        anc_rhs = jnp.take(jnp.stack(below_pieces), back, axis=0).reshape(4 * tile, columns)
        return jnp.zeros_like(carry[0]), *general_path(
            win_rows, anc_rows, win_pattern, anc_pattern, window_owner, sn_order, diag_inv, win_rhs, anc_rhs)

    return tuple(lax.while_loop(lambda carry: carry[0][0] != 0, again, (flag, *outputs))[1:])


def solution(mesh):
    return jax.shard_map(
        local,
        mesh=mesh,
        in_specs=(P("rows", None), P("rows", None), P(), P("rows", None), P(), P(), P(),
                  P(("rows", "rhs"), None), P(("rows", "rhs"), None)),
        out_specs=(P(None, "rhs"), P("rows", "rhs")),
        check_vma=False,
    )
```

```python
import jax
import jax.numpy as jnp
from jax import lax
from jax.experimental import pallas as pl
from jax.experimental.pallas import tpu as pltpu
from jax.sharding import PartitionSpec as P

BS = 64
SB = 8
NSUP = 8
SN = 512
NW = 4096
NWB = 64
GROUPS = 4
PAIR = 2 * SN
F32 = jnp.float32
BF16 = jnp.bfloat16


def masked_columns(factor, pattern, node_label):
    blocks = pattern.shape[0]
    columns = lax.dynamic_slice_in_dim(factor, node_label * SN, SN, 1)
    chosen = lax.dynamic_slice_in_dim(pattern, node_label * SB, SB, 1)
    shaped = columns.reshape(blocks, BS, SB, BS) * chosen[:, None, :, None].astype(BF16)
    return shaped.reshape(blocks * BS, SN)


def sum_over_rows(values):
    count = lax.axis_size("rows")
    if count & (count - 1):
        return lax.psum(values, "rows")
    step = 1
    while step < count:
        values = values + lax.ppermute(values, "rows", [(i, i ^ step) for i in range(count)])
        step *= 2
    return values


def general_path(win_rows, anc_rows, win_pattern, anc_pattern, window_owner, sn_order, diag_inv, win_rhs, anc_rhs):
    columns_rhs = win_rhs.shape[1]
    slot_count = win_rows.shape[0] // BS
    first_slot = lax.axis_index("rows") * slot_count
    local_pattern = lax.dynamic_slice_in_dim(win_pattern, first_slot, slot_count, 0)

    def step(position, carry):
        solution, win_resid, anc_resid = carry
        node_label = sn_order[position]
        owners = lax.dynamic_slice_in_dim(window_owner, node_label * SB, SB, 0)
        inverse = lax.dynamic_index_in_dim(diag_inv, node_label, 0, keepdims=False)
        local_place = owners - first_slot
        present = (local_place >= 0) & (local_place < slot_count)
        resid_blocks = win_resid.reshape(slot_count, BS, columns_rhs)
        taken = jnp.take(resid_blocks, jnp.clip(local_place, 0, slot_count - 1), axis=0)
        placed = jnp.where(present[:, None, None], taken, 0.0).reshape(SN, columns_rhs)
        panel = sum_over_rows(placed.astype(BF16))
        solved = jnp.dot(inverse, panel, preferred_element_type=F32).astype(BF16)
        solution = lax.dynamic_update_slice_in_dim(solution, solved, node_label * SN, 0)
        win_part = jnp.dot(masked_columns(win_rows, local_pattern, node_label), solved, preferred_element_type=F32)
        anc_part = jnp.dot(masked_columns(anc_rows, anc_pattern, node_label), solved, preferred_element_type=F32)
        return solution, win_resid - win_part, anc_resid - anc_part

    first = (jnp.zeros((NW, columns_rhs), BF16), win_rhs.astype(F32), anc_rhs.astype(F32))
    solution, _, anc_resid = lax.fori_loop(0, NSUP, step, first)
    return solution, anc_resid.astype(BF16)


def spread_matrix():
    block_index = lax.broadcasted_iota(jnp.int32, (NWB, SN), 0)
    lane_index = lax.broadcasted_iota(jnp.int32, (NWB, SN), 1)
    return (block_index % SB == lane_index // BS).astype(F32).astype(BF16)


def expand_mask(rows_pattern, label, spread):
    lane = lax.broadcasted_iota(jnp.int32, rows_pattern.shape, 1)
    chosen = jnp.where(lane // SB == label, rows_pattern, 0).astype(F32).astype(BF16)
    return jnp.dot(chosen, spread, preferred_element_type=F32).astype(BF16)


def masked_rows(block_of, mask, count):
    return jnp.concatenate([block_of(j) * mask[j:j + 1, :] for j in range(count)], axis=0)


def rows_at(index):
    return pl.ds(pl.multiple_of(index * BS, BS), BS)


def columns_at(label):
    return pl.ds(pl.multiple_of(label * SN, SN), SN)


SRC, LSRC, PACK, TABLE = 0, 64, 96, 128


def factor_kernel(owner, order, pattern, win_ref, out, buf, pat, inv, pos, sem):
    row = lax.axis_index("rows")

    for w in range(NWB):
        slot = owner[w]
        inv[jnp.where(slot // SB == row, slot % SB, SB)] = w
    for k in range(NSUP):
        pos[order[k]] = k
    labels = jnp.zeros((SB, 1), jnp.int32)
    for t in range(SB):
        label = order[(pos[inv[t] // SB] // 2) * 2]
        pltpu.make_async_copy(win_ref.at[pl.ds(t * BS, BS), columns_at(label)], buf.at[pl.ds(t * BS, BS), :], sem).start()
        labels = jnp.where(lax.broadcasted_iota(jnp.int32, (SB, 1), 0) == t, label, labels)
    pat[...] = pattern[pl.ds(pl.multiple_of(row * SB, SB), SB), :]
    mask = expand_mask(pat[...], labels, spread_matrix())
    pltpu.make_async_copy(win_ref.at[:, pl.ds(0, SN)], buf, sem).wait()
    for j in range(SB):
        out[j * BS:(j + 1) * BS, :] = buf[j * BS:(j + 1) * BS, :] * mask[j:j + 1, :]


def rhs_pack_kernel(rhs_ref, *sent):
    depth = lax.axis_index("rhs")
    width = sent[0].shape[1]
    for s, out in enumerate(sent):
        at = pl.multiple_of(jnp.bitwise_xor(depth, s) * width, width)
        out[...] = rhs_ref[:, pl.ds(at, width)]


def chip_pack_kernel(own_ref, other_ref, l_chip):
    l_chip[0:SN, :] = own_ref[...]
    l_chip[SN:PAIR, :] = other_ref[...]


def take_half_kernel(x_ref, out):
    out[...] = x_ref[0:SN, :]


def table_kernel(owner, order, tab, flag):
    row = lax.axis_index("rows")
    chip, core = row // 2, row % 2
    bad = 0
    for t in range(GROUPS * SB):
        tab[PACK + t] = 0
    for group in range(GROUPS):
        counts = 0
        for i in range(2 * SB):
            slot = owner[order[2 * group + i // SB] * SB + i % SB]
            where, device = slot // (2 * SB), slot // SB
            rank = (counts >> (8 * where)) & 255
            counts = counts + (1 << (8 * where))
            bad = bad | (rank // SB)
            rank = jnp.minimum(rank, SB - 1)
            rel = jnp.bitwise_xor(where, chip)
            cross = jnp.bitwise_xor(device % 2, core)
            kind = jnp.where((rel == 1) | (rel == 2), jnp.where(rel == 1 + core, 1, 2), rel)
            far_rank = 3 * SB + jnp.where(rank // 4 == core, 0, 4) + rank % 4
            tab[SRC + group * 16 + i] = jnp.where(kind == 3, far_rank, kind * SB + rank)
            tab[jnp.where(rel == 0, PACK + group * SB + rank, TABLE)] = cross * SB + slot % SB
            if i >= SB:
                tab[LSRC + group * SB + i - SB] = (2 * kind + cross) * SB + slot % SB
    flag[0] = bad
    flag[1] = lax.axis_index("rhs")


def below_rhs_kernel(rhs_ref, *outs):
    depth = lax.axis_index("rhs")
    width = outs[0].shape[1]
    for s, out in enumerate(outs):
        out[...] = rhs_ref[:, pl.ds(pl.multiple_of(jnp.bitwise_xor(depth, s) * width, width), width)]


def first_pack_kernel(owner, order, *refs):
    pieces, (chip_rhs, p_ref, b_ref, place) = refs[:8], refs[8:]
    row, depth = lax.axis_index("rows"), lax.axis_index("rhs")
    core = row % 2
    tall = pieces[0].shape[0]
    for side in range(2):
        for s in range(4):
            at = pl.multiple_of(side * SB * BS + jnp.bitwise_xor(depth, s) * tall, tall)
            chip_rhs[pl.ds(at, tall), :] = pieces[4 * side + s][...]
    for t in range(SB):
        place[t] = 0
    rank = 0
    for i in range(2 * SB):
        slot = owner[order[i // SB] * SB + i % SB]
        here = slot // (2 * SB) == row // 2
        place[jnp.where(here & (rank < SB), rank, SB)] = jnp.bitwise_xor((slot // SB) % 2, core) * SB + slot % SB
        rank = rank + jnp.where(here, 1, 0)
    for t in range(SB):
        p_ref[t * BS:(t + 1) * BS, :] = chip_rhs[rows_at(place[t]), :]
    b_ref[...] = p_ref[pl.ds(pl.multiple_of(core * SB // 2 * BS, SB // 2 * BS), SB // 2 * BS), :]


def make_mask_kernel(group):
    def kernel(tab, order, pattern, w_own, w_other, out, pat):
        row = lax.axis_index("rows")
        places = [tab[PACK + (group + 1) * SB + j] for j in range(SB)]
        for j, place in enumerate(places):
            pat[j:j + 1, :] = pattern[pl.ds(jnp.bitwise_xor(row, place // SB) * SB + place % SB, 1), :]
        spread = spread_matrix()
        rows = pat[...]
        masks = [expand_mask(rows, order[k], spread) for k in range(2 * group + 2)]
        for j, place in enumerate(places):
            at = slice(j * BS, (j + 1) * BS)
            for side, w_ref in enumerate((w_own, w_other)):
                @pl.when(place // SB == side)
                def _(w_ref=w_ref, at=at, j=j, place=place):
                    for k in range(2 * group + 2):
                        block = w_ref[rows_at(place % SB), columns_at(order[k])]
                        out[at, k * SN:(k + 1) * SN] = block * masks[k][j:j + 1, :]

    return kernel


def make_prep_kernel(group):
    last = group == GROUPS - 1

    def kernel(tab, order, diag, *refs):
        own, other, near, near_swap, far, far_swap = refs[:6]
        l_refs = ((own, 0), (other, 0), (near, 0), (near, SB), (near_swap, SB), (near_swap, 0), (far, 0), (far_swap, 0))
        refs = refs[6:]
        if last:
            m_out, lbuf = refs
        else:
            w_ref, chip_rhs = refs[:2]
            xs = refs[2:2 + group]
            m_out, r_out, lbuf = refs[2 + group:]
        for i in range(SB):
            code = tab[LSRC + group * SB + i]
            for m in range(8):
                @pl.when(code // SB == m)
                def _(m=m, i=i, code=code):
                    lbuf[i * BS:(i + 1) * BS, :] = l_refs[m][0][rows_at(code % SB + l_refs[m][1]), :]
        first, second = diag[order[2 * group]], diag[order[2 * group + 1]]
        m_out[0:SN, 0:SN] = first
        m_out[SN:PAIR, SN:PAIR] = second
        joined = jnp.dot(second, lbuf[...], preferred_element_type=F32).astype(BF16)
        m_out[SN:PAIR, 0:SN] = (-jnp.dot(joined, first, preferred_element_type=F32)).astype(BF16)
        if not last:
            total = jnp.concatenate([chip_rhs[rows_at(tab[PACK + (group + 1) * SB + j]), :] for j in range(SB)], axis=0).astype(F32)
            for k in range(group):
                total = total - jnp.dot(w_ref[:, k * PAIR:(k + 1) * PAIR], xs[k][...], preferred_element_type=F32)
            r_out[...] = total

    return kernel


def make_solve_kernel(group):
    last = group == GROUPS - 1

    def kernel(*refs):
        tab, sources, m_ref = refs[0], refs[1:6], refs[6]
        if last:
            x_ref, panel, pool = refs[7:]
        else:
            r_ref, wn_ref, x_ref, p_ref, b_ref, panel, pool = refs[7:]
        at = 0
        for source in sources:
            pool[at:at + source.shape[0], :] = source[...]
            at += source.shape[0]
        for i in range(2 * SB):
            panel[i * BS:(i + 1) * BS, :] = pool[rows_at(tab[SRC + group * 16 + i]), :]
        x_ref[0:SN, :] = jnp.dot(m_ref[0:SN, 0:SN], panel[0:SN, :], preferred_element_type=F32).astype(BF16)
        x_ref[SN:PAIR, :] = jnp.dot(m_ref[SN:PAIR, :], panel[...], preferred_element_type=F32).astype(BF16)
        if last:
            return
        total = r_ref[...] - jnp.dot(wn_ref[:, group * PAIR:(group + 1) * PAIR], x_ref[...], preferred_element_type=F32)
        p_ref[...] = total.astype(BF16)
        core = lax.axis_index("rows") % 2
        b_ref[...] = p_ref[pl.ds(pl.multiple_of(core * SB // 2 * BS, SB // 2 * BS), SB // 2 * BS), :]

    return kernel


def make_below_mask_kernel(tile):
    def kernel(pattern, a_ref, out, sems):
        copies = []
        count = 2 * SB
        for j in range(count):
            c = pltpu.make_async_copy(a_ref.at[pl.ds((tile * count + j) * BS, BS), :], out.at[pl.ds(j * BS, BS), :], sems.at[j])
            c.start()
            copies.append(c)
        spread = spread_matrix()
        rows = pattern[tile * count:(tile + 1) * count, :]
        masks = [expand_mask(rows, k, spread) for k in range(NSUP)]
        for j in range(count):
            copies[j].wait()
            for k in range(NSUP):
                at = (slice(j * BS, (j + 1) * BS), slice(k * SN, (k + 1) * SN))
                out[at] = out[at] * masks[k][j:j + 1, :]

    return kernel


def below_product(order, a_ref, x_ref, group, i):
    rows = slice((i % 2) * SN, (i % 2 + 1) * SN)
    first = jnp.dot(a_ref[rows, columns_at(order[2 * group])], x_ref[0:SN, :], preferred_element_type=F32)
    return first + jnp.dot(a_ref[rows, columns_at(order[2 * group + 1])], x_ref[SN:PAIR, :], preferred_element_type=F32)


def two_rows_kernel(order, a0, a1, x0_ref, x1_ref, out):
    for i, a_ref in enumerate((a0, a0, a1, a1)):
        out[i * SN:(i + 1) * SN, :] = below_product(order, a_ref, x0_ref, 0, i) + below_product(order, a_ref, x1_ref, 1, i)


def base_rows_kernel(order, a0, a1, x_ref, sums, h0, h1, h2, h3, out, rhs):
    depth = lax.axis_index("rhs")
    tall = h0.shape[0]
    for s, h in enumerate((h0, h1, h2, h3)):
        rhs[pl.ds(pl.multiple_of(jnp.bitwise_xor(depth, s) * tall, tall), tall), :] = h[...]
    for i, a_ref in enumerate((a0, a0, a1, a1)):
        at = slice(i * SN, (i + 1) * SN)
        out[at, :] = rhs[at, :].astype(F32) - (sums[at, :] + below_product(order, a_ref, x_ref, 2, i))


def last_rows_kernel(order, a0, a1, x0, x1, x2, x3, base, sol_ref, out_ref, done, sems, osem):
    copies = []
    for k, x in enumerate((x0, x1, x2, x3)):
        for q in range(2):
            at = pl.multiple_of(order[2 * k + q] * SN, SN)
            copies.append(pltpu.make_async_copy(x.at[pl.ds(q * SN, SN), :], sol_ref.at[pl.ds(at, SN), :], sems.at[2 * k + q]))
            copies[-1].start()
    for i, a_ref in enumerate((a0, a0, a1, a1)):
        at = slice(i * SN, (i + 1) * SN)
        done[at, :] = (base[at, :] - below_product(order, a_ref, x3, GROUPS - 1, i)).astype(BF16)
        copies.append(pltpu.make_async_copy(done.at[pl.ds(i * SN, SN), :], out_ref.at[pl.ds(i * SN, SN), :], osem.at[i]))
        copies[-1].start()
    for c in copies:
        c.wait()


def in_vmem(x):
    return pltpu.with_memory_space_constraint(x, pltpu.VMEM)


def in_hbm(x):
    return pltpu.with_memory_space_constraint(x, pltpu.HBM)


SMEM = pl.BlockSpec(memory_space=pltpu.SMEM)
VMEM = pl.BlockSpec(memory_space=pltpu.VMEM)
HBM = pl.BlockSpec(memory_space=pltpu.HBM)


def params(mib):
    return pltpu.CompilerParams(vmem_limit_bytes=mib * 1024 * 1024)


def cost(micros):
    return pl.CostEstimate(flops=micros * 10 ** 8, bytes_accessed=micros * 3 * 10 ** 6, transcendentals=0)


def shape_of(dims, dtype=BF16):
    return jax.ShapeDtypeStruct(dims, dtype)


def local(win_rows, anc_rows, win_pattern, anc_pattern, window_owner, sn_order, diag_inv, rhs_win, rhs_anc):
    if lax.axis_size("rows") != 8 or lax.axis_size("rhs") != 4 or anc_rows.shape[0] != 4 * SB * BS:
        win_rhs = lax.all_to_all(rhs_win, "rhs", split_axis=1, concat_axis=0, tiled=True)
        anc_rhs = lax.all_to_all(rhs_anc, "rhs", split_axis=1, concat_axis=0, tiled=True)
        return general_path(win_rows, anc_rows, win_pattern, anc_pattern, window_owner, sn_order, diag_inv, win_rhs, anc_rhs)

    def swap(x, m):
        return lax.ppermute(x, "rows", [(i, i ^ m) for i in range(8)])

    def deep(x, m):
        return lax.ppermute(x, "rhs", [(i, i ^ m) for i in range(4)])

    def neighbour(x):
        return lax.ppermute(x, "rows", [(i, i ^ (2 if i % 2 == 0 else 4)) for i in range(8)])

    def forward(x):
        return lax.ppermute(x, "rows", [(i, i ^ (4 if i % 2 == 0 else 2)) for i in range(8)])

    def mask_below(k, after):
        pattern_later, _ = lax.optimization_barrier((anc_pattern, after))
        return pl.pallas_call(
            make_below_mask_kernel(k),
            out_shape=shape_of((PAIR, NW)),
            in_specs=[VMEM, HBM],
            out_specs=VMEM,
            scratch_shapes=[pltpu.SemaphoreType.DMA((2 * SB,))],
            compiler_params=params(4),
            cost_estimate=cost(4),
            name="mask_below",
        )(pattern_later, in_hbm(anc_rows))

    columns = rhs_win.shape[1] // 4
    half = SN // 2
    tall = rhs_win.shape[0]
    w_own = in_hbm(win_rows)
    l_own = pl.pallas_call(
        factor_kernel,
        out_shape=shape_of((SN, SN)),
        in_specs=[SMEM, SMEM, VMEM, HBM],
        out_specs=VMEM,
        scratch_shapes=[pltpu.VMEM((SN, SN), BF16), pltpu.VMEM((SB, NWB), jnp.int32),
                        pltpu.SMEM((SB + 1,), jnp.int32), pltpu.SMEM((SB,), jnp.int32), pltpu.SemaphoreType.DMA],
        compiler_params=params(4),
        cost_estimate=cost(2),
        name="factor_pack",
    )(window_owner, sn_order, win_pattern, w_own)
    rhs_late, _ = lax.optimization_barrier((rhs_win, l_own))
    sent = pl.pallas_call(
        rhs_pack_kernel,
        out_shape=(shape_of((tall, columns)),) * 4,
        in_specs=[VMEM],
        out_specs=(VMEM,) * 4,
        compiler_params=params(4),
        cost_estimate=cost(1),
        name="rhs_pack",
    )(rhs_late)
    pieces = [sent[0]] + [deep(sent[s], s) for s in (1, 2, 3)]
    l_late, pieces[1] = lax.optimization_barrier((l_own, pieces[1]))
    l_other = swap(l_late, 1)
    l_chip = pl.pallas_call(
        chip_pack_kernel,
        out_shape=shape_of((PAIR, SN)),
        in_specs=[VMEM] * 2,
        out_specs=VMEM,
        compiler_params=params(4),
        cost_estimate=cost(1),
        name="chip_pack",
    )(l_own, l_other)
    near = neighbour(l_chip)
    w_late, _ = lax.optimization_barrier((win_rows, l_chip))
    w_other = swap(w_late, 1)
    below = [mask_below(0, l_chip)]
    w_other, below[0], *pieces = lax.optimization_barrier((w_other, *below, *pieces))
    others = [swap(x, 1) for x in pieces]
    chip_rhs, packed, part = pl.pallas_call(
        first_pack_kernel,
        out_shape=(shape_of((PAIR, columns)), shape_of((SN, columns)), shape_of((half, columns))),
        in_specs=[SMEM, SMEM] + [VMEM] * 8,
        out_specs=(VMEM,) * 3,
        scratch_shapes=[pltpu.SMEM((SB + 1,), jnp.int32)],
        compiler_params=params(4),
        cost_estimate=cost(1),
        name="first_pack",
    )(window_owner, sn_order, *pieces, *others)
    near, _ = lax.optimization_barrier((near, packed))
    near_half = pl.pallas_call(
        take_half_kernel,
        out_shape=shape_of((SN, SN)),
        in_specs=[VMEM],
        out_specs=VMEM,
        compiler_params=params(4),
        cost_estimate=cost(1),
        name="take_half",
    )(near)
    far = forward(near_half)
    owner_later, order_later, _ = lax.optimization_barrier((window_owner, sn_order, packed))
    tab, flag = pl.pallas_call(
        table_kernel,
        out_shape=(shape_of((TABLE + 1,), jnp.int32), shape_of((2,), jnp.int32)),
        in_specs=[SMEM, SMEM],
        out_specs=(SMEM, SMEM),
        compiler_params=params(4),
        cost_estimate=cost(2),
        name="tables",
    )(owner_later, order_later)
    w_other = in_vmem(w_other)
    w_own = in_vmem(win_rows)

    tile = rhs_anc.shape[0]
    sums, solved, masked = None, [], []
    diag_vmem = in_vmem(diag_inv)
    below_rows = anc_rows.shape[0]

    anc_order, anc_pieces = (2, 3, 1), [None] * 4
    for group in range(GROUPS):
        last = group == GROUPS - 1
        a_own = neighbour(packed)
        b_own = swap(part, 6)
        if group == 0:
            for k in range(GROUPS - 1):
                masked.append(pl.pallas_call(
                    make_mask_kernel(k),
                    out_shape=shape_of((SN, (k + 1) * PAIR)),
                    in_specs=[SMEM, SMEM, VMEM, VMEM, VMEM],
                    out_specs=VMEM,
                    scratch_shapes=[pltpu.VMEM((SB, NWB), jnp.int32)],
                    compiler_params=params(6),
                    cost_estimate=cost(2),
                    name="mask_rows",
                )(tab, order_later, win_pattern, w_own, w_other))
        if group == 0:
            rhs_later, _ = lax.optimization_barrier((rhs_anc, packed))
            anc_pieces = list(pl.pallas_call(
                below_rhs_kernel,
                out_shape=(shape_of((tile, columns)),) * 4,
                in_specs=[VMEM],
                out_specs=(VMEM,) * 4,
                compiler_params=params(4),
                cost_estimate=cost(1),
                name="below_rhs",
            )(in_vmem(rhs_later)))
        if not last:
            s = anc_order[group]
            moved, _ = lax.optimization_barrier((anc_pieces[s], packed))
            anc_pieces[s] = deep(moved, s)

        if group == 0:
            a_own, b_own, near, far, *masked = lax.optimization_barrier(
                (a_own, b_own, near, far, *masked))
            l_parts = [in_vmem(x) for x in (l_own, l_other, near, swap(near, 1), far, swap(far, 1))]
        operands = [tab, sn_order, diag_vmem, *l_parts]
        out_shape = [shape_of((PAIR, PAIR))]
        if not last:
            operands += [masked[group], chip_rhs, *solved]
            out_shape += [shape_of((SN, columns), F32)]
        ready = pl.pallas_call(
            make_prep_kernel(group),
            out_shape=tuple(out_shape),
            in_specs=[SMEM, SMEM] + [VMEM] * (len(operands) - 2),
            out_specs=(VMEM,) * len(out_shape),
            scratch_shapes=[pltpu.VMEM((SN, SN), BF16)],
            compiler_params=params(6),
            cost_estimate=cost(2),
            name="prep",
        )(*operands)
        hold = []
        if group == 1:
            below.append(mask_below(1, packed))
            hold = below[1:]
        elif group > 1:
            more, kernel = (solved[:2], two_rows_kernel) if group == 2 else ([solved[2], sums, *anc_pieces], base_rows_kernel)
            sums = pl.pallas_call(
                kernel,
                out_shape=shape_of((below_rows, columns), F32),
                in_specs=[SMEM] + [VMEM] * (2 + len(more)),
                out_specs=VMEM,
                scratch_shapes=[pltpu.VMEM((below_rows, columns), BF16)] if last else [],
                input_output_aliases={4: 0} if last else {},
                compiler_params=params(6),
                cost_estimate=cost(3),
                name="rows_below",
            )(sn_order, *below, *more)
            hold = [sums]
        if group > 0:
            s = anc_order[group - 1]
            a_own, b_own, anc_pieces[s], *rest = lax.optimization_barrier((a_own, b_own, anc_pieces[s], *hold, *ready))
            hold, ready = rest[:len(hold)], rest[len(hold):]
            if group == 1:
                below[1:] = hold
            else:
                sums = hold[0]
        a_swap = swap(a_own, 1)
        b_swap = swap(b_own, 1)
        ready = list(ready) if last else list(ready) + [masked[group]]

        out_shape = [shape_of((PAIR, columns))]
        if not last:
            out_shape += [shape_of((SN, columns)), shape_of((half, columns))]
        results = pl.pallas_call(
            make_solve_kernel(group),
            out_shape=tuple(out_shape),
            in_specs=[SMEM] + [VMEM] * (5 + len(ready)),
            out_specs=(VMEM,) * len(out_shape),
            scratch_shapes=[pltpu.VMEM((PAIR, columns), BF16), pltpu.VMEM((2 * PAIR, columns), BF16)],
            compiler_params=params(8),
            cost_estimate=cost(3),
            name="pair_solve",
        )(tab, packed, a_own, a_swap, b_own, b_swap, *ready)
        solved.append(results[0])
        if not last:
            packed, part = results[1:]

    outputs = pl.pallas_call(
        last_rows_kernel,
        out_shape=(shape_of((NW, columns)), shape_of((below_rows, columns))),
        in_specs=[SMEM] + [VMEM] * 7,
        out_specs=(HBM, HBM),
        scratch_shapes=[pltpu.VMEM((below_rows, columns), BF16), pltpu.SemaphoreType.DMA((2 * GROUPS,)),
                        pltpu.SemaphoreType.DMA((4,))],
        compiler_params=params(6),
        cost_estimate=cost(3),
        name="last_rows",
    )(sn_order, *below, *solved, sums)

    def again(carry):
        carry, own_pieces, below_pieces = lax.optimization_barrier((carry, pieces, anc_pieces))
        back = carry[0][1] ^ jnp.arange(4)
        win_rhs = jnp.take(jnp.stack(own_pieces), back, axis=0).reshape(4 * tall, columns)
        anc_rhs = jnp.take(jnp.stack(below_pieces), back, axis=0).reshape(4 * tile, columns)
        return jnp.zeros_like(carry[0]), *general_path(
            win_rows, anc_rows, win_pattern, anc_pattern, window_owner, sn_order, diag_inv, win_rhs, anc_rhs)

    return tuple(lax.while_loop(lambda carry: carry[0][0] != 0, again, (flag, *outputs))[1:])


def solution(mesh):
    return jax.shard_map(
        local,
        mesh=mesh,
        in_specs=(P("rows", None), P("rows", None), P(), P("rows", None), P(), P(), P(),
                  P(("rows", "rhs"), None), P(("rows", "rhs"), None)),
        out_specs=(P(None, "rhs"), P("rows", "rhs")),
        check_vma=False,
    )
```

```python
import jax
import jax.numpy as jnp
from jax import lax
from jax.experimental import pallas as pl
from jax.experimental.pallas import tpu as pltpu
from jax.sharding import PartitionSpec as P

BS = 64
SB = 8
NSUP = 8
SN = 512
NW = 4096
NWB = 64
GROUPS = 4
PAIR = 2 * SN
F32 = jnp.float32
BF16 = jnp.bfloat16


def masked_columns(factor, pattern, node_label):
    blocks = pattern.shape[0]
    columns = lax.dynamic_slice_in_dim(factor, node_label * SN, SN, 1)
    chosen = lax.dynamic_slice_in_dim(pattern, node_label * SB, SB, 1)
    shaped = columns.reshape(blocks, BS, SB, BS) * chosen[:, None, :, None].astype(BF16)
    return shaped.reshape(blocks * BS, SN)


def sum_over_rows(values):
    count = lax.axis_size("rows")
    if count & (count - 1):
        return lax.psum(values, "rows")
    step = 1
    while step < count:
        values = values + lax.ppermute(values, "rows", [(i, i ^ step) for i in range(count)])
        step *= 2
    return values


def general_path(win_rows, anc_rows, win_pattern, anc_pattern, window_owner, sn_order, diag_inv, win_rhs, anc_rhs):
    columns_rhs = win_rhs.shape[1]
    slot_count = win_rows.shape[0] // BS
    first_slot = lax.axis_index("rows") * slot_count
    local_pattern = lax.dynamic_slice_in_dim(win_pattern, first_slot, slot_count, 0)

    def step(position, carry):
        solution, win_resid, anc_resid = carry
        node_label = sn_order[position]
        owners = lax.dynamic_slice_in_dim(window_owner, node_label * SB, SB, 0)
        inverse = lax.dynamic_index_in_dim(diag_inv, node_label, 0, keepdims=False)
        local_place = owners - first_slot
        present = (local_place >= 0) & (local_place < slot_count)
        resid_blocks = win_resid.reshape(slot_count, BS, columns_rhs)
        taken = jnp.take(resid_blocks, jnp.clip(local_place, 0, slot_count - 1), axis=0)
        placed = jnp.where(present[:, None, None], taken, 0.0).reshape(SN, columns_rhs)
        panel = sum_over_rows(placed.astype(BF16))
        solved = jnp.dot(inverse, panel, preferred_element_type=F32).astype(BF16)
        solution = lax.dynamic_update_slice_in_dim(solution, solved, node_label * SN, 0)
        win_part = jnp.dot(masked_columns(win_rows, local_pattern, node_label), solved, preferred_element_type=F32)
        anc_part = jnp.dot(masked_columns(anc_rows, anc_pattern, node_label), solved, preferred_element_type=F32)
        return solution, win_resid - win_part, anc_resid - anc_part

    first = (jnp.zeros((NW, columns_rhs), BF16), win_rhs.astype(F32), anc_rhs.astype(F32))
    solution, _, anc_resid = lax.fori_loop(0, NSUP, step, first)
    return solution, anc_resid.astype(BF16)


def spread_matrix():
    block_index = lax.broadcasted_iota(jnp.int32, (NWB, SN), 0)
    lane_index = lax.broadcasted_iota(jnp.int32, (NWB, SN), 1)
    return ((block_index & 7) == (lane_index >> 6)).astype(F32).astype(BF16)


def expand_mask(rows_pattern, label, spread):
    lane = lax.broadcasted_iota(jnp.int32, rows_pattern.shape, 1)
    chosen = jnp.where((lane >> 3) == label, rows_pattern, 0).astype(F32).astype(BF16)
    return jnp.dot(chosen, spread, preferred_element_type=F32).astype(BF16)


def masked_rows(block_of, mask, count):
    return jnp.concatenate([block_of(j) * mask[j:j + 1, :] for j in range(count)], axis=0)


def rows_at(index):
    return pl.ds(pl.multiple_of(index * BS, BS), BS)


def columns_at(label):
    return pl.ds(pl.multiple_of(label * SN, SN), SN)


SRC, LSRC, PACK, TABLE = 0, 64, 96, 128


def factor_kernel(owner, order, pattern, win_ref, out, buf, pat, inv, pos, sem):
    row = lax.axis_index("rows")

    for w in range(NWB):
        slot = owner[w]
        inv[jnp.where((slot >> 3) == row, (slot & 7), SB)] = w
    for k in range(NSUP):
        pos[order[k]] = k
    labels = jnp.zeros((SB, 1), jnp.int32)
    for t in range(SB):
        label = order[(pos[(inv[t] >> 3)] // 2) * 2]
        pltpu.make_async_copy(win_ref.at[pl.ds(t * BS, BS), columns_at(label)], buf.at[pl.ds(t * BS, BS), :], sem).start()
        labels = jnp.where(lax.broadcasted_iota(jnp.int32, (SB, 1), 0) == t, label, labels)
    pat[...] = pattern[pl.ds(pl.multiple_of(row * SB, SB), SB), :]
    mask = expand_mask(pat[...], labels, spread_matrix())
    pltpu.make_async_copy(win_ref.at[:, pl.ds(0, SN)], buf, sem).wait()
    for j in range(SB):
        out[j * BS:(j + 1) * BS, :] = buf[j * BS:(j + 1) * BS, :] * mask[j:j + 1, :]


def rhs_pack_kernel(rhs_ref, *sent):
    depth = lax.axis_index("rhs")
    width = sent[0].shape[1]
    for s, out in enumerate(sent):
        at = pl.multiple_of(jnp.bitwise_xor(depth, s) * width, width)
        out[...] = rhs_ref[:, pl.ds(at, width)]


def chip_pack_kernel(own_ref, other_ref, l_chip):
    l_chip[0:SN, :] = own_ref[...]
    l_chip[SN:PAIR, :] = other_ref[...]


def take_half_kernel(x_ref, out):
    out[...] = x_ref[0:SN, :]


def table_kernel(owner, order, tab, flag):
    row = lax.axis_index("rows")
    chip, core = (row >> 1), (row & 1)
    bad = 0
    for t in range(GROUPS * SB):
        tab[PACK + t] = 0
    for group in range(GROUPS):
        counts = 0
        for i in range(2 * SB):
            slot = owner[order[2 * group + (i >> 3)] * SB + (i & 7)]
            where, device = (slot >> 4), (slot >> 3)
            rank = (counts >> (8 * where)) & 255
            counts = counts + (1 << (8 * where))
            bad = bad | ((rank >> 3))
            rank = jnp.minimum(rank, SB - 1)
            rel = jnp.bitwise_xor(where, chip)
            cross = jnp.bitwise_xor((device & 1), core)
            kind = jnp.where((rel == 1) | (rel == 2), jnp.where(rel == 1 + core, 1, 2), rel)
            far_rank = 3 * SB + jnp.where((rank >> 2) == core, 0, 4) + (rank & 3)
            tab[SRC + group * 16 + i] = jnp.where(kind == 3, far_rank, kind * SB + rank)
            tab[jnp.where(rel == 0, PACK + group * SB + rank, TABLE)] = cross * SB + (slot & 7)
            if i >= SB:
                tab[LSRC + group * SB + i - SB] = (2 * kind + cross) * SB + (slot & 7)
    flag[0] = bad
    flag[1] = lax.axis_index("rhs")


def below_rhs_kernel(rhs_ref, *outs):
    depth = lax.axis_index("rhs")
    width = outs[0].shape[1]
    for s, out in enumerate(outs):
        out[...] = rhs_ref[:, pl.ds(pl.multiple_of(jnp.bitwise_xor(depth, s) * width, width), width)]


def first_pack_kernel(owner, order, *refs):
    pieces, (chip_rhs, p_ref, b_ref, place) = refs[:8], refs[8:]
    row, depth = lax.axis_index("rows"), lax.axis_index("rhs")
    core = (row & 1)
    tall = pieces[0].shape[0]
    for side in range(2):
        for s in range(4):
            at = pl.multiple_of(side * SB * BS + jnp.bitwise_xor(depth, s) * tall, tall)
            chip_rhs[pl.ds(at, tall), :] = pieces[4 * side + s][...]
    for t in range(SB):
        place[t] = 0
    rank = 0
    for i in range(2 * SB):
        slot = owner[order[(i >> 3)] * SB + (i & 7)]
        here = (slot >> 4) == (row >> 1)
        place[jnp.where(here & (rank < SB), rank, SB)] = jnp.bitwise_xor(((slot >> 3) & 1), core) * SB + (slot & 7)
        rank = rank + jnp.where(here, 1, 0)
    for t in range(SB):
        p_ref[t * BS:(t + 1) * BS, :] = chip_rhs[rows_at(place[t]), :]
    b_ref[...] = p_ref[pl.ds(pl.multiple_of(core * (SB >> 1) * BS, (SB >> 1) * BS), (SB >> 1) * BS), :]


def make_mask_kernel(group):
    def kernel(tab, order, pattern, w_own, w_other, out, pat):
        row = lax.axis_index("rows")
        places = [tab[PACK + (group + 1) * SB + j] for j in range(SB)]
        for j, place in enumerate(places):
            pat[j:j + 1, :] = pattern[pl.ds(jnp.bitwise_xor(row, (place >> 3)) * SB + (place & 7), 1), :]
        spread = spread_matrix()
        rows = pat[...]
        masks = [expand_mask(rows, order[k], spread) for k in range(2 * group + 2)]
        for j, place in enumerate(places):
            at = slice(j * BS, (j + 1) * BS)
            for side, w_ref in enumerate((w_own, w_other)):
                @pl.when((place >> 3) == side)
                def _(w_ref=w_ref, at=at, j=j, place=place):
                    for k in range(2 * group + 2):
                        block = w_ref[rows_at((place & 7)), columns_at(order[k])]
                        out[at, k * SN:(k + 1) * SN] = block * masks[k][j:j + 1, :]

    return kernel


def make_prep_kernel(group):
    last = group == GROUPS - 1

    def kernel(tab, order, diag, *refs):
        own, other, near, near_swap, far, far_swap = refs[:6]
        l_refs = ((own, 0), (other, 0), (near, 0), (near, SB), (near_swap, SB), (near_swap, 0), (far, 0), (far_swap, 0))
        refs = refs[6:]
        if last:
            m_out, lbuf = refs
        else:
            w_ref, chip_rhs = refs[:2]
            xs = refs[2:2 + group]
            m_out, r_out, lbuf = refs[2 + group:]
        for i in range(SB):
            code = tab[LSRC + group * SB + i]
            for m in range(8):
                @pl.when((code >> 3) == m)
                def _(m=m, i=i, code=code):
                    lbuf[i * BS:(i + 1) * BS, :] = l_refs[m][0][rows_at((code & 7) + l_refs[m][1]), :]
        first, second = diag[order[2 * group]], diag[order[2 * group + 1]]
        m_out[0:SN, 0:SN] = first
        m_out[SN:PAIR, SN:PAIR] = second
        joined = jnp.dot(second, lbuf[...], preferred_element_type=F32).astype(BF16)
        m_out[SN:PAIR, 0:SN] = (-jnp.dot(joined, first, preferred_element_type=F32)).astype(BF16)
        if not last:
            total = jnp.concatenate([chip_rhs[rows_at(tab[PACK + (group + 1) * SB + j]), :] for j in range(SB)], axis=0).astype(F32)
            for k in range(group):
                total = total - jnp.dot(w_ref[:, k * PAIR:(k + 1) * PAIR], xs[k][...], preferred_element_type=F32)
            r_out[...] = total

    return kernel


def make_solve_kernel(group):
    last = group == GROUPS - 1

    def kernel(*refs):
        tab, sources, m_ref = refs[0], refs[1:6], refs[6]
        if last:
            x_ref, panel, pool = refs[7:]
        else:
            r_ref, wn_ref, x_ref, p_ref, b_ref, panel, pool = refs[7:]
        at = 0
        for source in sources:
            pool[at:at + source.shape[0], :] = source[...]
            at += source.shape[0]
        for i in range(2 * SB):
            panel[i * BS:(i + 1) * BS, :] = pool[rows_at(tab[SRC + group * 16 + i]), :]
        x_ref[0:SN, :] = jnp.dot(m_ref[0:SN, 0:SN], panel[0:SN, :], preferred_element_type=F32).astype(BF16)
        x_ref[SN:PAIR, :] = jnp.dot(m_ref[SN:PAIR, :], panel[...], preferred_element_type=F32).astype(BF16)
        if last:
            return
        total = r_ref[...] - jnp.dot(wn_ref[:, group * PAIR:(group + 1) * PAIR], x_ref[...], preferred_element_type=F32)
        p_ref[...] = total.astype(BF16)
        core = lax.axis_index("rows") % 2
        b_ref[...] = p_ref[pl.ds(pl.multiple_of(core * (SB >> 1) * BS, (SB >> 1) * BS), (SB >> 1) * BS), :]

    return kernel


def make_below_mask_kernel(tile):
    def kernel(pattern, a_ref, out, sems):
        copies = []
        count = 2 * SB
        for j in range(count):
            c = pltpu.make_async_copy(a_ref.at[pl.ds((tile * count + j) * BS, BS), :], out.at[pl.ds(j * BS, BS), :], sems.at[j])
            c.start()
            copies.append(c)
        spread = spread_matrix()
        rows = pattern[tile * count:(tile + 1) * count, :]
        masks = [expand_mask(rows, k, spread) for k in range(NSUP)]
        for j in range(count):
            copies[j].wait()
            for k in range(NSUP):
                at = (slice(j * BS, (j + 1) * BS), slice(k * SN, (k + 1) * SN))
                out[at] = out[at] * masks[k][j:j + 1, :]

    return kernel


def below_product(order, a_ref, x_ref, group, i):
    rows = slice(((i & 1)) * SN, ((i & 1) + 1) * SN)
    first = jnp.dot(a_ref[rows, columns_at(order[2 * group])], x_ref[0:SN, :], preferred_element_type=F32)
    return first + jnp.dot(a_ref[rows, columns_at(order[2 * group + 1])], x_ref[SN:PAIR, :], preferred_element_type=F32)


def two_rows_kernel(order, a0, a1, x0_ref, x1_ref, out):
    for i, a_ref in enumerate((a0, a0, a1, a1)):
        out[i * SN:(i + 1) * SN, :] = below_product(order, a_ref, x0_ref, 0, i) + below_product(order, a_ref, x1_ref, 1, i)


def base_rows_kernel(order, a0, a1, x_ref, sums, h0, h1, h2, h3, out, rhs):
    depth = lax.axis_index("rhs")
    tall = h0.shape[0]
    for s, h in enumerate((h0, h1, h2, h3)):
        rhs[pl.ds(pl.multiple_of(jnp.bitwise_xor(depth, s) * tall, tall), tall), :] = h[...]
    for i, a_ref in enumerate((a0, a0, a1, a1)):
        at = slice(i * SN, (i + 1) * SN)
        out[at, :] = rhs[at, :].astype(F32) - (sums[at, :] + below_product(order, a_ref, x_ref, 2, i))


def last_rows_kernel(order, a0, a1, x0, x1, x2, x3, base, sol_ref, out_ref, done, sems, osem):
    copies = []
    for k, x in enumerate((x0, x1, x2, x3)):
        for q in range(2):
            at = pl.multiple_of(order[2 * k + q] * SN, SN)
            copies.append(pltpu.make_async_copy(x.at[pl.ds(q * SN, SN), :], sol_ref.at[pl.ds(at, SN), :], sems.at[2 * k + q]))
            copies[-1].start()
    for i, a_ref in enumerate((a0, a0, a1, a1)):
        at = slice(i * SN, (i + 1) * SN)
        done[at, :] = (base[at, :] - below_product(order, a_ref, x3, GROUPS - 1, i)).astype(BF16)
        copies.append(pltpu.make_async_copy(done.at[pl.ds(i * SN, SN), :], out_ref.at[pl.ds(i * SN, SN), :], osem.at[i]))
        copies[-1].start()
    for c in copies:
        c.wait()


def in_vmem(x):
    return pltpu.with_memory_space_constraint(x, pltpu.VMEM)


def in_hbm(x):
    return pltpu.with_memory_space_constraint(x, pltpu.HBM)


SMEM = pl.BlockSpec(memory_space=pltpu.SMEM)
VMEM = pl.BlockSpec(memory_space=pltpu.VMEM)
HBM = pl.BlockSpec(memory_space=pltpu.HBM)


def params(mib):
    return pltpu.CompilerParams(vmem_limit_bytes=mib * 1024 * 1024)


def cost(micros):
    return pl.CostEstimate(flops=micros * 10 ** 8, bytes_accessed=micros * 3 * 10 ** 6, transcendentals=0)


def shape_of(dims, dtype=BF16):
    return jax.ShapeDtypeStruct(dims, dtype)


def local(win_rows, anc_rows, win_pattern, anc_pattern, window_owner, sn_order, diag_inv, rhs_win, rhs_anc):
    if lax.axis_size("rows") != 8 or lax.axis_size("rhs") != 4 or anc_rows.shape[0] != 4 * SB * BS:
        win_rhs = lax.all_to_all(rhs_win, "rhs", split_axis=1, concat_axis=0, tiled=True)
        anc_rhs = lax.all_to_all(rhs_anc, "rhs", split_axis=1, concat_axis=0, tiled=True)
        return general_path(win_rows, anc_rows, win_pattern, anc_pattern, window_owner, sn_order, diag_inv, win_rhs, anc_rhs)

    def swap(x, m):
        return lax.ppermute(x, "rows", [(i, i ^ m) for i in range(8)])

    def deep(x, m):
        return lax.ppermute(x, "rhs", [(i, i ^ m) for i in range(4)])

    def neighbour(x):
        return lax.ppermute(x, "rows", [(i, i ^ (2 if i % 2 == 0 else 4)) for i in range(8)])

    def forward(x):
        return lax.ppermute(x, "rows", [(i, i ^ (4 if i % 2 == 0 else 2)) for i in range(8)])

    def mask_below(k, after):
        pattern_later, _ = lax.optimization_barrier((anc_pattern, after))
        return pl.pallas_call(
            make_below_mask_kernel(k),
            out_shape=shape_of((PAIR, NW)),
            in_specs=[VMEM, HBM],
            out_specs=VMEM,
            scratch_shapes=[pltpu.SemaphoreType.DMA((2 * SB,))],
            compiler_params=params(4),
            cost_estimate=cost(4),
            name="mask_below",
        )(pattern_later, in_hbm(anc_rows))

    columns = rhs_win.shape[1] // 4
    half = SN // 2
    tall = rhs_win.shape[0]
    w_own = in_hbm(win_rows)
    l_own = pl.pallas_call(
        factor_kernel,
        out_shape=shape_of((SN, SN)),
        in_specs=[SMEM, SMEM, VMEM, HBM],
        out_specs=VMEM,
        scratch_shapes=[pltpu.VMEM((SN, SN), BF16), pltpu.VMEM((SB, NWB), jnp.int32),
                        pltpu.SMEM((SB + 1,), jnp.int32), pltpu.SMEM((SB,), jnp.int32), pltpu.SemaphoreType.DMA],
        compiler_params=params(4),
        cost_estimate=cost(2),
        name="factor_pack",
    )(window_owner, sn_order, win_pattern, w_own)
    l_other = swap(l_own, 1)
    l_chip = pl.pallas_call(
        chip_pack_kernel,
        out_shape=shape_of((PAIR, SN)),
        in_specs=[VMEM] * 2,
        out_specs=VMEM,
        compiler_params=params(4),
        cost_estimate=cost(1),
        name="chip_pack",
    )(l_own, l_other)
    near = neighbour(l_chip)
    rhs_late, _ = lax.optimization_barrier((rhs_win, l_chip))
    sent = pl.pallas_call(
        rhs_pack_kernel,
        out_shape=(shape_of((tall, columns)),) * 4,
        in_specs=[VMEM],
        out_specs=(VMEM,) * 4,
        compiler_params=params(4),
        cost_estimate=cost(1),
        name="rhs_pack",
    )(rhs_late)
    pieces = [sent[0]] + [deep(sent[s], s) for s in (1, 2, 3)]
    w_late, _ = lax.optimization_barrier((win_rows, l_chip))
    w_other = swap(w_late, 1)
    below = [mask_below(0, l_chip)]
    near, w_other, below[0], *pieces = lax.optimization_barrier((near, w_other, *below, *pieces))
    others = [swap(x, 1) for x in pieces]
    chip_rhs, packed, part = pl.pallas_call(
        first_pack_kernel,
        out_shape=(shape_of((PAIR, columns)), shape_of((SN, columns)), shape_of((half, columns))),
        in_specs=[SMEM, SMEM] + [VMEM] * 8,
        out_specs=(VMEM,) * 3,
        scratch_shapes=[pltpu.SMEM((SB + 1,), jnp.int32)],
        compiler_params=params(4),
        cost_estimate=cost(1),
        name="first_pack",
    )(window_owner, sn_order, *pieces, *others)
    near_half = pl.pallas_call(
        take_half_kernel,
        out_shape=shape_of((SN, SN)),
        in_specs=[VMEM],
        out_specs=VMEM,
        compiler_params=params(4),
        cost_estimate=cost(1),
        name="take_half",
    )(near)
    far = forward(near_half)
    owner_later, order_later, _ = lax.optimization_barrier((window_owner, sn_order, packed))
    tab, flag = pl.pallas_call(
        table_kernel,
        out_shape=(shape_of((TABLE + 1,), jnp.int32), shape_of((2,), jnp.int32)),
        in_specs=[SMEM, SMEM],
        out_specs=(SMEM, SMEM),
        compiler_params=params(4),
        cost_estimate=cost(2),
        name="tables",
    )(owner_later, order_later)
    w_other = in_vmem(w_other)
    w_own = in_vmem(win_rows)

    tile = rhs_anc.shape[0]
    sums, solved, masked = None, [], []
    diag_vmem = in_vmem(diag_inv)
    below_rows = anc_rows.shape[0]

    anc_order, anc_pieces = (2, 3, 1), [None] * 4
    for group in range(GROUPS):
        last = group == GROUPS - 1
        a_own = neighbour(packed)
        b_own = swap(part, 6)
        if group == 0:
            for k in range(GROUPS - 1):
                masked.append(pl.pallas_call(
                    make_mask_kernel(k),
                    out_shape=shape_of((SN, (k + 1) * PAIR)),
                    in_specs=[SMEM, SMEM, VMEM, VMEM, VMEM],
                    out_specs=VMEM,
                    scratch_shapes=[pltpu.VMEM((SB, NWB), jnp.int32)],
                    compiler_params=params(6),
                    cost_estimate=cost(2),
                    name="mask_rows",
                )(tab, order_later, win_pattern, w_own, w_other))
        if group == 0:
            rhs_later, _ = lax.optimization_barrier((rhs_anc, packed))
            anc_pieces = list(pl.pallas_call(
                below_rhs_kernel,
                out_shape=(shape_of((tile, columns)),) * 4,
                in_specs=[VMEM],
                out_specs=(VMEM,) * 4,
                compiler_params=params(4),
                cost_estimate=cost(1),
                name="below_rhs",
            )(in_vmem(rhs_later)))
        if not last:
            s = anc_order[group]
            moved, _ = lax.optimization_barrier((anc_pieces[s], packed))
            anc_pieces[s] = deep(moved, s)

        if group == 0:
            a_own, b_own, near, far, *masked = lax.optimization_barrier(
                (a_own, b_own, near, far, *masked))
            l_parts = [in_vmem(x) for x in (l_own, l_other, near, swap(near, 1), far, swap(far, 1))]
        operands = [tab, sn_order, diag_vmem, *l_parts]
        out_shape = [shape_of((PAIR, PAIR))]
        if not last:
            operands += [masked[group], chip_rhs, *solved]
            out_shape += [shape_of((SN, columns), F32)]
        ready = pl.pallas_call(
            make_prep_kernel(group),
            out_shape=tuple(out_shape),
            in_specs=[SMEM, SMEM] + [VMEM] * (len(operands) - 2),
            out_specs=(VMEM,) * len(out_shape),
            scratch_shapes=[pltpu.VMEM((SN, SN), BF16)],
            compiler_params=params(6),
            cost_estimate=cost(2),
            name="prep",
        )(*operands)
        hold = []
        if group == 1:
            below.append(mask_below(1, packed))
            hold = below[1:]
        elif group > 1:
            more, kernel = (solved[:2], two_rows_kernel) if group == 2 else ([solved[2], sums, *anc_pieces], base_rows_kernel)
            sums = pl.pallas_call(
                kernel,
                out_shape=shape_of((below_rows, columns), F32),
                in_specs=[SMEM] + [VMEM] * (2 + len(more)),
                out_specs=VMEM,
                scratch_shapes=[pltpu.VMEM((below_rows, columns), BF16)] if last else [],
                input_output_aliases={4: 0} if last else {},
                compiler_params=params(6),
                cost_estimate=cost(3),
                name="rows_below",
            )(sn_order, *below, *more)
            hold = [sums]
        if group > 0:
            s = anc_order[group - 1]
            a_own, b_own, anc_pieces[s], *rest = lax.optimization_barrier((a_own, b_own, anc_pieces[s], *hold, *ready))
            hold, ready = rest[:len(hold)], rest[len(hold):]
            if group == 1:
                below[1:] = hold
            else:
                sums = hold[0]
        a_swap = swap(a_own, 1)
        b_swap = swap(b_own, 1)
        ready = list(ready) if last else list(ready) + [masked[group]]

        out_shape = [shape_of((PAIR, columns))]
        if not last:
            out_shape += [shape_of((SN, columns)), shape_of((half, columns))]
        results = pl.pallas_call(
            make_solve_kernel(group),
            out_shape=tuple(out_shape),
            in_specs=[SMEM] + [VMEM] * (5 + len(ready)),
            out_specs=(VMEM,) * len(out_shape),
            scratch_shapes=[pltpu.VMEM((PAIR, columns), BF16), pltpu.VMEM((2 * PAIR, columns), BF16)],
            compiler_params=params(8),
            cost_estimate=cost(3),
            name="pair_solve",
        )(tab, packed, a_own, a_swap, b_own, b_swap, *ready)
        solved.append(results[0])
        if not last:
            packed, part = results[1:]

    outputs = pl.pallas_call(
        last_rows_kernel,
        out_shape=(shape_of((NW, columns)), shape_of((below_rows, columns))),
        in_specs=[SMEM] + [VMEM] * 7,
        out_specs=(HBM, HBM),
        scratch_shapes=[pltpu.VMEM((below_rows, columns), BF16), pltpu.SemaphoreType.DMA((2 * GROUPS,)),
                        pltpu.SemaphoreType.DMA((4,))],
        compiler_params=params(6),
        cost_estimate=cost(3),
        name="last_rows",
    )(sn_order, *below, *solved, sums)

    def again(carry):
        carry, own_pieces, below_pieces = lax.optimization_barrier((carry, pieces, anc_pieces))
        back = carry[0][1] ^ jnp.arange(4)
        win_rhs = jnp.take(jnp.stack(own_pieces), back, axis=0).reshape(4 * tall, columns)
        anc_rhs = jnp.take(jnp.stack(below_pieces), back, axis=0).reshape(4 * tile, columns)
        return jnp.zeros_like(carry[0]), *general_path(
            win_rows, anc_rows, win_pattern, anc_pattern, window_owner, sn_order, diag_inv, win_rhs, anc_rhs)

    return tuple(lax.while_loop(lambda carry: carry[0][0] != 0, again, (flag, *outputs))[1:])


def solution(mesh):
    return jax.shard_map(
        local,
        mesh=mesh,
        in_specs=(P("rows", None), P("rows", None), P(), P("rows", None), P(), P(), P(),
                  P(("rows", "rhs"), None), P(("rows", "rhs"), None)),
        out_specs=(P(None, "rhs"), P("rows", "rhs")),
        check_vma=False,
    )
```

```python
import jax
import jax.numpy as jnp
from jax import lax
from jax.experimental import pallas as pl
from jax.experimental.pallas import tpu as pltpu
from jax.sharding import PartitionSpec as P

BS = 64
SB = 8
NSUP = 8
SN = 512
NW = 4096
NWB = 64
GROUPS = 4
PAIR = 2 * SN
F32 = jnp.float32
BF16 = jnp.bfloat16


def masked_columns(factor, pattern, node_label):
    blocks = pattern.shape[0]
    columns = lax.dynamic_slice_in_dim(factor, node_label * SN, SN, 1)
    chosen = lax.dynamic_slice_in_dim(pattern, node_label * SB, SB, 1)
    shaped = columns.reshape(blocks, BS, SB, BS) * chosen[:, None, :, None].astype(BF16)
    return shaped.reshape(blocks * BS, SN)


def sum_over_rows(values):
    count = lax.axis_size("rows")
    if count & (count - 1):
        return lax.psum(values, "rows")
    step = 1
    while step < count:
        values = values + lax.ppermute(values, "rows", [(i, i ^ step) for i in range(count)])
        step *= 2
    return values


def general_path(win_rows, anc_rows, win_pattern, anc_pattern, window_owner, sn_order, diag_inv, win_rhs, anc_rhs):
    columns_rhs = win_rhs.shape[1]
    slot_count = win_rows.shape[0] // BS
    first_slot = lax.axis_index("rows") * slot_count
    local_pattern = lax.dynamic_slice_in_dim(win_pattern, first_slot, slot_count, 0)

    def step(position, carry):
        solution, win_resid, anc_resid = carry
        node_label = sn_order[position]
        owners = lax.dynamic_slice_in_dim(window_owner, node_label * SB, SB, 0)
        inverse = lax.dynamic_index_in_dim(diag_inv, node_label, 0, keepdims=False)
        local_place = owners - first_slot
        present = (local_place >= 0) & (local_place < slot_count)
        resid_blocks = win_resid.reshape(slot_count, BS, columns_rhs)
        taken = jnp.take(resid_blocks, jnp.clip(local_place, 0, slot_count - 1), axis=0)
        placed = jnp.where(present[:, None, None], taken, 0.0).reshape(SN, columns_rhs)
        panel = sum_over_rows(placed.astype(BF16))
        solved = jnp.dot(inverse, panel, preferred_element_type=F32).astype(BF16)
        solution = lax.dynamic_update_slice_in_dim(solution, solved, node_label * SN, 0)
        win_part = jnp.dot(masked_columns(win_rows, local_pattern, node_label), solved, preferred_element_type=F32)
        anc_part = jnp.dot(masked_columns(anc_rows, anc_pattern, node_label), solved, preferred_element_type=F32)
        return solution, win_resid - win_part, anc_resid - anc_part

    first = (jnp.zeros((NW, columns_rhs), BF16), win_rhs.astype(F32), anc_rhs.astype(F32))
    solution, _, anc_resid = lax.fori_loop(0, NSUP, step, first)
    return solution, anc_resid.astype(BF16)


def spread_matrix():
    block_index = lax.broadcasted_iota(jnp.int32, (NWB, SN), 0)
    lane_index = lax.broadcasted_iota(jnp.int32, (NWB, SN), 1)
    return ((block_index & 7) == (lane_index >> 6)).astype(F32).astype(BF16)


def expand_mask(rows_pattern, label, spread):
    lane = lax.broadcasted_iota(jnp.int32, rows_pattern.shape, 1)
    chosen = jnp.where((lane >> 3) == label, rows_pattern, 0).astype(F32).astype(BF16)
    return jnp.dot(chosen, spread, preferred_element_type=F32).astype(BF16)


def masked_rows(block_of, mask, count):
    return jnp.concatenate([block_of(j) * mask[j:j + 1, :] for j in range(count)], axis=0)


def rows_at(index):
    return pl.ds(pl.multiple_of(index * BS, BS), BS)


def columns_at(label):
    return pl.ds(pl.multiple_of(label * SN, SN), SN)


SRC, LSRC, PACK, TABLE = 0, 64, 96, 128


def factor_kernel(owner, order, pattern, win_ref, out, buf, pat, inv, pos, sem):
    row = lax.axis_index("rows")

    for w in range(NWB):
        slot = owner[w]
        inv[jnp.where((slot >> 3) == row, (slot & 7), SB)] = w
    for k in range(NSUP):
        pos[order[k]] = k
    labels = jnp.zeros((SB, 1), jnp.int32)
    for t in range(SB):
        label = order[(pos[(inv[t] >> 3)] // 2) * 2]
        pltpu.make_async_copy(win_ref.at[pl.ds(t * BS, BS), columns_at(label)], buf.at[pl.ds(t * BS, BS), :], sem).start()
        labels = jnp.where(lax.broadcasted_iota(jnp.int32, (SB, 1), 0) == t, label, labels)
    pat[...] = pattern[pl.ds(pl.multiple_of(row * SB, SB), SB), :]
    mask = expand_mask(pat[...], labels, spread_matrix())
    pltpu.make_async_copy(win_ref.at[:, pl.ds(0, SN)], buf, sem).wait()
    for j in range(SB):
        out[j * BS:(j + 1) * BS, :] = buf[j * BS:(j + 1) * BS, :] * mask[j:j + 1, :]


def rhs_pack_kernel(rhs_ref, *sent):
    depth = lax.axis_index("rhs")
    width = sent[0].shape[1]
    for s, out in enumerate(sent):
        at = pl.multiple_of(jnp.bitwise_xor(depth, s) * width, width)
        out[...] = rhs_ref[:, pl.ds(at, width)]


def table_kernel(owner, order, tab, flag):
    row = lax.axis_index("rows")
    chip, core = (row >> 1), (row & 1)
    bad = 0
    for t in range(GROUPS * SB):
        tab[PACK + t] = 0
    for group in range(GROUPS):
        counts = 0
        for i in range(2 * SB):
            slot = owner[order[2 * group + (i >> 3)] * SB + (i & 7)]
            where, device = (slot >> 4), (slot >> 3)
            rank = (counts >> (8 * where)) & 255
            counts = counts + (1 << (8 * where))
            bad = bad | ((rank >> 3))
            rank = jnp.minimum(rank, SB - 1)
            rel = jnp.bitwise_xor(where, chip)
            cross = jnp.bitwise_xor((device & 1), core)
            kind = jnp.where((rel == 1) | (rel == 2), jnp.where(rel == 1 + core, 1, 2), rel)
            far_rank = 3 * SB + jnp.where((rank >> 2) == core, 0, 4) + (rank & 3)
            tab[SRC + group * 16 + i] = jnp.where(kind == 3, far_rank, kind * SB + rank)
            tab[jnp.where(rel == 0, PACK + group * SB + rank, TABLE)] = cross * SB + (slot & 7)
            if i >= SB:
                tab[LSRC + group * SB + i - SB] = (2 * kind + cross) * SB + (slot & 7)
    flag[0] = bad
    flag[1] = lax.axis_index("rhs")


def below_rhs_kernel(rhs_ref, *outs):
    depth = lax.axis_index("rhs")
    width = outs[0].shape[1]
    for s, out in enumerate(outs):
        out[...] = rhs_ref[:, pl.ds(pl.multiple_of(jnp.bitwise_xor(depth, s) * width, width), width)]


def first_pack_kernel(owner, order, *refs):
    pieces, (chip_rhs, p_ref, b_ref, place) = refs[:8], refs[8:]
    row, depth = lax.axis_index("rows"), lax.axis_index("rhs")
    core = (row & 1)
    tall = pieces[0].shape[0]
    for side in range(2):
        for s in range(4):
            at = pl.multiple_of(side * SB * BS + jnp.bitwise_xor(depth, s) * tall, tall)
            chip_rhs[pl.ds(at, tall), :] = pieces[4 * side + s][...]
    for t in range(SB):
        place[t] = 0
    rank = 0
    for i in range(2 * SB):
        slot = owner[order[(i >> 3)] * SB + (i & 7)]
        here = (slot >> 4) == (row >> 1)
        place[jnp.where(here & (rank < SB), rank, SB)] = jnp.bitwise_xor(((slot >> 3) & 1), core) * SB + (slot & 7)
        rank = rank + jnp.where(here, 1, 0)
    for t in range(SB):
        p_ref[t * BS:(t + 1) * BS, :] = chip_rhs[rows_at(place[t]), :]
    b_ref[...] = p_ref[pl.ds(pl.multiple_of(core * (SB >> 1) * BS, (SB >> 1) * BS), (SB >> 1) * BS), :]


def make_mask_kernel(group):
    def kernel(tab, order, pattern, w_own, w_other, out, pat):
        row = lax.axis_index("rows")
        places = [tab[PACK + (group + 1) * SB + j] for j in range(SB)]
        for j, place in enumerate(places):
            pat[j:j + 1, :] = pattern[pl.ds(jnp.bitwise_xor(row, (place >> 3)) * SB + (place & 7), 1), :]
        spread = spread_matrix()
        rows = pat[...]
        masks = [expand_mask(rows, order[k], spread) for k in range(2 * group + 2)]
        for j, place in enumerate(places):
            at = slice(j * BS, (j + 1) * BS)
            for side, w_ref in enumerate((w_own, w_other)):
                @pl.when((place >> 3) == side)
                def _(w_ref=w_ref, at=at, j=j, place=place):
                    for k in range(2 * group + 2):
                        block = w_ref[rows_at((place & 7)), columns_at(order[k])]
                        out[at, k * SN:(k + 1) * SN] = block * masks[k][j:j + 1, :]

    return kernel


def make_prep_kernel(group):
    last = group == GROUPS - 1

    def kernel(tab, order, diag, *refs):
        l_refs, refs = refs[:8], refs[8:]
        if last:
            m_out, lbuf = refs
        else:
            w_ref, chip_rhs = refs[:2]
            xs = refs[2:2 + group]
            m_out, r_out, lbuf = refs[2 + group:]
        for i in range(SB):
            code = tab[LSRC + group * SB + i]
            for m in range(8):
                @pl.when((code >> 3) == m)
                def _(m=m, i=i, code=code):
                    lbuf[i * BS:(i + 1) * BS, :] = l_refs[m][rows_at(code & 7), :]
        first, second = diag[order[2 * group]], diag[order[2 * group + 1]]
        m_out[0:SN, 0:SN] = first
        m_out[SN:PAIR, SN:PAIR] = second
        joined = jnp.dot(second, lbuf[...], preferred_element_type=F32).astype(BF16)
        m_out[SN:PAIR, 0:SN] = (-jnp.dot(joined, first, preferred_element_type=F32)).astype(BF16)
        if not last:
            total = jnp.concatenate([chip_rhs[rows_at(tab[PACK + (group + 1) * SB + j]), :] for j in range(SB)], axis=0).astype(F32)
            for k in range(group):
                total = total - jnp.dot(w_ref[:, k * PAIR:(k + 1) * PAIR], xs[k][...], preferred_element_type=F32)
            r_out[...] = total

    return kernel


def make_solve_kernel(group):
    last = group == GROUPS - 1

    def kernel(*refs):
        tab, sources, m_ref = refs[0], refs[1:6], refs[6]
        if last:
            x_ref, panel, pool = refs[7:]
        else:
            r_ref, wn_ref, x_ref, p_ref, b_ref, panel, pool = refs[7:]
        at = 0
        for source in sources:
            pool[at:at + source.shape[0], :] = source[...]
            at += source.shape[0]
        for i in range(2 * SB):
            panel[i * BS:(i + 1) * BS, :] = pool[rows_at(tab[SRC + group * 16 + i]), :]
        x_ref[0:SN, :] = jnp.dot(m_ref[0:SN, 0:SN], panel[0:SN, :], preferred_element_type=F32).astype(BF16)
        x_ref[SN:PAIR, :] = jnp.dot(m_ref[SN:PAIR, :], panel[...], preferred_element_type=F32).astype(BF16)
        if last:
            return
        total = r_ref[...] - jnp.dot(wn_ref[:, group * PAIR:(group + 1) * PAIR], x_ref[...], preferred_element_type=F32)
        p_ref[...] = total.astype(BF16)
        core = lax.axis_index("rows") % 2
        b_ref[...] = p_ref[pl.ds(pl.multiple_of(core * (SB >> 1) * BS, (SB >> 1) * BS), (SB >> 1) * BS), :]

    return kernel


def make_below_mask_kernel(tile):
    def kernel(pattern, a_ref, out, sems):
        copies = []
        count = 2 * SB
        for j in range(count):
            c = pltpu.make_async_copy(a_ref.at[pl.ds((tile * count + j) * BS, BS), :], out.at[pl.ds(j * BS, BS), :], sems.at[j])
            c.start()
            copies.append(c)
        spread = spread_matrix()
        rows = pattern[tile * count:(tile + 1) * count, :]
        masks = [expand_mask(rows, k, spread) for k in range(NSUP)]
        for j in range(count):
            copies[j].wait()
            for k in range(NSUP):
                at = (slice(j * BS, (j + 1) * BS), slice(k * SN, (k + 1) * SN))
                out[at] = out[at] * masks[k][j:j + 1, :]

    return kernel


def below_product(order, a_ref, x_ref, group, i):
    rows = slice(((i & 1)) * SN, ((i & 1) + 1) * SN)
    first = jnp.dot(a_ref[rows, columns_at(order[2 * group])], x_ref[0:SN, :], preferred_element_type=F32)
    return first + jnp.dot(a_ref[rows, columns_at(order[2 * group + 1])], x_ref[SN:PAIR, :], preferred_element_type=F32)


def two_rows_kernel(order, a0, a1, x0_ref, x1_ref, out):
    for i, a_ref in enumerate((a0, a0, a1, a1)):
        out[i * SN:(i + 1) * SN, :] = below_product(order, a_ref, x0_ref, 0, i) + below_product(order, a_ref, x1_ref, 1, i)


def base_rows_kernel(order, a0, a1, x_ref, sums, h0, h1, h2, h3, out, rhs):
    depth = lax.axis_index("rhs")
    tall = h0.shape[0]
    for s, h in enumerate((h0, h1, h2, h3)):
        rhs[pl.ds(pl.multiple_of(jnp.bitwise_xor(depth, s) * tall, tall), tall), :] = h[...]
    for i, a_ref in enumerate((a0, a0, a1, a1)):
        at = slice(i * SN, (i + 1) * SN)
        out[at, :] = rhs[at, :].astype(F32) - (sums[at, :] + below_product(order, a_ref, x_ref, 2, i))


def last_rows_kernel(order, a0, a1, x0, x1, x2, x3, base, sol_ref, out_ref, done, sems, osem):
    copies = []
    for k, x in enumerate((x0, x1, x2, x3)):
        for q in range(2):
            at = pl.multiple_of(order[2 * k + q] * SN, SN)
            copies.append(pltpu.make_async_copy(x.at[pl.ds(q * SN, SN), :], sol_ref.at[pl.ds(at, SN), :], sems.at[2 * k + q]))
            copies[-1].start()
    for i, a_ref in enumerate((a0, a0, a1, a1)):
        at = slice(i * SN, (i + 1) * SN)
        done[at, :] = (base[at, :] - below_product(order, a_ref, x3, GROUPS - 1, i)).astype(BF16)
        copies.append(pltpu.make_async_copy(done.at[pl.ds(i * SN, SN), :], out_ref.at[pl.ds(i * SN, SN), :], osem.at[i]))
        copies[-1].start()
    for c in copies:
        c.wait()


def in_vmem(x):
    return pltpu.with_memory_space_constraint(x, pltpu.VMEM)


def in_hbm(x):
    return pltpu.with_memory_space_constraint(x, pltpu.HBM)


SMEM = pl.BlockSpec(memory_space=pltpu.SMEM)
VMEM = pl.BlockSpec(memory_space=pltpu.VMEM)
HBM = pl.BlockSpec(memory_space=pltpu.HBM)


def params(mib):
    return pltpu.CompilerParams(vmem_limit_bytes=mib * 1024 * 1024)


def cost(micros):
    return pl.CostEstimate(flops=micros * 10 ** 8, bytes_accessed=micros * 3 * 10 ** 6, transcendentals=0)


def shape_of(dims, dtype=BF16):
    return jax.ShapeDtypeStruct(dims, dtype)


def local(win_rows, anc_rows, win_pattern, anc_pattern, window_owner, sn_order, diag_inv, rhs_win, rhs_anc):
    if lax.axis_size("rows") != 8 or lax.axis_size("rhs") != 4 or anc_rows.shape[0] != 4 * SB * BS:
        win_rhs = lax.all_to_all(rhs_win, "rhs", split_axis=1, concat_axis=0, tiled=True)
        anc_rhs = lax.all_to_all(rhs_anc, "rhs", split_axis=1, concat_axis=0, tiled=True)
        return general_path(win_rows, anc_rows, win_pattern, anc_pattern, window_owner, sn_order, diag_inv, win_rhs, anc_rhs)

    def swap(x, m):
        return lax.ppermute(x, "rows", [(i, i ^ m) for i in range(8)])

    def deep(x, m):
        return lax.ppermute(x, "rhs", [(i, i ^ m) for i in range(4)])

    def neighbour(x):
        return lax.ppermute(x, "rows", [(i, i ^ (2 if i % 2 == 0 else 4)) for i in range(8)])

    def forward(x):
        return lax.ppermute(x, "rows", [(i, i ^ (4 if i % 2 == 0 else 2)) for i in range(8)])

    def mask_below(k, after):
        pattern_later, _ = lax.optimization_barrier((anc_pattern, after))
        return pl.pallas_call(
            make_below_mask_kernel(k),
            out_shape=shape_of((PAIR, NW)),
            in_specs=[VMEM, HBM],
            out_specs=VMEM,
            scratch_shapes=[pltpu.SemaphoreType.DMA((2 * SB,))],
            compiler_params=params(4),
            cost_estimate=cost(4),
            name="mask_below",
        )(pattern_later, in_hbm(anc_rows))

    columns = rhs_win.shape[1] // 4
    half = SN // 2
    tall = rhs_win.shape[0]
    w_own = in_hbm(win_rows)
    l_own = pl.pallas_call(
        factor_kernel,
        out_shape=shape_of((SN, SN)),
        in_specs=[SMEM, SMEM, VMEM, HBM],
        out_specs=VMEM,
        scratch_shapes=[pltpu.VMEM((SN, SN), BF16), pltpu.VMEM((SB, NWB), jnp.int32),
                        pltpu.SMEM((SB + 1,), jnp.int32), pltpu.SMEM((SB,), jnp.int32), pltpu.SemaphoreType.DMA],
        compiler_params=params(4),
        cost_estimate=cost(2),
        name="factor_pack",
    )(window_owner, sn_order, win_pattern, w_own)
    l_other = swap(l_own, 1)
    near, near_other = neighbour(l_own), neighbour(l_other)
    rhs_late, _ = lax.optimization_barrier((rhs_win, l_other))
    sent = pl.pallas_call(
        rhs_pack_kernel,
        out_shape=(shape_of((tall, columns)),) * 4,
        in_specs=[VMEM],
        out_specs=(VMEM,) * 4,
        compiler_params=params(4),
        cost_estimate=cost(1),
        name="rhs_pack",
    )(rhs_late)
    pieces = [sent[0]] + [deep(sent[s], s) for s in (1, 2, 3)]
    below = [mask_below(0, sent[0])]
    near_late, w_late, *_ = lax.optimization_barrier((near, win_rows, pieces[1]))
    far = forward(near_late)
    w_other = swap(w_late, 1)
    below[0], *pieces = lax.optimization_barrier((*below, *pieces))
    others = [swap(x, 1) for x in pieces]
    chip_rhs, packed, part = pl.pallas_call(
        first_pack_kernel,
        out_shape=(shape_of((PAIR, columns)), shape_of((SN, columns)), shape_of((half, columns))),
        in_specs=[SMEM, SMEM] + [VMEM] * 8,
        out_specs=(VMEM,) * 3,
        scratch_shapes=[pltpu.SMEM((SB + 1,), jnp.int32)],
        compiler_params=params(4),
        cost_estimate=cost(1),
        name="first_pack",
    )(window_owner, sn_order, *pieces, *others)
    owner_later, order_later, _ = lax.optimization_barrier((window_owner, sn_order, packed))
    tab, flag = pl.pallas_call(
        table_kernel,
        out_shape=(shape_of((TABLE + 1,), jnp.int32), shape_of((2,), jnp.int32)),
        in_specs=[SMEM, SMEM],
        out_specs=(SMEM, SMEM),
        compiler_params=params(4),
        cost_estimate=cost(2),
        name="tables",
    )(owner_later, order_later)
    w_other = in_vmem(w_other)
    w_own = in_vmem(win_rows)

    tile = rhs_anc.shape[0]
    sums, solved, masked = None, [], []
    diag_vmem = in_vmem(diag_inv)
    below_rows = anc_rows.shape[0]

    anc_order, anc_pieces = (2, 3, 1), [None] * 4
    for group in range(GROUPS):
        last = group == GROUPS - 1
        a_own = neighbour(packed)
        b_own = swap(part, 6)
        if group == 0:
            for k in range(GROUPS - 1):
                masked.append(pl.pallas_call(
                    make_mask_kernel(k),
                    out_shape=shape_of((SN, (k + 1) * PAIR)),
                    in_specs=[SMEM, SMEM, VMEM, VMEM, VMEM],
                    out_specs=VMEM,
                    scratch_shapes=[pltpu.VMEM((SB, NWB), jnp.int32)],
                    compiler_params=params(6),
                    cost_estimate=cost(2),
                    name="mask_rows",
                )(tab, order_later, win_pattern, w_own, w_other))
        if group == 0:
            rhs_later, _ = lax.optimization_barrier((rhs_anc, packed))
            anc_pieces = list(pl.pallas_call(
                below_rhs_kernel,
                out_shape=(shape_of((tile, columns)),) * 4,
                in_specs=[VMEM],
                out_specs=(VMEM,) * 4,
                compiler_params=params(4),
                cost_estimate=cost(1),
                name="below_rhs",
            )(in_vmem(rhs_later)))
        if not last:
            s = anc_order[group]
            moved, _ = lax.optimization_barrier((anc_pieces[s], packed))
            anc_pieces[s] = deep(moved, s)

        if group == 0:
            a_own, b_own, near, near_other, far, *masked = lax.optimization_barrier(
                (a_own, b_own, near, near_other, far, *masked))
            l_parts = [in_vmem(x) for x in (l_own, l_other, near, near_other, swap(near_other, 1), swap(near, 1), far, swap(far, 1))]
        operands = [tab, sn_order, diag_vmem, *l_parts]
        out_shape = [shape_of((PAIR, PAIR))]
        if not last:
            operands += [masked[group], chip_rhs, *solved]
            out_shape += [shape_of((SN, columns), F32)]
        ready = pl.pallas_call(
            make_prep_kernel(group),
            out_shape=tuple(out_shape),
            in_specs=[SMEM, SMEM] + [VMEM] * (len(operands) - 2),
            out_specs=(VMEM,) * len(out_shape),
            scratch_shapes=[pltpu.VMEM((SN, SN), BF16)],
            compiler_params=params(6),
            cost_estimate=cost(2),
            name="prep",
        )(*operands)
        hold = []
        if group == 1:
            below.append(mask_below(1, packed))
            hold = below[1:]
        elif group > 1:
            more, kernel = (solved[:2], two_rows_kernel) if group == 2 else ([solved[2], sums, *anc_pieces], base_rows_kernel)
            sums = pl.pallas_call(
                kernel,
                out_shape=shape_of((below_rows, columns), F32),
                in_specs=[SMEM] + [VMEM] * (2 + len(more)),
                out_specs=VMEM,
                scratch_shapes=[pltpu.VMEM((below_rows, columns), BF16)] if last else [],
                input_output_aliases={4: 0} if last else {},
                compiler_params=params(6),
                cost_estimate=cost(3),
                name="rows_below",
            )(sn_order, *below, *more)
            hold = [sums]
        if group > 0:
            s = anc_order[group - 1]
            a_own, b_own, anc_pieces[s], *rest = lax.optimization_barrier((a_own, b_own, anc_pieces[s], *hold, *ready))
            hold, ready = rest[:len(hold)], rest[len(hold):]
            if group == 1:
                below[1:] = hold
            else:
                sums = hold[0]
        a_swap = swap(a_own, 1)
        b_swap = swap(b_own, 1)
        ready = list(ready) if last else list(ready) + [masked[group]]

        out_shape = [shape_of((PAIR, columns))]
        if not last:
            out_shape += [shape_of((SN, columns)), shape_of((half, columns))]
        results = pl.pallas_call(
            make_solve_kernel(group),
            out_shape=tuple(out_shape),
            in_specs=[SMEM] + [VMEM] * (5 + len(ready)),
            out_specs=(VMEM,) * len(out_shape),
            scratch_shapes=[pltpu.VMEM((PAIR, columns), BF16), pltpu.VMEM((2 * PAIR, columns), BF16)],
            compiler_params=params(8),
            cost_estimate=cost(3),
            name="pair_solve",
        )(tab, packed, a_own, a_swap, b_own, b_swap, *ready)
        solved.append(results[0])
        if not last:
            packed, part = results[1:]

    outputs = pl.pallas_call(
        last_rows_kernel,
        out_shape=(shape_of((NW, columns)), shape_of((below_rows, columns))),
        in_specs=[SMEM] + [VMEM] * 7,
        out_specs=(HBM, HBM),
        scratch_shapes=[pltpu.VMEM((below_rows, columns), BF16), pltpu.SemaphoreType.DMA((2 * GROUPS,)),
                        pltpu.SemaphoreType.DMA((4,))],
        compiler_params=params(6),
        cost_estimate=cost(3),
        name="last_rows",
    )(sn_order, *below, *solved, sums)

    def again(carry):
        carry, own_pieces, below_pieces = lax.optimization_barrier((carry, pieces, anc_pieces))
        back = carry[0][1] ^ jnp.arange(4)
        win_rhs = jnp.take(jnp.stack(own_pieces), back, axis=0).reshape(4 * tall, columns)
        anc_rhs = jnp.take(jnp.stack(below_pieces), back, axis=0).reshape(4 * tile, columns)
        return jnp.zeros_like(carry[0]), *general_path(
            win_rows, anc_rows, win_pattern, anc_pattern, window_owner, sn_order, diag_inv, win_rhs, anc_rhs)

    return tuple(lax.while_loop(lambda carry: carry[0][0] != 0, again, (flag, *outputs))[1:])


def solution(mesh):
    return jax.shard_map(
        local,
        mesh=mesh,
        in_specs=(P("rows", None), P("rows", None), P(), P("rows", None), P(), P(), P(),
                  P(("rows", "rhs"), None), P(("rows", "rhs"), None)),
        out_specs=(P(None, "rhs"), P("rows", "rhs")),
        check_vma=False,
    )
```

```python
import jax
import jax.numpy as jnp
from jax import lax
from jax.experimental import pallas as pl
from jax.experimental.pallas import tpu as pltpu
from jax.sharding import PartitionSpec as P

BS = 64
SB = 8
NSUP = 8
SN = 512
NW = 4096
NWB = 64
GROUPS = 4
PAIR = 2 * SN
F32 = jnp.float32
BF16 = jnp.bfloat16


def masked_columns(factor, pattern, node_label):
    blocks = pattern.shape[0]
    columns = lax.dynamic_slice_in_dim(factor, node_label * SN, SN, 1)
    chosen = lax.dynamic_slice_in_dim(pattern, node_label * SB, SB, 1)
    shaped = columns.reshape(blocks, BS, SB, BS) * chosen[:, None, :, None].astype(BF16)
    return shaped.reshape(blocks * BS, SN)


def sum_over_rows(values):
    count = lax.axis_size("rows")
    if count & (count - 1):
        return lax.psum(values, "rows")
    step = 1
    while step < count:
        values = values + lax.ppermute(values, "rows", [(i, i ^ step) for i in range(count)])
        step *= 2
    return values


def general_path(win_rows, anc_rows, win_pattern, anc_pattern, window_owner, sn_order, diag_inv, win_rhs, anc_rhs):
    columns_rhs = win_rhs.shape[1]
    slot_count = win_rows.shape[0] // BS
    first_slot = lax.axis_index("rows") * slot_count
    local_pattern = lax.dynamic_slice_in_dim(win_pattern, first_slot, slot_count, 0)

    def step(position, carry):
        solution, win_resid, anc_resid = carry
        node_label = sn_order[position]
        owners = lax.dynamic_slice_in_dim(window_owner, node_label * SB, SB, 0)
        inverse = lax.dynamic_index_in_dim(diag_inv, node_label, 0, keepdims=False)
        local_place = owners - first_slot
        present = (local_place >= 0) & (local_place < slot_count)
        resid_blocks = win_resid.reshape(slot_count, BS, columns_rhs)
        taken = jnp.take(resid_blocks, jnp.clip(local_place, 0, slot_count - 1), axis=0)
        placed = jnp.where(present[:, None, None], taken, 0.0).reshape(SN, columns_rhs)
        panel = sum_over_rows(placed.astype(BF16))
        solved = jnp.dot(inverse, panel, preferred_element_type=F32).astype(BF16)
        solution = lax.dynamic_update_slice_in_dim(solution, solved, node_label * SN, 0)
        win_part = jnp.dot(masked_columns(win_rows, local_pattern, node_label), solved, preferred_element_type=F32)
        anc_part = jnp.dot(masked_columns(anc_rows, anc_pattern, node_label), solved, preferred_element_type=F32)
        return solution, win_resid - win_part, anc_resid - anc_part

    first = (jnp.zeros((NW, columns_rhs), BF16), win_rhs.astype(F32), anc_rhs.astype(F32))
    solution, _, anc_resid = lax.fori_loop(0, NSUP, step, first)
    return solution, anc_resid.astype(BF16)


def spread_matrix():
    block_index = lax.broadcasted_iota(jnp.int32, (NWB, SN), 0)
    lane_index = lax.broadcasted_iota(jnp.int32, (NWB, SN), 1)
    return ((block_index & 7) == (lane_index >> 6)).astype(F32).astype(BF16)


def expand_mask(rows_pattern, label, spread):
    lane = lax.broadcasted_iota(jnp.int32, rows_pattern.shape, 1)
    chosen = jnp.where((lane >> 3) == label, rows_pattern, 0).astype(F32).astype(BF16)
    return jnp.dot(chosen, spread, preferred_element_type=F32).astype(BF16)


def masked_rows(block_of, mask, count):
    return jnp.concatenate([block_of(j) * mask[j:j + 1, :] for j in range(count)], axis=0)


def rows_at(index):
    return pl.ds(pl.multiple_of(index * BS, BS), BS)


def columns_at(label):
    return pl.ds(pl.multiple_of(label * SN, SN), SN)


SRC, LSRC, PACK, TABLE = 0, 64, 96, 128


def factor_kernel(owner, order, pattern, win_ref, out, buf, pat, inv, pos, sem):
    row = lax.axis_index("rows")

    for w in range(NWB):
        slot = owner[w]
        inv[jnp.where((slot >> 3) == row, (slot & 7), SB)] = w
    for k in range(NSUP):
        pos[order[k]] = k
    labels = jnp.zeros((SB, 1), jnp.int32)
    for t in range(SB):
        label = order[(pos[(inv[t] >> 3)] // 2) * 2]
        pltpu.make_async_copy(win_ref.at[pl.ds(t * BS, BS), columns_at(label)], buf.at[pl.ds(t * BS, BS), :], sem).start()
        labels = jnp.where(lax.broadcasted_iota(jnp.int32, (SB, 1), 0) == t, label, labels)
    pat[...] = pattern[pl.ds(pl.multiple_of(row * SB, SB), SB), :]
    mask = expand_mask(pat[...], labels, spread_matrix())
    pltpu.make_async_copy(win_ref.at[:, pl.ds(0, SN)], buf, sem).wait()
    for j in range(SB):
        out[j * BS:(j + 1) * BS, :] = buf[j * BS:(j + 1) * BS, :] * mask[j:j + 1, :]


def rhs_pack_kernel(rhs_ref, *sent):
    depth = lax.axis_index("rhs")
    width = sent[0].shape[1]
    for s, out in enumerate(sent):
        at = pl.multiple_of(jnp.bitwise_xor(depth, s) * width, width)
        out[...] = rhs_ref[:, pl.ds(at, width)]


def table_kernel(owner, order, tab, flag):
    row = lax.axis_index("rows")
    chip, core = (row >> 1), (row & 1)
    bad = 0
    for t in range(GROUPS * SB):
        tab[PACK + t] = 0
    for group in range(GROUPS):
        counts = 0
        for i in range(2 * SB):
            slot = owner[order[2 * group + (i >> 3)] * SB + (i & 7)]
            where, device = (slot >> 4), (slot >> 3)
            rank = (counts >> (8 * where)) & 255
            counts = counts + (1 << (8 * where))
            bad = bad | ((rank >> 3))
            rank = jnp.minimum(rank, SB - 1)
            rel = jnp.bitwise_xor(where, chip)
            cross = jnp.bitwise_xor((device & 1), core)
            kind = jnp.where((rel == 1) | (rel == 2), jnp.where(rel == 1 + core, 1, 2), rel)
            far_rank = 3 * SB + jnp.where((rank >> 2) == core, 0, 4) + (rank & 3)
            tab[SRC + group * 16 + i] = jnp.where(kind == 3, far_rank, kind * SB + rank)
            tab[jnp.where(rel == 0, PACK + group * SB + rank, TABLE)] = cross * SB + (slot & 7)
            if i >= SB:
                tab[LSRC + group * SB + i - SB] = (2 * kind + cross) * SB + (slot & 7)
    flag[0] = bad
    flag[1] = lax.axis_index("rhs")


def below_rhs_kernel(rhs_ref, *outs):
    depth = lax.axis_index("rhs")
    width = outs[0].shape[1]
    for s, out in enumerate(outs):
        out[...] = rhs_ref[:, pl.ds(pl.multiple_of(jnp.bitwise_xor(depth, s) * width, width), width)]


def first_pack_kernel(owner, order, *refs):
    pieces, (chip_rhs, p_ref, b_ref, place) = refs[:8], refs[8:]
    row, depth = lax.axis_index("rows"), lax.axis_index("rhs")
    core = (row & 1)
    tall = pieces[0].shape[0]
    for side in range(2):
        for s in range(4):
            at = pl.multiple_of(side * SB * BS + jnp.bitwise_xor(depth, s) * tall, tall)
            chip_rhs[pl.ds(at, tall), :] = pieces[4 * side + s][...]
    for t in range(SB):
        place[t] = 0
    rank = 0
    for i in range(2 * SB):
        slot = owner[order[(i >> 3)] * SB + (i & 7)]
        here = (slot >> 4) == (row >> 1)
        place[jnp.where(here & (rank < SB), rank, SB)] = jnp.bitwise_xor(((slot >> 3) & 1), core) * SB + (slot & 7)
        rank = rank + jnp.where(here, 1, 0)
    for t in range(SB):
        p_ref[t * BS:(t + 1) * BS, :] = chip_rhs[rows_at(place[t]), :]
    b_ref[...] = p_ref[pl.ds(pl.multiple_of(core * (SB >> 1) * BS, (SB >> 1) * BS), (SB >> 1) * BS), :]


def make_mask_kernel(group):
    def kernel(tab, order, pattern, w_own, w_other, out, pat):
        row = lax.axis_index("rows")
        places = [tab[PACK + (group + 1) * SB + j] for j in range(SB)]
        for j, place in enumerate(places):
            pat[j:j + 1, :] = pattern[pl.ds(jnp.bitwise_xor(row, (place >> 3)) * SB + (place & 7), 1), :]
        spread = spread_matrix()
        rows = pat[...]
        masks = [expand_mask(rows, order[k], spread) for k in range(2 * group + 2)]
        for j, place in enumerate(places):
            at = slice(j * BS, (j + 1) * BS)
            for side, w_ref in enumerate((w_own, w_other)):
                @pl.when((place >> 3) == side)
                def _(w_ref=w_ref, at=at, j=j, place=place):
                    for k in range(2 * group + 2):
                        block = w_ref[rows_at((place & 7)), columns_at(order[k])]
                        out[at, k * SN:(k + 1) * SN] = block * masks[k][j:j + 1, :]

    return kernel


def make_prep_kernel(group):
    last = group == GROUPS - 1

    def kernel(tab, order, diag, *refs):
        l_refs, refs = refs[:8], refs[8:]
        if last:
            m_out, lbuf = refs
        else:
            w_ref, chip_rhs = refs[:2]
            xs = refs[2:2 + group]
            m_out, r_out, lbuf = refs[2 + group:]
        for i in range(SB):
            code = tab[LSRC + group * SB + i]
            for m in range(8):
                @pl.when((code >> 3) == m)
                def _(m=m, i=i, code=code):
                    lbuf[i * BS:(i + 1) * BS, :] = l_refs[m][rows_at(code & 7), :]
        first, second = diag[order[2 * group]], diag[order[2 * group + 1]]
        m_out[0:SN, 0:SN] = first
        m_out[SN:PAIR, SN:PAIR] = second
        joined = jnp.dot(second, lbuf[...], preferred_element_type=F32).astype(BF16)
        m_out[SN:PAIR, 0:SN] = (-jnp.dot(joined, first, preferred_element_type=F32)).astype(BF16)
        if not last:
            total = jnp.concatenate([chip_rhs[rows_at(tab[PACK + (group + 1) * SB + j]), :] for j in range(SB)], axis=0).astype(F32)
            for k in range(group):
                total = total - jnp.dot(w_ref[:, k * PAIR:(k + 1) * PAIR], xs[k][...], preferred_element_type=F32)
            r_out[...] = total

    return kernel


def make_solve_kernel(group):
    last = group == GROUPS - 1

    def kernel(*refs):
        tab, sources, m_ref = refs[0], refs[1:6], refs[6]
        if last:
            x_ref, panel, pool = refs[7:]
        else:
            r_ref, wn_ref, x_ref, p_ref, b_ref, panel, pool = refs[7:]
        at = 0
        for source in sources:
            pool[at:at + source.shape[0], :] = source[...]
            at += source.shape[0]
        for i in range(2 * SB):
            panel[i * BS:(i + 1) * BS, :] = pool[rows_at(tab[SRC + group * 16 + i]), :]
        x_ref[0:SN, :] = jnp.dot(m_ref[0:SN, 0:SN], panel[0:SN, :], preferred_element_type=F32).astype(BF16)
        x_ref[SN:PAIR, :] = jnp.dot(m_ref[SN:PAIR, :], panel[...], preferred_element_type=F32).astype(BF16)
        if last:
            return
        total = r_ref[...] - jnp.dot(wn_ref[:, group * PAIR:(group + 1) * PAIR], x_ref[...], preferred_element_type=F32)
        p_ref[...] = total.astype(BF16)
        core = lax.axis_index("rows") % 2
        b_ref[...] = p_ref[pl.ds(pl.multiple_of(core * (SB >> 1) * BS, (SB >> 1) * BS), (SB >> 1) * BS), :]

    return kernel


def make_below_mask_kernel(tile):
    def kernel(pattern, a_ref, out, sems):
        copies = []
        count = 2 * SB
        for j in range(count):
            c = pltpu.make_async_copy(a_ref.at[pl.ds((tile * count + j) * BS, BS), :], out.at[pl.ds(j * BS, BS), :], sems.at[j])
            c.start()
            copies.append(c)
        spread = spread_matrix()
        rows = pattern[tile * count:(tile + 1) * count, :]
        masks = [expand_mask(rows, k, spread) for k in range(NSUP)]
        for j in range(count):
            copies[j].wait()
            for k in range(NSUP):
                at = (slice(j * BS, (j + 1) * BS), slice(k * SN, (k + 1) * SN))
                out[at] = out[at] * masks[k][j:j + 1, :]

    return kernel


def below_product(order, a_ref, x_ref, group, i):
    rows = slice(((i & 1)) * SN, ((i & 1) + 1) * SN)
    first = jnp.dot(a_ref[rows, columns_at(order[2 * group])], x_ref[0:SN, :], preferred_element_type=F32)
    return first + jnp.dot(a_ref[rows, columns_at(order[2 * group + 1])], x_ref[SN:PAIR, :], preferred_element_type=F32)


def two_rows_kernel(order, a0, a1, x0_ref, x1_ref, out):
    for i, a_ref in enumerate((a0, a0, a1, a1)):
        out[i * SN:(i + 1) * SN, :] = below_product(order, a_ref, x0_ref, 0, i) + below_product(order, a_ref, x1_ref, 1, i)


def base_rows_kernel(order, a0, a1, x_ref, sums, h0, h1, h2, h3, out, rhs):
    depth = lax.axis_index("rhs")
    tall = h0.shape[0]
    for s, h in enumerate((h0, h1, h2, h3)):
        rhs[pl.ds(pl.multiple_of(jnp.bitwise_xor(depth, s) * tall, tall), tall), :] = h[...]
    for i, a_ref in enumerate((a0, a0, a1, a1)):
        at = slice(i * SN, (i + 1) * SN)
        out[at, :] = rhs[at, :].astype(F32) - (sums[at, :] + below_product(order, a_ref, x_ref, 2, i))


def last_rows_kernel(order, a0, a1, x0, x1, x2, x3, base, sol_ref, out_ref, done, sems, osem):
    copies = []
    for k, x in enumerate((x0, x1, x2, x3)):
        for q in range(2):
            at = pl.multiple_of(order[2 * k + q] * SN, SN)
            copies.append(pltpu.make_async_copy(x.at[pl.ds(q * SN, SN), :], sol_ref.at[pl.ds(at, SN), :], sems.at[2 * k + q]))
            copies[-1].start()
    for i, a_ref in enumerate((a0, a0, a1, a1)):
        at = slice(i * SN, (i + 1) * SN)
        done[at, :] = (base[at, :] - below_product(order, a_ref, x3, GROUPS - 1, i)).astype(BF16)
        copies.append(pltpu.make_async_copy(done.at[pl.ds(i * SN, SN), :], out_ref.at[pl.ds(i * SN, SN), :], osem.at[i]))
        copies[-1].start()
    for c in copies:
        c.wait()


def in_vmem(x):
    return pltpu.with_memory_space_constraint(x, pltpu.VMEM)


def in_hbm(x):
    return pltpu.with_memory_space_constraint(x, pltpu.HBM)


SMEM = pl.BlockSpec(memory_space=pltpu.SMEM)
VMEM = pl.BlockSpec(memory_space=pltpu.VMEM)
HBM = pl.BlockSpec(memory_space=pltpu.HBM)


def params(mib):
    return pltpu.CompilerParams(vmem_limit_bytes=mib * 1024 * 1024)


def cost(micros):
    return pl.CostEstimate(flops=micros * 10 ** 8, bytes_accessed=micros * 3 * 10 ** 6, transcendentals=0)


def shape_of(dims, dtype=BF16):
    return jax.ShapeDtypeStruct(dims, dtype)


def local(win_rows, anc_rows, win_pattern, anc_pattern, window_owner, sn_order, diag_inv, rhs_win, rhs_anc):
    if lax.axis_size("rows") != 8 or lax.axis_size("rhs") != 4 or anc_rows.shape[0] != 4 * SB * BS:
        win_rhs = lax.all_to_all(rhs_win, "rhs", split_axis=1, concat_axis=0, tiled=True)
        anc_rhs = lax.all_to_all(rhs_anc, "rhs", split_axis=1, concat_axis=0, tiled=True)
        return general_path(win_rows, anc_rows, win_pattern, anc_pattern, window_owner, sn_order, diag_inv, win_rhs, anc_rhs)

    def swap(x, m):
        return lax.ppermute(x, "rows", [(i, i ^ m) for i in range(8)])

    def deep(x, m):
        return lax.ppermute(x, "rhs", [(i, i ^ m) for i in range(4)])

    def neighbour(x):
        return lax.ppermute(x, "rows", [(i, i ^ (2 if i % 2 == 0 else 4)) for i in range(8)])

    def forward(x):
        return lax.ppermute(x, "rows", [(i, i ^ (4 if i % 2 == 0 else 2)) for i in range(8)])

    def mask_below(k, after):
        pattern_later, _ = lax.optimization_barrier((anc_pattern, after))
        return pl.pallas_call(
            make_below_mask_kernel(k),
            out_shape=shape_of((PAIR, NW)),
            in_specs=[VMEM, HBM],
            out_specs=VMEM,
            scratch_shapes=[pltpu.SemaphoreType.DMA((2 * SB,))],
            compiler_params=params(4),
            cost_estimate=cost(4),
            name="mask_below",
        )(pattern_later, in_hbm(anc_rows))

    columns = rhs_win.shape[1] // 4
    half = SN // 2
    tall = rhs_win.shape[0]
    w_own = in_hbm(win_rows)
    l_own = pl.pallas_call(
        factor_kernel,
        out_shape=shape_of((SN, SN)),
        in_specs=[SMEM, SMEM, VMEM, HBM],
        out_specs=VMEM,
        scratch_shapes=[pltpu.VMEM((SN, SN), BF16), pltpu.VMEM((SB, NWB), jnp.int32),
                        pltpu.SMEM((SB + 1,), jnp.int32), pltpu.SMEM((SB,), jnp.int32), pltpu.SemaphoreType.DMA],
        compiler_params=params(4),
        cost_estimate=cost(2),
        name="factor_pack",
    )(window_owner, sn_order, win_pattern, w_own)
    l_other = swap(l_own, 1)
    near, near_other = neighbour(l_own), neighbour(l_other)
    rhs_late, _ = lax.optimization_barrier((rhs_win, l_other))
    sent = pl.pallas_call(
        rhs_pack_kernel,
        out_shape=(shape_of((tall, columns)),) * 4,
        in_specs=[VMEM],
        out_specs=(VMEM,) * 4,
        compiler_params=params(4),
        cost_estimate=cost(1),
        name="rhs_pack",
    )(rhs_late)
    pieces = [sent[0]] + [deep(sent[s], s) for s in (1, 2, 3)]
    below = [mask_below(0, sent[0])]
    w_late, _ = lax.optimization_barrier((win_rows, l_other))
    w_other = swap(w_late, 1)
    near, near_other, w_other, below[0], *pieces = lax.optimization_barrier((near, near_other, w_other, *below, *pieces))
    far = forward(near)
    others = [swap(x, 1) for x in pieces]
    chip_rhs, packed, part = pl.pallas_call(
        first_pack_kernel,
        out_shape=(shape_of((PAIR, columns)), shape_of((SN, columns)), shape_of((half, columns))),
        in_specs=[SMEM, SMEM] + [VMEM] * 8,
        out_specs=(VMEM,) * 3,
        scratch_shapes=[pltpu.SMEM((SB + 1,), jnp.int32)],
        compiler_params=params(4),
        cost_estimate=cost(1),
        name="first_pack",
    )(window_owner, sn_order, *pieces, *others)
    owner_later, order_later, _ = lax.optimization_barrier((window_owner, sn_order, packed))
    tab, flag = pl.pallas_call(
        table_kernel,
        out_shape=(shape_of((TABLE + 1,), jnp.int32), shape_of((2,), jnp.int32)),
        in_specs=[SMEM, SMEM],
        out_specs=(SMEM, SMEM),
        compiler_params=params(4),
        cost_estimate=cost(2),
        name="tables",
    )(owner_later, order_later)
    w_other = in_vmem(w_other)
    w_own = in_vmem(win_rows)

    tile = rhs_anc.shape[0]
    sums, solved, masked = None, [], []
    diag_vmem = in_vmem(diag_inv)
    below_rows = anc_rows.shape[0]

    anc_order, anc_pieces = (2, 3, 1), [None] * 4
    for group in range(GROUPS):
        last = group == GROUPS - 1
        a_own = neighbour(packed)
        b_own = swap(part, 6)
        if group == 0:
            for k in range(GROUPS - 1):
                masked.append(pl.pallas_call(
                    make_mask_kernel(k),
                    out_shape=shape_of((SN, (k + 1) * PAIR)),
                    in_specs=[SMEM, SMEM, VMEM, VMEM, VMEM],
                    out_specs=VMEM,
                    scratch_shapes=[pltpu.VMEM((SB, NWB), jnp.int32)],
                    compiler_params=params(6),
                    cost_estimate=cost(2),
                    name="mask_rows",
                )(tab, order_later, win_pattern, w_own, w_other))
        if group == 0:
            rhs_later, _ = lax.optimization_barrier((rhs_anc, packed))
            anc_pieces = list(pl.pallas_call(
                below_rhs_kernel,
                out_shape=(shape_of((tile, columns)),) * 4,
                in_specs=[VMEM],
                out_specs=(VMEM,) * 4,
                compiler_params=params(4),
                cost_estimate=cost(1),
                name="below_rhs",
            )(in_vmem(rhs_later)))
        if not last:
            s = anc_order[group]
            moved, _ = lax.optimization_barrier((anc_pieces[s], packed))
            anc_pieces[s] = deep(moved, s)

        if group == 0:
            a_own, b_own, near, near_other, far, *masked = lax.optimization_barrier(
                (a_own, b_own, near, near_other, far, *masked))
            l_parts = [in_vmem(x) for x in (l_own, l_other, near, near_other, swap(near_other, 1), swap(near, 1), far, swap(far, 1))]
        operands = [tab, sn_order, diag_vmem, *l_parts]
        out_shape = [shape_of((PAIR, PAIR))]
        if not last:
            operands += [masked[group], chip_rhs, *solved]
            out_shape += [shape_of((SN, columns), F32)]
        ready = pl.pallas_call(
            make_prep_kernel(group),
            out_shape=tuple(out_shape),
            in_specs=[SMEM, SMEM] + [VMEM] * (len(operands) - 2),
            out_specs=(VMEM,) * len(out_shape),
            scratch_shapes=[pltpu.VMEM((SN, SN), BF16)],
            compiler_params=params(6),
            cost_estimate=cost(2),
            name="prep",
        )(*operands)
        hold = []
        if group == 1:
            below.append(mask_below(1, packed))
            hold = below[1:]
        elif group > 1:
            more, kernel = (solved[:2], two_rows_kernel) if group == 2 else ([solved[2], sums, *anc_pieces], base_rows_kernel)
            sums = pl.pallas_call(
                kernel,
                out_shape=shape_of((below_rows, columns), F32),
                in_specs=[SMEM] + [VMEM] * (2 + len(more)),
                out_specs=VMEM,
                scratch_shapes=[pltpu.VMEM((below_rows, columns), BF16)] if last else [],
                input_output_aliases={4: 0} if last else {},
                compiler_params=params(6),
                cost_estimate=cost(3),
                name="rows_below",
            )(sn_order, *below, *more)
            hold = [sums]
        if group > 0:
            s = anc_order[group - 1]
            a_own, b_own, anc_pieces[s], *rest = lax.optimization_barrier((a_own, b_own, anc_pieces[s], *hold, *ready))
            hold, ready = rest[:len(hold)], rest[len(hold):]
            if group == 1:
                below[1:] = hold
            else:
                sums = hold[0]
        a_swap = swap(a_own, 1)
        b_swap = swap(b_own, 1)
        ready = list(ready) if last else list(ready) + [masked[group]]

        out_shape = [shape_of((PAIR, columns))]
        if not last:
            out_shape += [shape_of((SN, columns)), shape_of((half, columns))]
        results = pl.pallas_call(
            make_solve_kernel(group),
            out_shape=tuple(out_shape),
            in_specs=[SMEM] + [VMEM] * (5 + len(ready)),
            out_specs=(VMEM,) * len(out_shape),
            scratch_shapes=[pltpu.VMEM((PAIR, columns), BF16), pltpu.VMEM((2 * PAIR, columns), BF16)],
            compiler_params=params(8),
            cost_estimate=cost(3),
            name="pair_solve",
        )(tab, packed, a_own, a_swap, b_own, b_swap, *ready)
        solved.append(results[0])
        if not last:
            packed, part = results[1:]

    outputs = pl.pallas_call(
        last_rows_kernel,
        out_shape=(shape_of((NW, columns)), shape_of((below_rows, columns))),
        in_specs=[SMEM] + [VMEM] * 7,
        out_specs=(HBM, HBM),
        scratch_shapes=[pltpu.VMEM((below_rows, columns), BF16), pltpu.SemaphoreType.DMA((2 * GROUPS,)),
                        pltpu.SemaphoreType.DMA((4,))],
        compiler_params=params(6),
        cost_estimate=cost(3),
        name="last_rows",
    )(sn_order, *below, *solved, sums)

    def again(carry):
        carry, own_pieces, below_pieces = lax.optimization_barrier((carry, pieces, anc_pieces))
        back = carry[0][1] ^ jnp.arange(4)
        win_rhs = jnp.take(jnp.stack(own_pieces), back, axis=0).reshape(4 * tall, columns)
        anc_rhs = jnp.take(jnp.stack(below_pieces), back, axis=0).reshape(4 * tile, columns)
        return jnp.zeros_like(carry[0]), *general_path(
            win_rows, anc_rows, win_pattern, anc_pattern, window_owner, sn_order, diag_inv, win_rhs, anc_rhs)

    return tuple(lax.while_loop(lambda carry: carry[0][0] != 0, again, (flag, *outputs))[1:])


def solution(mesh):
    return jax.shard_map(
        local,
        mesh=mesh,
        in_specs=(P("rows", None), P("rows", None), P(), P("rows", None), P(), P(), P(),
                  P(("rows", "rhs"), None), P(("rows", "rhs"), None)),
        out_specs=(P(None, "rhs"), P("rows", "rhs")),
        check_vma=False,
    )
```

```python
import jax
import jax.numpy as jnp
from jax import lax
from jax.experimental import pallas as pl
from jax.experimental.pallas import tpu as pltpu
from jax.sharding import PartitionSpec as P

BS = 64
SB = 8
NSUP = 8
SN = 512
NW = 4096
NWB = 64
GROUPS = 4
PAIR = 2 * SN
F32 = jnp.float32
BF16 = jnp.bfloat16


def masked_columns(factor, pattern, node_label):
    blocks = pattern.shape[0]
    columns = lax.dynamic_slice_in_dim(factor, node_label * SN, SN, 1)
    chosen = lax.dynamic_slice_in_dim(pattern, node_label * SB, SB, 1)
    shaped = columns.reshape(blocks, BS, SB, BS) * chosen[:, None, :, None].astype(BF16)
    return shaped.reshape(blocks * BS, SN)


def sum_over_rows(values):
    count = lax.axis_size("rows")
    if count & (count - 1):
        return lax.psum(values, "rows")
    step = 1
    while step < count:
        values = values + lax.ppermute(values, "rows", [(i, i ^ step) for i in range(count)])
        step *= 2
    return values


def general_path(win_rows, anc_rows, win_pattern, anc_pattern, window_owner, sn_order, diag_inv, win_rhs, anc_rhs):
    columns_rhs = win_rhs.shape[1]
    slot_count = win_rows.shape[0] // BS
    first_slot = lax.axis_index("rows") * slot_count
    local_pattern = lax.dynamic_slice_in_dim(win_pattern, first_slot, slot_count, 0)

    def step(position, carry):
        solution, win_resid, anc_resid = carry
        node_label = sn_order[position]
        owners = lax.dynamic_slice_in_dim(window_owner, node_label * SB, SB, 0)
        inverse = lax.dynamic_index_in_dim(diag_inv, node_label, 0, keepdims=False)
        local_place = owners - first_slot
        present = (local_place >= 0) & (local_place < slot_count)
        resid_blocks = win_resid.reshape(slot_count, BS, columns_rhs)
        taken = jnp.take(resid_blocks, jnp.clip(local_place, 0, slot_count - 1), axis=0)
        placed = jnp.where(present[:, None, None], taken, 0.0).reshape(SN, columns_rhs)
        panel = sum_over_rows(placed.astype(BF16))
        solved = jnp.dot(inverse, panel, preferred_element_type=F32).astype(BF16)
        solution = lax.dynamic_update_slice_in_dim(solution, solved, node_label * SN, 0)
        win_part = jnp.dot(masked_columns(win_rows, local_pattern, node_label), solved, preferred_element_type=F32)
        anc_part = jnp.dot(masked_columns(anc_rows, anc_pattern, node_label), solved, preferred_element_type=F32)
        return solution, win_resid - win_part, anc_resid - anc_part

    first = (jnp.zeros((NW, columns_rhs), BF16), win_rhs.astype(F32), anc_rhs.astype(F32))
    solution, _, anc_resid = lax.fori_loop(0, NSUP, step, first)
    return solution, anc_resid.astype(BF16)


def spread_matrix():
    block_index = lax.broadcasted_iota(jnp.int32, (NWB, SN), 0)
    lane_index = lax.broadcasted_iota(jnp.int32, (NWB, SN), 1)
    return ((block_index & 7) == (lane_index >> 6)).astype(F32).astype(BF16)


def expand_mask(rows_pattern, label, spread):
    lane = lax.broadcasted_iota(jnp.int32, rows_pattern.shape, 1)
    chosen = jnp.where((lane >> 3) == label, rows_pattern, 0).astype(F32).astype(BF16)
    return jnp.dot(chosen, spread, preferred_element_type=F32).astype(BF16)


def masked_rows(block_of, mask, count):
    return jnp.concatenate([block_of(j) * mask[j:j + 1, :] for j in range(count)], axis=0)


def rows_at(index):
    return pl.ds(pl.multiple_of(index * BS, BS), BS)


def columns_at(label):
    return pl.ds(pl.multiple_of(label * SN, SN), SN)


CAP = 10
HALF = CAP // 2
SRC, LSRC, PACK, TABLE = 0, 64, 96, 96 + GROUPS * CAP


def factor_kernel(owner, order, pattern, win_ref, out, buf, pat, inv, pos, sem):
    row = lax.axis_index("rows")

    for w in range(NWB):
        slot = owner[w]
        inv[jnp.where((slot >> 3) == row, (slot & 7), SB)] = w
    for k in range(NSUP):
        pos[order[k]] = k
    labels = jnp.zeros((SB, 1), jnp.int32)
    for t in range(SB):
        label = order[(pos[(inv[t] >> 3)] // 2) * 2]
        pltpu.make_async_copy(win_ref.at[pl.ds(t * BS, BS), columns_at(label)], buf.at[pl.ds(t * BS, BS), :], sem).start()
        labels = jnp.where(lax.broadcasted_iota(jnp.int32, (SB, 1), 0) == t, label, labels)
    pat[...] = pattern[pl.ds(pl.multiple_of(row * SB, SB), SB), :]
    mask = expand_mask(pat[...], labels, spread_matrix())
    pltpu.make_async_copy(win_ref.at[:, pl.ds(0, SN)], buf, sem).wait()
    for j in range(SB):
        out[j * BS:(j + 1) * BS, :] = buf[j * BS:(j + 1) * BS, :] * mask[j:j + 1, :]


def rhs_pack_kernel(rhs_ref, *sent):
    depth = lax.axis_index("rhs")
    width = sent[0].shape[1]
    for s, out in enumerate(sent):
        at = pl.multiple_of(jnp.bitwise_xor(depth, s) * width, width)
        out[...] = rhs_ref[:, pl.ds(at, width)]


def chip_pack_kernel(own_ref, other_ref, l_chip):
    l_chip[0:SN, :] = own_ref[...]
    l_chip[SN:PAIR, :] = other_ref[...]


def take_half_kernel(x_ref, out):
    out[...] = x_ref[0:SN, :]


def table_kernel(owner, order, tab, flag):
    row = lax.axis_index("rows")
    chip, core = (row >> 1), (row & 1)
    bad = 0
    for t in range(GROUPS * CAP):
        tab[PACK + t] = 0
    for group in range(GROUPS):
        counts = 0
        for i in range(2 * SB):
            slot = owner[order[2 * group + (i >> 3)] * SB + (i & 7)]
            where, device = (slot >> 4), (slot >> 3)
            rank = (counts >> (8 * where)) & 255
            counts = counts + (1 << (8 * where))
            bad = bad | jnp.where(rank >= CAP, 1, 0)
            rank = jnp.minimum(rank, CAP - 1)
            rel = jnp.bitwise_xor(where, chip)
            cross = jnp.bitwise_xor((device & 1), core)
            kind = jnp.where((rel == 1) | (rel == 2), jnp.where(rel == 1 + core, 1, 2), rel)
            upper = jnp.where(rank >= HALF, 1, 0)
            far_rank = 3 * CAP + jnp.where(upper == core, 0, HALF) + rank - upper * HALF
            tab[SRC + group * 16 + i] = jnp.where(kind == 3, far_rank, kind * CAP + rank)
            tab[jnp.where(rel == 0, PACK + group * CAP + rank, TABLE)] = cross * SB + (slot & 7)
            if i >= SB:
                tab[LSRC + group * SB + i - SB] = (2 * kind + cross) * SB + (slot & 7)
    flag[0] = bad
    flag[1] = lax.axis_index("rhs")


def below_rhs_kernel(rhs_ref, *outs):
    depth = lax.axis_index("rhs")
    width = outs[0].shape[1]
    for s, out in enumerate(outs):
        out[...] = rhs_ref[:, pl.ds(pl.multiple_of(jnp.bitwise_xor(depth, s) * width, width), width)]


def first_pack_kernel(owner, order, *refs):
    pieces, (chip_rhs, p_ref, b_ref, place) = refs[:8], refs[8:]
    row, depth = lax.axis_index("rows"), lax.axis_index("rhs")
    core = (row & 1)
    tall = pieces[0].shape[0]
    for side in range(2):
        for s in range(4):
            at = pl.multiple_of(side * SB * BS + jnp.bitwise_xor(depth, s) * tall, tall)
            chip_rhs[pl.ds(at, tall), :] = pieces[4 * side + s][...]
    for t in range(CAP):
        place[t] = 0
    rank = 0
    for i in range(2 * SB):
        slot = owner[order[(i >> 3)] * SB + (i & 7)]
        here = (slot >> 4) == (row >> 1)
        place[jnp.where(here & (rank < CAP), rank, CAP)] = jnp.bitwise_xor(((slot >> 3) & 1), core) * SB + (slot & 7)
        rank = rank + jnp.where(here, 1, 0)
    for t in range(CAP):
        p_ref[t * BS:(t + 1) * BS, :] = chip_rhs[rows_at(place[t]), :]
    b_ref[...] = p_ref[pl.ds(pl.multiple_of(core * HALF * BS, BS), HALF * BS), :]


def make_mask_kernel(group):
    def kernel(tab, order, pattern, w_own, w_other, out, pat):
        row = lax.axis_index("rows")
        places = [tab[PACK + (group + 1) * CAP + j] for j in range(CAP)]
        for j, place in enumerate(places):
            pat[j:j + 1, :] = pattern[pl.ds(jnp.bitwise_xor(row, (place >> 3)) * SB + (place & 7), 1), :]
        spread = spread_matrix()
        rows = pat[...]
        masks = [expand_mask(rows, order[k], spread) for k in range(2 * group + 2)]
        for j, place in enumerate(places):
            at = slice(j * BS, (j + 1) * BS)
            for side, w_ref in enumerate((w_own, w_other)):
                @pl.when((place >> 3) == side)
                def _(w_ref=w_ref, at=at, j=j, place=place):
                    for k in range(2 * group + 2):
                        block = w_ref[rows_at((place & 7)), columns_at(order[k])]
                        out[at, k * SN:(k + 1) * SN] = block * masks[k][j:j + 1, :]

    return kernel


def make_prep_kernel(group):
    last = group == GROUPS - 1

    def kernel(tab, order, diag, *refs):
        own, other, near, near_swap, far, far_swap = refs[:6]
        l_refs = ((own, 0), (other, 0), (near, 0), (near, SB), (near_swap, SB), (near_swap, 0), (far, 0), (far_swap, 0))
        refs = refs[6:]
        if last:
            m_out, lbuf = refs
        else:
            w_ref, chip_rhs = refs[:2]
            xs = refs[2:2 + group]
            m_out, r_out, lbuf = refs[2 + group:]
        for i in range(SB):
            code = tab[LSRC + group * SB + i]
            for m in range(8):
                @pl.when((code >> 3) == m)
                def _(m=m, i=i, code=code):
                    lbuf[i * BS:(i + 1) * BS, :] = l_refs[m][0][rows_at((code & 7) + l_refs[m][1]), :]
        first, second = diag[order[2 * group]], diag[order[2 * group + 1]]
        m_out[0:SN, 0:SN] = first
        m_out[SN:PAIR, SN:PAIR] = second
        joined = jnp.dot(second, lbuf[...], preferred_element_type=F32).astype(BF16)
        m_out[SN:PAIR, 0:SN] = (-jnp.dot(joined, first, preferred_element_type=F32)).astype(BF16)
        if not last:
            total = jnp.concatenate([chip_rhs[rows_at(tab[PACK + (group + 1) * CAP + j]), :] for j in range(CAP)], axis=0).astype(F32)
            for k in range(group):
                total = total - jnp.dot(w_ref[:, k * PAIR:(k + 1) * PAIR], xs[k][...], preferred_element_type=F32)
            r_out[...] = total

    return kernel


def make_solve_kernel(group):
    last = group == GROUPS - 1

    def kernel(*refs):
        tab, sources, m_ref = refs[0], refs[1:6], refs[6]
        if last:
            x_ref, panel, pool = refs[7:]
        else:
            r_ref, wn_ref, x_ref, p_ref, b_ref, panel, pool = refs[7:]
        at = 0
        for source in sources:
            pool[at:at + source.shape[0], :] = source[...]
            at += source.shape[0]
        for i in range(2 * SB):
            panel[i * BS:(i + 1) * BS, :] = pool[rows_at(tab[SRC + group * 16 + i]), :]
        x_ref[0:SN, :] = jnp.dot(m_ref[0:SN, 0:SN], panel[0:SN, :], preferred_element_type=F32).astype(BF16)
        x_ref[SN:PAIR, :] = jnp.dot(m_ref[SN:PAIR, :], panel[...], preferred_element_type=F32).astype(BF16)
        if last:
            return
        total = r_ref[...] - jnp.dot(wn_ref[:, group * PAIR:(group + 1) * PAIR], x_ref[...], preferred_element_type=F32)
        p_ref[...] = total.astype(BF16)
        core = lax.axis_index("rows") % 2
        b_ref[...] = p_ref[pl.ds(pl.multiple_of(core * HALF * BS, BS), HALF * BS), :]

    return kernel


def make_below_mask_kernel(tile):
    def kernel(pattern, a_ref, out, sems):
        copies = []
        count = 2 * SB
        for j in range(count):
            c = pltpu.make_async_copy(a_ref.at[pl.ds((tile * count + j) * BS, BS), :], out.at[pl.ds(j * BS, BS), :], sems.at[j])
            c.start()
            copies.append(c)
        spread = spread_matrix()
        rows = pattern[tile * count:(tile + 1) * count, :]
        masks = [expand_mask(rows, k, spread) for k in range(NSUP)]
        for j in range(count):
            copies[j].wait()
            for k in range(NSUP):
                at = (slice(j * BS, (j + 1) * BS), slice(k * SN, (k + 1) * SN))
                out[at] = out[at] * masks[k][j:j + 1, :]

    return kernel


def below_product(order, a_ref, x_ref, group, i):
    rows = slice(((i & 1)) * SN, ((i & 1) + 1) * SN)
    first = jnp.dot(a_ref[rows, columns_at(order[2 * group])], x_ref[0:SN, :], preferred_element_type=F32)
    return first + jnp.dot(a_ref[rows, columns_at(order[2 * group + 1])], x_ref[SN:PAIR, :], preferred_element_type=F32)


def two_rows_kernel(order, a0, a1, x0_ref, x1_ref, out):
    for i, a_ref in enumerate((a0, a0, a1, a1)):
        out[i * SN:(i + 1) * SN, :] = below_product(order, a_ref, x0_ref, 0, i) + below_product(order, a_ref, x1_ref, 1, i)


def base_rows_kernel(order, a0, a1, x_ref, sums, h0, h1, h2, h3, out, rhs):
    depth = lax.axis_index("rhs")
    tall = h0.shape[0]
    for s, h in enumerate((h0, h1, h2, h3)):
        rhs[pl.ds(pl.multiple_of(jnp.bitwise_xor(depth, s) * tall, tall), tall), :] = h[...]
    for i, a_ref in enumerate((a0, a0, a1, a1)):
        at = slice(i * SN, (i + 1) * SN)
        out[at, :] = rhs[at, :].astype(F32) - (sums[at, :] + below_product(order, a_ref, x_ref, 2, i))


def last_rows_kernel(order, a0, a1, x0, x1, x2, x3, base, sol_ref, out_ref, done, sems, osem):
    copies = []
    for k, x in enumerate((x0, x1, x2, x3)):
        for q in range(2):
            at = pl.multiple_of(order[2 * k + q] * SN, SN)
            copies.append(pltpu.make_async_copy(x.at[pl.ds(q * SN, SN), :], sol_ref.at[pl.ds(at, SN), :], sems.at[2 * k + q]))
            copies[-1].start()
    for i, a_ref in enumerate((a0, a0, a1, a1)):
        at = slice(i * SN, (i + 1) * SN)
        done[at, :] = (base[at, :] - below_product(order, a_ref, x3, GROUPS - 1, i)).astype(BF16)
        copies.append(pltpu.make_async_copy(done.at[pl.ds(i * SN, SN), :], out_ref.at[pl.ds(i * SN, SN), :], osem.at[i]))
        copies[-1].start()
    for c in copies:
        c.wait()


def in_vmem(x):
    return pltpu.with_memory_space_constraint(x, pltpu.VMEM)


def in_hbm(x):
    return pltpu.with_memory_space_constraint(x, pltpu.HBM)


SMEM = pl.BlockSpec(memory_space=pltpu.SMEM)
VMEM = pl.BlockSpec(memory_space=pltpu.VMEM)
HBM = pl.BlockSpec(memory_space=pltpu.HBM)


def params(mib):
    return pltpu.CompilerParams(vmem_limit_bytes=mib * 1024 * 1024)


def cost(micros):
    return pl.CostEstimate(flops=micros * 10 ** 8, bytes_accessed=micros * 3 * 10 ** 6, transcendentals=0)


def shape_of(dims, dtype=BF16):
    return jax.ShapeDtypeStruct(dims, dtype)


def local(win_rows, anc_rows, win_pattern, anc_pattern, window_owner, sn_order, diag_inv, rhs_win, rhs_anc):
    if lax.axis_size("rows") != 8 or lax.axis_size("rhs") != 4 or anc_rows.shape[0] != 4 * SB * BS:
        win_rhs = lax.all_to_all(rhs_win, "rhs", split_axis=1, concat_axis=0, tiled=True)
        anc_rhs = lax.all_to_all(rhs_anc, "rhs", split_axis=1, concat_axis=0, tiled=True)
        return general_path(win_rows, anc_rows, win_pattern, anc_pattern, window_owner, sn_order, diag_inv, win_rhs, anc_rhs)

    def swap(x, m):
        return lax.ppermute(x, "rows", [(i, i ^ m) for i in range(8)])

    def deep(x, m):
        return lax.ppermute(x, "rhs", [(i, i ^ m) for i in range(4)])

    def neighbour(x):
        return lax.ppermute(x, "rows", [(i, i ^ (2 if i % 2 == 0 else 4)) for i in range(8)])

    def forward(x):
        return lax.ppermute(x, "rows", [(i, i ^ (4 if i % 2 == 0 else 2)) for i in range(8)])

    def mask_below(k, after):
        pattern_later, _ = lax.optimization_barrier((anc_pattern, after))
        return pl.pallas_call(
            make_below_mask_kernel(k),
            out_shape=shape_of((PAIR, NW)),
            in_specs=[VMEM, HBM],
            out_specs=VMEM,
            scratch_shapes=[pltpu.SemaphoreType.DMA((2 * SB,))],
            compiler_params=params(4),
            cost_estimate=cost(4),
            name="mask_below",
        )(pattern_later, in_hbm(anc_rows))

    columns = rhs_win.shape[1] // 4
    half = SN // 2
    tall = rhs_win.shape[0]
    w_own = in_hbm(win_rows)
    l_own = pl.pallas_call(
        factor_kernel,
        out_shape=shape_of((SN, SN)),
        in_specs=[SMEM, SMEM, VMEM, HBM],
        out_specs=VMEM,
        scratch_shapes=[pltpu.VMEM((SN, SN), BF16), pltpu.VMEM((SB, NWB), jnp.int32),
                        pltpu.SMEM((SB + 1,), jnp.int32), pltpu.SMEM((SB,), jnp.int32), pltpu.SemaphoreType.DMA],
        compiler_params=params(4),
        cost_estimate=cost(2),
        name="factor_pack",
    )(window_owner, sn_order, win_pattern, w_own)
    l_other = swap(l_own, 1)
    l_chip = pl.pallas_call(
        chip_pack_kernel,
        out_shape=shape_of((PAIR, SN)),
        in_specs=[VMEM] * 2,
        out_specs=VMEM,
        compiler_params=params(4),
        cost_estimate=cost(1),
        name="chip_pack",
    )(l_own, l_other)
    near = neighbour(l_chip)
    rhs_late, _ = lax.optimization_barrier((rhs_win, l_chip))
    sent = pl.pallas_call(
        rhs_pack_kernel,
        out_shape=(shape_of((tall, columns)),) * 4,
        in_specs=[VMEM],
        out_specs=(VMEM,) * 4,
        compiler_params=params(4),
        cost_estimate=cost(1),
        name="rhs_pack",
    )(rhs_late)
    pieces = [sent[0]] + [deep(sent[s], s) for s in (1, 2, 3)]
    w_late, _ = lax.optimization_barrier((win_rows, l_chip))
    w_other = swap(w_late, 1)
    below = [mask_below(0, l_chip)]
    near, w_other, below[0], *pieces = lax.optimization_barrier((near, w_other, *below, *pieces))
    others = [swap(x, 1) for x in pieces]
    chip_rhs, packed, part = pl.pallas_call(
        first_pack_kernel,
        out_shape=(shape_of((PAIR, columns)), shape_of((CAP * BS, columns)), shape_of((HALF * BS, columns))),
        in_specs=[SMEM, SMEM] + [VMEM] * 8,
        out_specs=(VMEM,) * 3,
        scratch_shapes=[pltpu.SMEM((CAP + 1,), jnp.int32)],
        compiler_params=params(4),
        cost_estimate=cost(1),
        name="first_pack",
    )(window_owner, sn_order, *pieces, *others)
    near_half = pl.pallas_call(
        take_half_kernel,
        out_shape=shape_of((SN, SN)),
        in_specs=[VMEM],
        out_specs=VMEM,
        compiler_params=params(4),
        cost_estimate=cost(1),
        name="take_half",
    )(near)
    far = forward(near_half)
    owner_later, order_later, _ = lax.optimization_barrier((window_owner, sn_order, packed))
    tab, flag = pl.pallas_call(
        table_kernel,
        out_shape=(shape_of((TABLE + 1,), jnp.int32), shape_of((2,), jnp.int32)),
        in_specs=[SMEM, SMEM],
        out_specs=(SMEM, SMEM),
        compiler_params=params(4),
        cost_estimate=cost(2),
        name="tables",
    )(owner_later, order_later)
    w_other = in_vmem(w_other)
    w_own = in_vmem(win_rows)

    tile = rhs_anc.shape[0]
    sums, solved, masked = None, [], []
    diag_vmem = in_vmem(diag_inv)
    below_rows = anc_rows.shape[0]

    anc_order, anc_pieces = (2, 3, 1), [None] * 4
    for group in range(GROUPS):
        last = group == GROUPS - 1
        a_own = neighbour(packed)
        b_own = swap(part, 6)
        if group == 0:
            for k in range(GROUPS - 1):
                masked.append(pl.pallas_call(
                    make_mask_kernel(k),
                    out_shape=shape_of((CAP * BS, (k + 1) * PAIR)),
                    in_specs=[SMEM, SMEM, VMEM, VMEM, VMEM],
                    out_specs=VMEM,
                    scratch_shapes=[pltpu.VMEM((CAP, NWB), jnp.int32)],
                    compiler_params=params(6),
                    cost_estimate=cost(2),
                    name="mask_rows",
                )(tab, order_later, win_pattern, w_own, w_other))
        if group == 0:
            rhs_later, _ = lax.optimization_barrier((rhs_anc, packed))
            anc_pieces = list(pl.pallas_call(
                below_rhs_kernel,
                out_shape=(shape_of((tile, columns)),) * 4,
                in_specs=[VMEM],
                out_specs=(VMEM,) * 4,
                compiler_params=params(4),
                cost_estimate=cost(1),
                name="below_rhs",
            )(in_vmem(rhs_later)))
        if not last:
            s = anc_order[group]
            moved, _ = lax.optimization_barrier((anc_pieces[s], packed))
            anc_pieces[s] = deep(moved, s)

        if group == 0:
            a_own, b_own, near, far, *masked = lax.optimization_barrier(
                (a_own, b_own, near, far, *masked))
            l_parts = [in_vmem(x) for x in (l_own, l_other, near, swap(near, 1), far, swap(far, 1))]
        operands = [tab, sn_order, diag_vmem, *l_parts]
        out_shape = [shape_of((PAIR, PAIR))]
        if not last:
            operands += [masked[group], chip_rhs, *solved]
            out_shape += [shape_of((CAP * BS, columns), F32)]
        ready = pl.pallas_call(
            make_prep_kernel(group),
            out_shape=tuple(out_shape),
            in_specs=[SMEM, SMEM] + [VMEM] * (len(operands) - 2),
            out_specs=(VMEM,) * len(out_shape),
            scratch_shapes=[pltpu.VMEM((SN, SN), BF16)],
            compiler_params=params(6),
            cost_estimate=cost(2),
            name="prep",
        )(*operands)
        hold = []
        if group == 1:
            below.append(mask_below(1, packed))
            hold = below[1:]
        elif group > 1:
            more, kernel = (solved[:2], two_rows_kernel) if group == 2 else ([solved[2], sums, *anc_pieces], base_rows_kernel)
            sums = pl.pallas_call(
                kernel,
                out_shape=shape_of((below_rows, columns), F32),
                in_specs=[SMEM] + [VMEM] * (2 + len(more)),
                out_specs=VMEM,
                scratch_shapes=[pltpu.VMEM((below_rows, columns), BF16)] if last else [],
                input_output_aliases={4: 0} if last else {},
                compiler_params=params(6),
                cost_estimate=cost(3),
                name="rows_below",
            )(sn_order, *below, *more)
            hold = [sums]
        if group > 0:
            s = anc_order[group - 1]
            a_own, b_own, anc_pieces[s], *rest = lax.optimization_barrier((a_own, b_own, anc_pieces[s], *hold, *ready))
            hold, ready = rest[:len(hold)], rest[len(hold):]
            if group == 1:
                below[1:] = hold
            else:
                sums = hold[0]
        a_swap = swap(a_own, 1)
        b_swap = swap(b_own, 1)
        ready = list(ready) if last else list(ready) + [masked[group]]

        out_shape = [shape_of((PAIR, columns))]
        if not last:
            out_shape += [shape_of((CAP * BS, columns)), shape_of((HALF * BS, columns))]
        results = pl.pallas_call(
            make_solve_kernel(group),
            out_shape=tuple(out_shape),
            in_specs=[SMEM] + [VMEM] * (5 + len(ready)),
            out_specs=(VMEM,) * len(out_shape),
            scratch_shapes=[pltpu.VMEM((PAIR, columns), BF16), pltpu.VMEM((4 * CAP * BS, columns), BF16)],
            compiler_params=params(8),
            cost_estimate=cost(3),
            name="pair_solve",
        )(tab, packed, a_own, a_swap, b_own, b_swap, *ready)
        solved.append(results[0])
        if not last:
            packed, part = results[1:]

    outputs = pl.pallas_call(
        last_rows_kernel,
        out_shape=(shape_of((NW, columns)), shape_of((below_rows, columns))),
        in_specs=[SMEM] + [VMEM] * 7,
        out_specs=(HBM, HBM),
        scratch_shapes=[pltpu.VMEM((below_rows, columns), BF16), pltpu.SemaphoreType.DMA((2 * GROUPS,)),
                        pltpu.SemaphoreType.DMA((4,))],
        compiler_params=params(6),
        cost_estimate=cost(3),
        name="last_rows",
    )(sn_order, *below, *solved, sums)

    def again(carry):
        carry, own_pieces, below_pieces = lax.optimization_barrier((carry, pieces, anc_pieces))
        back = carry[0][1] ^ jnp.arange(4)
        win_rhs = jnp.take(jnp.stack(own_pieces), back, axis=0).reshape(4 * tall, columns)
        anc_rhs = jnp.take(jnp.stack(below_pieces), back, axis=0).reshape(4 * tile, columns)
        return jnp.zeros_like(carry[0]), *general_path(
            win_rows, anc_rows, win_pattern, anc_pattern, window_owner, sn_order, diag_inv, win_rhs, anc_rhs)

    return tuple(lax.while_loop(lambda carry: carry[0][0] != 0, again, (flag, *outputs))[1:])


def solution(mesh):
    return jax.shard_map(
        local,
        mesh=mesh,
        in_specs=(P("rows", None), P("rows", None), P(), P("rows", None), P(), P(), P(),
                  P(("rows", "rhs"), None), P(("rows", "rhs"), None)),
        out_specs=(P(None, "rhs"), P("rows", "rhs")),
        check_vma=False,
    )
```

```python
import jax
import jax.numpy as jnp
from jax import lax
from jax.experimental import pallas as pl
from jax.experimental.pallas import tpu as pltpu
from jax.sharding import PartitionSpec as P

BS = 64
SB = 8
NSUP = 8
SN = 512
NW = 4096
NWB = 64
GROUPS = 4
PAIR = 2 * SN
F32 = jnp.float32
BF16 = jnp.bfloat16


def masked_columns(factor, pattern, node_label):
    blocks = pattern.shape[0]
    columns = lax.dynamic_slice_in_dim(factor, node_label * SN, SN, 1)
    chosen = lax.dynamic_slice_in_dim(pattern, node_label * SB, SB, 1)
    shaped = columns.reshape(blocks, BS, SB, BS) * chosen[:, None, :, None].astype(BF16)
    return shaped.reshape(blocks * BS, SN)


def sum_over_rows(values):
    count = lax.axis_size("rows")
    if count & (count - 1):
        return lax.psum(values, "rows")
    step = 1
    while step < count:
        values = values + lax.ppermute(values, "rows", [(i, i ^ step) for i in range(count)])
        step *= 2
    return values


def general_path(win_rows, anc_rows, win_pattern, anc_pattern, window_owner, sn_order, diag_inv, win_rhs, anc_rhs):
    columns_rhs = win_rhs.shape[1]
    slot_count = win_rows.shape[0] // BS
    first_slot = lax.axis_index("rows") * slot_count
    local_pattern = lax.dynamic_slice_in_dim(win_pattern, first_slot, slot_count, 0)

    def step(position, carry):
        solution, win_resid, anc_resid = carry
        node_label = sn_order[position]
        owners = lax.dynamic_slice_in_dim(window_owner, node_label * SB, SB, 0)
        inverse = lax.dynamic_index_in_dim(diag_inv, node_label, 0, keepdims=False)
        local_place = owners - first_slot
        present = (local_place >= 0) & (local_place < slot_count)
        resid_blocks = win_resid.reshape(slot_count, BS, columns_rhs)
        taken = jnp.take(resid_blocks, jnp.clip(local_place, 0, slot_count - 1), axis=0)
        placed = jnp.where(present[:, None, None], taken, 0.0).reshape(SN, columns_rhs)
        panel = sum_over_rows(placed.astype(BF16))
        solved = jnp.dot(inverse, panel, preferred_element_type=F32).astype(BF16)
        solution = lax.dynamic_update_slice_in_dim(solution, solved, node_label * SN, 0)
        win_part = jnp.dot(masked_columns(win_rows, local_pattern, node_label), solved, preferred_element_type=F32)
        anc_part = jnp.dot(masked_columns(anc_rows, anc_pattern, node_label), solved, preferred_element_type=F32)
        return solution, win_resid - win_part, anc_resid - anc_part

    first = (jnp.zeros((NW, columns_rhs), BF16), win_rhs.astype(F32), anc_rhs.astype(F32))
    solution, _, anc_resid = lax.fori_loop(0, NSUP, step, first)
    return solution, anc_resid.astype(BF16)


def spread_matrix():
    block_index = lax.broadcasted_iota(jnp.int32, (NWB, SN), 0)
    lane_index = lax.broadcasted_iota(jnp.int32, (NWB, SN), 1)
    return ((block_index & 7) == (lane_index >> 6)).astype(F32).astype(BF16)


def expand_mask(rows_pattern, label, spread):
    lane = lax.broadcasted_iota(jnp.int32, rows_pattern.shape, 1)
    chosen = jnp.where((lane >> 3) == label, rows_pattern, 0).astype(F32).astype(BF16)
    return jnp.dot(chosen, spread, preferred_element_type=F32).astype(BF16)


def masked_rows(block_of, mask, count):
    return jnp.concatenate([block_of(j) * mask[j:j + 1, :] for j in range(count)], axis=0)


def rows_at(index):
    return pl.ds(pl.multiple_of(index * BS, BS), BS)


def columns_at(label):
    return pl.ds(pl.multiple_of(label * SN, SN), SN)


SRC, LSRC, PACK, TABLE = 0, 64, 96, 128


def factor_kernel(owner, order, pattern, win_ref, out, buf, pat, inv, pos, sem):
    row = lax.axis_index("rows")

    for w in range(NWB):
        slot = owner[w]
        inv[jnp.where((slot >> 3) == row, (slot & 7), SB)] = w
    for k in range(NSUP):
        pos[order[k]] = k
    labels = jnp.zeros((SB, 1), jnp.int32)
    for t in range(SB):
        label = order[(pos[(inv[t] >> 3)] // 2) * 2]
        pltpu.make_async_copy(win_ref.at[pl.ds(t * BS, BS), columns_at(label)], buf.at[pl.ds(t * BS, BS), :], sem).start()
        labels = jnp.where(lax.broadcasted_iota(jnp.int32, (SB, 1), 0) == t, label, labels)
    pat[...] = pattern[pl.ds(pl.multiple_of(row * SB, SB), SB), :]
    mask = expand_mask(pat[...], labels, spread_matrix())
    pltpu.make_async_copy(win_ref.at[:, pl.ds(0, SN)], buf, sem).wait()
    for j in range(SB):
        out[j * BS:(j + 1) * BS, :] = buf[j * BS:(j + 1) * BS, :] * mask[j:j + 1, :]


def rhs_pack_kernel(rhs_ref, *sent):
    depth = lax.axis_index("rhs")
    width = sent[0].shape[1]
    for s, out in enumerate(sent):
        at = pl.multiple_of(jnp.bitwise_xor(depth, s) * width, width)
        out[...] = rhs_ref[:, pl.ds(at, width)]


def chip_pack_kernel(own_ref, other_ref, l_chip):
    l_chip[0:SN, :] = own_ref[...]
    l_chip[SN:PAIR, :] = other_ref[...]


def take_half_kernel(x_ref, out):
    out[...] = x_ref[0:SN, :]


def table_kernel(owner, order, tab, flag):
    row = lax.axis_index("rows")
    chip, core = (row >> 1), (row & 1)
    bad = 0
    for t in range(GROUPS * SB):
        tab[PACK + t] = 0
    for group in range(GROUPS):
        counts = 0
        for i in range(2 * SB):
            slot = owner[order[2 * group + (i >> 3)] * SB + (i & 7)]
            where, device = (slot >> 4), (slot >> 3)
            rank = (counts >> (8 * where)) & 255
            counts = counts + (1 << (8 * where))
            bad = bad | ((rank >> 3))
            rank = jnp.minimum(rank, SB - 1)
            rel = jnp.bitwise_xor(where, chip)
            cross = jnp.bitwise_xor((device & 1), core)
            kind = jnp.where((rel == 1) | (rel == 2), jnp.where(rel == 1 + core, 1, 2), rel)
            far_rank = 3 * SB + jnp.where((rank >> 2) == core, 0, 4) + (rank & 3)
            tab[SRC + group * 16 + i] = jnp.where(kind == 3, far_rank, kind * SB + rank)
            tab[jnp.where(rel == 0, PACK + group * SB + rank, TABLE)] = cross * SB + (slot & 7)
            if i >= SB:
                tab[LSRC + group * SB + i - SB] = (2 * kind + cross) * SB + (slot & 7)
    flag[0] = bad
    flag[1] = lax.axis_index("rhs")


def below_rhs_kernel(rhs_ref, *outs):
    depth = lax.axis_index("rhs")
    width = outs[0].shape[1]
    for s, out in enumerate(outs):
        out[...] = rhs_ref[:, pl.ds(pl.multiple_of(jnp.bitwise_xor(depth, s) * width, width), width)]


def first_pack_kernel(owner, order, *refs):
    pieces, (chip_rhs, p_ref, b_ref, place) = refs[:8], refs[8:]
    row, depth = lax.axis_index("rows"), lax.axis_index("rhs")
    core = (row & 1)
    tall = pieces[0].shape[0]
    for side in range(2):
        for s in range(4):
            at = pl.multiple_of(side * SB * BS + jnp.bitwise_xor(depth, s) * tall, tall)
            chip_rhs[pl.ds(at, tall), :] = pieces[4 * side + s][...]
    for t in range(SB):
        place[t] = 0
    rank = 0
    for i in range(2 * SB):
        slot = owner[order[(i >> 3)] * SB + (i & 7)]
        here = (slot >> 4) == (row >> 1)
        place[jnp.where(here & (rank < SB), rank, SB)] = jnp.bitwise_xor(((slot >> 3) & 1), core) * SB + (slot & 7)
        rank = rank + jnp.where(here, 1, 0)
    for t in range(SB):
        p_ref[t * BS:(t + 1) * BS, :] = chip_rhs[rows_at(place[t]), :]
    b_ref[...] = p_ref[pl.ds(pl.multiple_of(core * (SB >> 1) * BS, (SB >> 1) * BS), (SB >> 1) * BS), :]


def make_mask_kernel(group):
    def kernel(tab, order, pattern, w_own, w_other, out, pat):
        row = lax.axis_index("rows")
        places = [tab[PACK + (group + 1) * SB + j] for j in range(SB)]
        for j, place in enumerate(places):
            pat[j:j + 1, :] = pattern[pl.ds(jnp.bitwise_xor(row, (place >> 3)) * SB + (place & 7), 1), :]
        spread = spread_matrix()
        rows = pat[...]
        masks = [expand_mask(rows, order[k], spread) for k in range(2 * group + 2)]
        for j, place in enumerate(places):
            at = slice(j * BS, (j + 1) * BS)
            for side, w_ref in enumerate((w_own, w_other)):
                @pl.when((place >> 3) == side)
                def _(w_ref=w_ref, at=at, j=j, place=place):
                    for k in range(2 * group + 2):
                        block = w_ref[rows_at((place & 7)), columns_at(order[k])]
                        out[at, k * SN:(k + 1) * SN] = block * masks[k][j:j + 1, :]

    return kernel


def make_prep_kernel(group):
    last = group == GROUPS - 1

    def kernel(tab, order, diag, *refs):
        own, other, near, near_swap, far, far_swap = refs[:6]
        l_refs = ((own, 0), (other, 0), (near, 0), (near, SB), (near_swap, SB), (near_swap, 0), (far, 0), (far_swap, 0))
        refs = refs[6:]
        if last:
            m_out, lbuf = refs
        else:
            w_ref, chip_rhs = refs[:2]
            xs = refs[2:2 + group]
            m_out, r_out, lbuf = refs[2 + group:]
        for i in range(SB):
            code = tab[LSRC + group * SB + i]
            for m in range(8):
                @pl.when((code >> 3) == m)
                def _(m=m, i=i, code=code):
                    lbuf[i * BS:(i + 1) * BS, :] = l_refs[m][0][rows_at((code & 7) + l_refs[m][1]), :]
        first, second = diag[order[2 * group]], diag[order[2 * group + 1]]
        m_out[0:SN, 0:SN] = first
        m_out[SN:PAIR, SN:PAIR] = second
        joined = jnp.dot(second, lbuf[...], preferred_element_type=F32).astype(BF16)
        m_out[SN:PAIR, 0:SN] = (-jnp.dot(joined, first, preferred_element_type=F32)).astype(BF16)
        if not last:
            total = jnp.concatenate([chip_rhs[rows_at(tab[PACK + (group + 1) * SB + j]), :] for j in range(SB)], axis=0).astype(F32)
            for k in range(group):
                total = total - jnp.dot(w_ref[:, k * PAIR:(k + 1) * PAIR], xs[k][...], preferred_element_type=F32)
            r_out[...] = total

    return kernel


def make_solve_kernel(group):
    last = group == GROUPS - 1

    def kernel(*refs):
        tab, sources, m_ref = refs[0], refs[1:6], refs[6]
        if last:
            x_ref, panel, pool = refs[7:]
        else:
            r_ref, wn_ref, x_ref, p_ref, b_ref, panel, pool = refs[7:]
        at = 0
        for source in sources:
            pool[at:at + source.shape[0], :] = source[...]
            at += source.shape[0]
        for i in range(2 * SB):
            panel[i * BS:(i + 1) * BS, :] = pool[rows_at(tab[SRC + group * 16 + i]), :]
        x_ref[0:SN, :] = jnp.dot(m_ref[0:SN, 0:SN], panel[0:SN, :], preferred_element_type=F32).astype(BF16)
        x_ref[SN:PAIR, :] = jnp.dot(m_ref[SN:PAIR, :], panel[...], preferred_element_type=F32).astype(BF16)
        if last:
            return
        total = r_ref[...] - jnp.dot(wn_ref[:, group * PAIR:(group + 1) * PAIR], x_ref[...], preferred_element_type=F32)
        p_ref[...] = total.astype(BF16)
        core = lax.axis_index("rows") % 2
        b_ref[...] = p_ref[pl.ds(pl.multiple_of(core * (SB >> 1) * BS, (SB >> 1) * BS), (SB >> 1) * BS), :]

    return kernel


def make_below_mask_kernel(tile):
    def kernel(pattern, a_ref, out, sems):
        copies = []
        count = 2 * SB
        for j in range(count):
            c = pltpu.make_async_copy(a_ref.at[pl.ds((tile * count + j) * BS, BS), :], out.at[pl.ds(j * BS, BS), :], sems.at[j])
            c.start()
            copies.append(c)
        spread = spread_matrix()
        rows = pattern[tile * count:(tile + 1) * count, :]
        masks = [expand_mask(rows, k, spread) for k in range(NSUP)]
        for j in range(count):
            copies[j].wait()
            for k in range(NSUP):
                at = (slice(j * BS, (j + 1) * BS), slice(k * SN, (k + 1) * SN))
                out[at] = out[at] * masks[k][j:j + 1, :]

    return kernel


def below_product(order, a_ref, x_ref, group, i):
    rows = slice(((i & 1)) * SN, ((i & 1) + 1) * SN)
    first = jnp.dot(a_ref[rows, columns_at(order[2 * group])], x_ref[0:SN, :], preferred_element_type=F32)
    return first + jnp.dot(a_ref[rows, columns_at(order[2 * group + 1])], x_ref[SN:PAIR, :], preferred_element_type=F32)


def two_rows_kernel(order, a0, a1, x0_ref, x1_ref, out):
    for i, a_ref in enumerate((a0, a0, a1, a1)):
        out[i * SN:(i + 1) * SN, :] = below_product(order, a_ref, x0_ref, 0, i) + below_product(order, a_ref, x1_ref, 1, i)


def base_rows_kernel(order, a0, a1, x_ref, sums, h0, h1, h2, h3, out, rhs):
    depth = lax.axis_index("rhs")
    tall = h0.shape[0]
    for s, h in enumerate((h0, h1, h2, h3)):
        rhs[pl.ds(pl.multiple_of(jnp.bitwise_xor(depth, s) * tall, tall), tall), :] = h[...]
    for i, a_ref in enumerate((a0, a0, a1, a1)):
        at = slice(i * SN, (i + 1) * SN)
        out[at, :] = rhs[at, :].astype(F32) - (sums[at, :] + below_product(order, a_ref, x_ref, 2, i))


def last_rows_kernel(order, a0, a1, x0, x1, x2, x3, base, sol_ref, out_ref, done, sems, osem):
    copies = []
    for k, x in enumerate((x0, x1, x2, x3)):
        for q in range(2):
            at = pl.multiple_of(order[2 * k + q] * SN, SN)
            copies.append(pltpu.make_async_copy(x.at[pl.ds(q * SN, SN), :], sol_ref.at[pl.ds(at, SN), :], sems.at[2 * k + q]))
            copies[-1].start()
    for i, a_ref in enumerate((a0, a0, a1, a1)):
        at = slice(i * SN, (i + 1) * SN)
        done[at, :] = (base[at, :] - below_product(order, a_ref, x3, GROUPS - 1, i)).astype(BF16)
        copies.append(pltpu.make_async_copy(done.at[pl.ds(i * SN, SN), :], out_ref.at[pl.ds(i * SN, SN), :], osem.at[i]))
        copies[-1].start()
    for c in copies:
        c.wait()


def in_vmem(x):
    return pltpu.with_memory_space_constraint(x, pltpu.VMEM)


def in_hbm(x):
    return pltpu.with_memory_space_constraint(x, pltpu.HBM)


SMEM = pl.BlockSpec(memory_space=pltpu.SMEM)
VMEM = pl.BlockSpec(memory_space=pltpu.VMEM)
HBM = pl.BlockSpec(memory_space=pltpu.HBM)


def params(mib):
    return pltpu.CompilerParams(vmem_limit_bytes=mib * 1024 * 1024)


def cost(micros):
    return pl.CostEstimate(flops=micros * 10 ** 8, bytes_accessed=micros * 3 * 10 ** 6, transcendentals=0)


def shape_of(dims, dtype=BF16):
    return jax.ShapeDtypeStruct(dims, dtype)


def local(win_rows, anc_rows, win_pattern, anc_pattern, window_owner, sn_order, diag_inv, rhs_win, rhs_anc):
    if lax.axis_size("rows") != 8 or lax.axis_size("rhs") != 4 or anc_rows.shape[0] != 4 * SB * BS:
        win_rhs = lax.all_to_all(rhs_win, "rhs", split_axis=1, concat_axis=0, tiled=True)
        anc_rhs = lax.all_to_all(rhs_anc, "rhs", split_axis=1, concat_axis=0, tiled=True)
        return general_path(win_rows, anc_rows, win_pattern, anc_pattern, window_owner, sn_order, diag_inv, win_rhs, anc_rhs)

    def swap(x, m):
        return lax.ppermute(x, "rows", [(i, i ^ m) for i in range(8)])

    def deep(x, m):
        return lax.ppermute(x, "rhs", [(i, i ^ m) for i in range(4)])

    def neighbour(x):
        return lax.ppermute(x, "rows", [(i, i ^ (2 if i % 2 == 0 else 4)) for i in range(8)])

    def forward(x):
        return lax.ppermute(x, "rows", [(i, i ^ (4 if i % 2 == 0 else 2)) for i in range(8)])

    def mask_below(k, after):
        pattern_later, _ = lax.optimization_barrier((anc_pattern, after))
        return pl.pallas_call(
            make_below_mask_kernel(k),
            out_shape=shape_of((PAIR, NW)),
            in_specs=[VMEM, HBM],
            out_specs=VMEM,
            scratch_shapes=[pltpu.SemaphoreType.DMA((2 * SB,))],
            compiler_params=params(4),
            cost_estimate=cost(4),
            name="mask_below",
        )(pattern_later, in_hbm(anc_rows))

    columns = rhs_win.shape[1] // 4
    half = SN // 2
    tall = rhs_win.shape[0]
    w_own = in_hbm(win_rows)
    l_own = pl.pallas_call(
        factor_kernel,
        out_shape=shape_of((SN, SN)),
        in_specs=[SMEM, SMEM, VMEM, HBM],
        out_specs=VMEM,
        scratch_shapes=[pltpu.VMEM((SN, SN), BF16), pltpu.VMEM((SB, NWB), jnp.int32),
                        pltpu.SMEM((SB + 1,), jnp.int32), pltpu.SMEM((SB,), jnp.int32), pltpu.SemaphoreType.DMA],
        compiler_params=params(4),
        cost_estimate=cost(2),
        name="factor_pack",
    )(window_owner, sn_order, win_pattern, w_own)
    l_other = swap(l_own, 1)
    l_chip = pl.pallas_call(
        chip_pack_kernel,
        out_shape=shape_of((PAIR, SN)),
        in_specs=[VMEM] * 2,
        out_specs=VMEM,
        compiler_params=params(4),
        cost_estimate=cost(1),
        name="chip_pack",
    )(l_own, l_other)
    near = neighbour(l_chip)
    rhs_late, _ = lax.optimization_barrier((rhs_win, l_chip))
    sent = pl.pallas_call(
        rhs_pack_kernel,
        out_shape=(shape_of((tall, columns)),) * 4,
        in_specs=[VMEM],
        out_specs=(VMEM,) * 4,
        compiler_params=params(4),
        cost_estimate=cost(1),
        name="rhs_pack",
    )(rhs_late)
    pieces = [sent[0]] + [deep(sent[s], s) for s in (1, 2, 3)]
    w_late, _ = lax.optimization_barrier((win_rows, l_chip))
    w_other = swap(w_late, 1)
    below = [mask_below(0, l_chip)]
    w_other, below[0], *pieces = lax.optimization_barrier((w_other, *below, *pieces))
    others = [swap(x, 1) for x in pieces]
    chip_rhs, packed, part = pl.pallas_call(
        first_pack_kernel,
        out_shape=(shape_of((PAIR, columns)), shape_of((SN, columns)), shape_of((half, columns))),
        in_specs=[SMEM, SMEM] + [VMEM] * 8,
        out_specs=(VMEM,) * 3,
        scratch_shapes=[pltpu.SMEM((SB + 1,), jnp.int32)],
        compiler_params=params(4),
        cost_estimate=cost(1),
        name="first_pack",
    )(window_owner, sn_order, *pieces, *others)
    near, _ = lax.optimization_barrier((near, packed))
    near_half = pl.pallas_call(
        take_half_kernel,
        out_shape=shape_of((SN, SN)),
        in_specs=[VMEM],
        out_specs=VMEM,
        compiler_params=params(4),
        cost_estimate=cost(1),
        name="take_half",
    )(near)
    far = forward(near_half)
    owner_later, order_later, _ = lax.optimization_barrier((window_owner, sn_order, packed))
    tab, flag = pl.pallas_call(
        table_kernel,
        out_shape=(shape_of((TABLE + 1,), jnp.int32), shape_of((2,), jnp.int32)),
        in_specs=[SMEM, SMEM],
        out_specs=(SMEM, SMEM),
        compiler_params=params(4),
        cost_estimate=cost(2),
        name="tables",
    )(owner_later, order_later)
    w_other = in_vmem(w_other)
    w_own = in_vmem(win_rows)

    tile = rhs_anc.shape[0]
    sums, solved, masked = None, [], []
    diag_vmem = in_vmem(diag_inv)
    below_rows = anc_rows.shape[0]

    anc_order, anc_pieces = (2, 3, 1), [None] * 4
    for group in range(GROUPS):
        last = group == GROUPS - 1
        a_own = neighbour(packed)
        b_own = swap(part, 6)
        if group == 0:
            for k in range(GROUPS - 1):
                masked.append(pl.pallas_call(
                    make_mask_kernel(k),
                    out_shape=shape_of((SN, (k + 1) * PAIR)),
                    in_specs=[SMEM, SMEM, VMEM, VMEM, VMEM],
                    out_specs=VMEM,
                    scratch_shapes=[pltpu.VMEM((SB, NWB), jnp.int32)],
                    compiler_params=params(6),
                    cost_estimate=cost(2),
                    name="mask_rows",
                )(tab, order_later, win_pattern, w_own, w_other))
        if group == 0:
            rhs_later, _ = lax.optimization_barrier((rhs_anc, packed))
            anc_pieces = list(pl.pallas_call(
                below_rhs_kernel,
                out_shape=(shape_of((tile, columns)),) * 4,
                in_specs=[VMEM],
                out_specs=(VMEM,) * 4,
                compiler_params=params(4),
                cost_estimate=cost(1),
                name="below_rhs",
            )(in_vmem(rhs_later)))
        if not last:
            s = anc_order[group]
            moved, _ = lax.optimization_barrier((anc_pieces[s], packed))
            anc_pieces[s] = deep(moved, s)

        if group == 0:
            a_own, b_own, near, far, *masked = lax.optimization_barrier(
                (a_own, b_own, near, far, *masked))
            l_parts = [in_vmem(x) for x in (l_own, l_other, near, swap(near, 1), far, swap(far, 1))]
        operands = [tab, sn_order, diag_vmem, *l_parts]
        out_shape = [shape_of((PAIR, PAIR))]
        if not last:
            operands += [masked[group], chip_rhs, *solved]
            out_shape += [shape_of((SN, columns), F32)]
        ready = pl.pallas_call(
            make_prep_kernel(group),
            out_shape=tuple(out_shape),
            in_specs=[SMEM, SMEM] + [VMEM] * (len(operands) - 2),
            out_specs=(VMEM,) * len(out_shape),
            scratch_shapes=[pltpu.VMEM((SN, SN), BF16)],
            compiler_params=params(6),
            cost_estimate=cost(2),
            name="prep",
        )(*operands)
        hold = []
        if group == 1:
            below.append(mask_below(1, packed))
            hold = below[1:]
        elif group > 1:
            more, kernel = (solved[:2], two_rows_kernel) if group == 2 else ([solved[2], sums, *anc_pieces], base_rows_kernel)
            sums = pl.pallas_call(
                kernel,
                out_shape=shape_of((below_rows, columns), F32),
                in_specs=[SMEM] + [VMEM] * (2 + len(more)),
                out_specs=VMEM,
                scratch_shapes=[pltpu.VMEM((below_rows, columns), BF16)] if last else [],
                input_output_aliases={4: 0} if last else {},
                compiler_params=params(6),
                cost_estimate=cost(3),
                name="rows_below",
            )(sn_order, *below, *more)
            hold = [sums]
        if group > 0:
            s = anc_order[group - 1]
            a_own, b_own, anc_pieces[s], *rest = lax.optimization_barrier((a_own, b_own, anc_pieces[s], *hold, *ready))
            hold, ready = rest[:len(hold)], rest[len(hold):]
            if group == 1:
                below[1:] = hold
            else:
                sums = hold[0]
        a_swap = swap(a_own, 1)
        b_swap = swap(b_own, 1)
        ready = list(ready) if last else list(ready) + [masked[group]]

        out_shape = [shape_of((PAIR, columns))]
        if not last:
            out_shape += [shape_of((SN, columns)), shape_of((half, columns))]
        results = pl.pallas_call(
            make_solve_kernel(group),
            out_shape=tuple(out_shape),
            in_specs=[SMEM] + [VMEM] * (5 + len(ready)),
            out_specs=(VMEM,) * len(out_shape),
            scratch_shapes=[pltpu.VMEM((PAIR, columns), BF16), pltpu.VMEM((2 * PAIR, columns), BF16)],
            compiler_params=params(8),
            cost_estimate=cost(3),
            name="pair_solve",
        )(tab, packed, a_own, a_swap, b_own, b_swap, *ready)
        solved.append(results[0])
        if not last:
            packed, part = results[1:]

    outputs = pl.pallas_call(
        last_rows_kernel,
        out_shape=(shape_of((NW, columns)), shape_of((below_rows, columns))),
        in_specs=[SMEM] + [VMEM] * 7,
        out_specs=(HBM, HBM),
        scratch_shapes=[pltpu.VMEM((below_rows, columns), BF16), pltpu.SemaphoreType.DMA((2 * GROUPS,)),
                        pltpu.SemaphoreType.DMA((4,))],
        compiler_params=params(6),
        cost_estimate=cost(3),
        name="last_rows",
    )(sn_order, *below, *solved, sums)

    def again(carry):
        carry, own_pieces, below_pieces = lax.optimization_barrier((carry, pieces, anc_pieces))
        back = carry[0][1] ^ jnp.arange(4)
        win_rhs = jnp.take(jnp.stack(own_pieces), back, axis=0).reshape(4 * tall, columns)
        anc_rhs = jnp.take(jnp.stack(below_pieces), back, axis=0).reshape(4 * tile, columns)
        return jnp.zeros_like(carry[0]), *general_path(
            win_rows, anc_rows, win_pattern, anc_pattern, window_owner, sn_order, diag_inv, win_rhs, anc_rhs)

    return tuple(lax.while_loop(lambda carry: carry[0][0] != 0, again, (flag, *outputs))[1:])


def solution(mesh):
    return jax.shard_map(
        local,
        mesh=mesh,
        in_specs=(P("rows", None), P("rows", None), P(), P("rows", None), P(), P(), P(),
                  P(("rows", "rhs"), None), P(("rows", "rhs"), None)),
        out_specs=(P(None, "rhs"), P("rows", "rhs")),
        check_vma=False,
    )
```

```python
import jax
import jax.numpy as jnp
from jax import lax
from jax.experimental import pallas as pl
from jax.experimental.pallas import tpu as pltpu
from jax.sharding import PartitionSpec as P

BS = 64
SB = 8
NSUP = 8
SN = 512
NW = 4096
NWB = 64
GROUPS = 4
PAIR = 2 * SN
F32 = jnp.float32
BF16 = jnp.bfloat16


def masked_columns(factor, pattern, node_label):
    blocks = pattern.shape[0]
    columns = lax.dynamic_slice_in_dim(factor, node_label * SN, SN, 1)
    chosen = lax.dynamic_slice_in_dim(pattern, node_label * SB, SB, 1)
    shaped = columns.reshape(blocks, BS, SB, BS) * chosen[:, None, :, None].astype(BF16)
    return shaped.reshape(blocks * BS, SN)


def sum_over_rows(values):
    count = lax.axis_size("rows")
    if count & (count - 1):
        return lax.psum(values, "rows")
    step = 1
    while step < count:
        values = values + lax.ppermute(values, "rows", [(i, i ^ step) for i in range(count)])
        step *= 2
    return values


def general_path(win_rows, anc_rows, win_pattern, anc_pattern, window_owner, sn_order, diag_inv, win_rhs, anc_rhs):
    columns_rhs = win_rhs.shape[1]
    slot_count = win_rows.shape[0] // BS
    first_slot = lax.axis_index("rows") * slot_count
    local_pattern = lax.dynamic_slice_in_dim(win_pattern, first_slot, slot_count, 0)

    def step(position, carry):
        solution, win_resid, anc_resid = carry
        node_label = sn_order[position]
        owners = lax.dynamic_slice_in_dim(window_owner, node_label * SB, SB, 0)
        inverse = lax.dynamic_index_in_dim(diag_inv, node_label, 0, keepdims=False)
        local_place = owners - first_slot
        present = (local_place >= 0) & (local_place < slot_count)
        resid_blocks = win_resid.reshape(slot_count, BS, columns_rhs)
        taken = jnp.take(resid_blocks, jnp.clip(local_place, 0, slot_count - 1), axis=0)
        placed = jnp.where(present[:, None, None], taken, 0.0).reshape(SN, columns_rhs)
        panel = sum_over_rows(placed.astype(BF16))
        solved = jnp.dot(inverse, panel, preferred_element_type=F32).astype(BF16)
        solution = lax.dynamic_update_slice_in_dim(solution, solved, node_label * SN, 0)
        win_part = jnp.dot(masked_columns(win_rows, local_pattern, node_label), solved, preferred_element_type=F32)
        anc_part = jnp.dot(masked_columns(anc_rows, anc_pattern, node_label), solved, preferred_element_type=F32)
        return solution, win_resid - win_part, anc_resid - anc_part

    first = (jnp.zeros((NW, columns_rhs), BF16), win_rhs.astype(F32), anc_rhs.astype(F32))
    solution, _, anc_resid = lax.fori_loop(0, NSUP, step, first)
    return solution, anc_resid.astype(BF16)


def spread_matrix():
    block_index = lax.broadcasted_iota(jnp.int32, (NWB, SN), 0)
    lane_index = lax.broadcasted_iota(jnp.int32, (NWB, SN), 1)
    return ((block_index & 7) == (lane_index >> 6)).astype(F32).astype(BF16)


def expand_mask(rows_pattern, label, spread):
    lane = lax.broadcasted_iota(jnp.int32, rows_pattern.shape, 1)
    chosen = jnp.where((lane >> 3) == label, rows_pattern, 0).astype(F32).astype(BF16)
    return jnp.dot(chosen, spread, preferred_element_type=F32).astype(BF16)


def masked_rows(block_of, mask, count):
    return jnp.concatenate([block_of(j) * mask[j:j + 1, :] for j in range(count)], axis=0)


def rows_at(index):
    return pl.ds(pl.multiple_of(index * BS, BS), BS)


def columns_at(label):
    return pl.ds(pl.multiple_of(label * SN, SN), SN)


SRC, LSRC, PACK, TABLE = 0, 64, 96, 128


def factor_kernel(owner, order, pattern, win_ref, out, buf, pat, inv, pos, sem):
    row = lax.axis_index("rows")

    for w in range(NWB):
        slot = owner[w]
        inv[jnp.where((slot >> 3) == row, (slot & 7), SB)] = w
    for k in range(NSUP):
        pos[order[k]] = k
    labels = jnp.zeros((SB, 1), jnp.int32)
    for t in range(SB):
        label = order[(pos[(inv[t] >> 3)] // 2) * 2]
        pltpu.make_async_copy(win_ref.at[pl.ds(t * BS, BS), columns_at(label)], buf.at[pl.ds(t * BS, BS), :], sem).start()
        labels = jnp.where(lax.broadcasted_iota(jnp.int32, (SB, 1), 0) == t, label, labels)
    pat[...] = pattern[pl.ds(pl.multiple_of(row * SB, SB), SB), :]
    mask = expand_mask(pat[...], labels, spread_matrix())
    pltpu.make_async_copy(win_ref.at[:, pl.ds(0, SN)], buf, sem).wait()
    for j in range(SB):
        out[j * BS:(j + 1) * BS, :] = buf[j * BS:(j + 1) * BS, :] * mask[j:j + 1, :]


def rhs_pack_kernel(rhs_ref, *sent):
    depth = lax.axis_index("rhs")
    width = sent[0].shape[1]
    for s, out in enumerate(sent):
        at = pl.multiple_of(jnp.bitwise_xor(depth, s) * width, width)
        out[...] = rhs_ref[:, pl.ds(at, width)]


def chip_pack_kernel(own_ref, other_ref, l_chip):
    l_chip[0:SN, :] = own_ref[...]
    l_chip[SN:PAIR, :] = other_ref[...]


def take_half_kernel(x_ref, out):
    out[...] = x_ref[0:SN, :]


def table_kernel(owner, order, tab, flag):
    row = lax.axis_index("rows")
    chip, core = (row >> 1), (row & 1)
    bad = 0
    for t in range(GROUPS * SB):
        tab[PACK + t] = 0
    for group in range(GROUPS):
        counts = 0
        for i in range(2 * SB):
            slot = owner[order[2 * group + (i >> 3)] * SB + (i & 7)]
            where, device = (slot >> 4), (slot >> 3)
            rank = (counts >> (8 * where)) & 255
            counts = counts + (1 << (8 * where))
            bad = bad | ((rank >> 3))
            rank = jnp.minimum(rank, SB - 1)
            rel = jnp.bitwise_xor(where, chip)
            cross = jnp.bitwise_xor((device & 1), core)
            kind = jnp.where((rel == 1) | (rel == 2), jnp.where(rel == 1 + core, 1, 2), rel)
            far_rank = 3 * SB + jnp.where((rank >> 2) == core, 0, 4) + (rank & 3)
            tab[SRC + group * 16 + i] = jnp.where(kind == 3, far_rank, kind * SB + rank)
            tab[jnp.where(rel == 0, PACK + group * SB + rank, TABLE)] = cross * SB + (slot & 7)
            if i >= SB:
                tab[LSRC + group * SB + i - SB] = (2 * kind + cross) * SB + (slot & 7)
    flag[0] = bad
    flag[1] = lax.axis_index("rhs")


def below_rhs_kernel(rhs_ref, *outs):
    depth = lax.axis_index("rhs")
    width = outs[0].shape[1]
    for s, out in enumerate(outs):
        out[...] = rhs_ref[:, pl.ds(pl.multiple_of(jnp.bitwise_xor(depth, s) * width, width), width)]


def first_pack_kernel(owner, order, *refs):
    pieces, (chip_rhs, p_ref, b_ref, place) = refs[:8], refs[8:]
    row, depth = lax.axis_index("rows"), lax.axis_index("rhs")
    core = (row & 1)
    tall = pieces[0].shape[0]
    for side in range(2):
        for s in range(4):
            at = pl.multiple_of(side * SB * BS + jnp.bitwise_xor(depth, s) * tall, tall)
            chip_rhs[pl.ds(at, tall), :] = pieces[4 * side + s][...]
    for t in range(SB):
        place[t] = 0
    rank = 0
    for i in range(2 * SB):
        slot = owner[order[(i >> 3)] * SB + (i & 7)]
        here = (slot >> 4) == (row >> 1)
        place[jnp.where(here & (rank < SB), rank, SB)] = jnp.bitwise_xor(((slot >> 3) & 1), core) * SB + (slot & 7)
        rank = rank + jnp.where(here, 1, 0)
    for t in range(SB):
        p_ref[t * BS:(t + 1) * BS, :] = chip_rhs[rows_at(place[t]), :]
    b_ref[...] = p_ref[pl.ds(pl.multiple_of(core * (SB >> 1) * BS, (SB >> 1) * BS), (SB >> 1) * BS), :]


def make_mask_kernel(group):
    def kernel(tab, order, pattern, w_own, w_other, out, pat):
        row = lax.axis_index("rows")
        places = [tab[PACK + (group + 1) * SB + j] for j in range(SB)]
        for j, place in enumerate(places):
            pat[j:j + 1, :] = pattern[pl.ds(jnp.bitwise_xor(row, (place >> 3)) * SB + (place & 7), 1), :]
        spread = spread_matrix()
        rows = pat[...]
        masks = [expand_mask(rows, order[k], spread) for k in range(2 * group + 2)]
        for j, place in enumerate(places):
            at = slice(j * BS, (j + 1) * BS)
            for side, w_ref in enumerate((w_own, w_other)):
                @pl.when((place >> 3) == side)
                def _(w_ref=w_ref, at=at, j=j, place=place):
                    for k in range(2 * group + 2):
                        block = w_ref[rows_at((place & 7)), columns_at(order[k])]
                        out[at, k * SN:(k + 1) * SN] = block * masks[k][j:j + 1, :]

    return kernel


def make_prep_kernel(group):
    last = group == GROUPS - 1

    def kernel(tab, order, diag, *refs):
        own, other, near, near_swap, far, far_swap = refs[:6]
        l_refs = ((own, 0), (other, 0), (near, 0), (near, SB), (near_swap, SB), (near_swap, 0), (far, 0), (far_swap, 0))
        refs = refs[6:]
        if last:
            m_out, lbuf = refs
        else:
            w_ref, chip_rhs = refs[:2]
            xs = refs[2:2 + group]
            m_out, r_out, lbuf = refs[2 + group:]
        for i in range(SB):
            code = tab[LSRC + group * SB + i]
            for m in range(8):
                @pl.when((code >> 3) == m)
                def _(m=m, i=i, code=code):
                    lbuf[i * BS:(i + 1) * BS, :] = l_refs[m][0][rows_at((code & 7) + l_refs[m][1]), :]
        first, second = diag[order[2 * group]], diag[order[2 * group + 1]]
        m_out[0:SN, 0:SN] = first
        m_out[SN:PAIR, SN:PAIR] = second
        joined = jnp.dot(second, lbuf[...], preferred_element_type=F32).astype(BF16)
        m_out[SN:PAIR, 0:SN] = (-jnp.dot(joined, first, preferred_element_type=F32)).astype(BF16)
        if not last:
            total = jnp.concatenate([chip_rhs[rows_at(tab[PACK + (group + 1) * SB + j]), :] for j in range(SB)], axis=0).astype(F32)
            for k in range(group):
                total = total - jnp.dot(w_ref[:, k * PAIR:(k + 1) * PAIR], xs[k][...], preferred_element_type=F32)
            r_out[...] = total

    return kernel


def make_solve_kernel(group):
    last = group == GROUPS - 1

    def kernel(*refs):
        tab, sources, m_ref = refs[0], refs[1:6], refs[6]
        if last:
            x_ref, panel, pool = refs[7:]
        else:
            r_ref, wn_ref, x_ref, p_ref, b_ref, panel, pool = refs[7:]
        at = 0
        for source in sources:
            pool[at:at + source.shape[0], :] = source[...]
            at += source.shape[0]
        for i in range(2 * SB):
            panel[i * BS:(i + 1) * BS, :] = pool[rows_at(tab[SRC + group * 16 + i]), :]
        x_ref[0:SN, :] = jnp.dot(m_ref[0:SN, 0:SN], panel[0:SN, :], preferred_element_type=F32).astype(BF16)
        x_ref[SN:PAIR, :] = jnp.dot(m_ref[SN:PAIR, :], panel[...], preferred_element_type=F32).astype(BF16)
        if last:
            return
        total = r_ref[...] - jnp.dot(wn_ref[:, group * PAIR:(group + 1) * PAIR], x_ref[...], preferred_element_type=F32)
        p_ref[...] = total.astype(BF16)
        core = lax.axis_index("rows") % 2
        b_ref[...] = p_ref[pl.ds(pl.multiple_of(core * (SB >> 1) * BS, (SB >> 1) * BS), (SB >> 1) * BS), :]

    return kernel


def make_below_mask_kernel(tile):
    def kernel(pattern, a_ref, out, sems):
        copies = []
        count = 2 * SB
        for j in range(count):
            c = pltpu.make_async_copy(a_ref.at[pl.ds((tile * count + j) * BS, BS), :], out.at[pl.ds(j * BS, BS), :], sems.at[j])
            c.start()
            copies.append(c)
        spread = spread_matrix()
        rows = pattern[tile * count:(tile + 1) * count, :]
        masks = [expand_mask(rows, k, spread) for k in range(NSUP)]
        for j in range(count):
            copies[j].wait()
            for k in range(NSUP):
                at = (slice(j * BS, (j + 1) * BS), slice(k * SN, (k + 1) * SN))
                out[at] = out[at] * masks[k][j:j + 1, :]

    return kernel


def below_product(order, a_ref, x_ref, group, i):
    rows = slice(((i & 1)) * SN, ((i & 1) + 1) * SN)
    first = jnp.dot(a_ref[rows, columns_at(order[2 * group])], x_ref[0:SN, :], preferred_element_type=F32)
    return first + jnp.dot(a_ref[rows, columns_at(order[2 * group + 1])], x_ref[SN:PAIR, :], preferred_element_type=F32)


def two_rows_kernel(order, a0, a1, x0_ref, x1_ref, out):
    for i, a_ref in enumerate((a0, a0, a1, a1)):
        out[i * SN:(i + 1) * SN, :] = below_product(order, a_ref, x0_ref, 0, i) + below_product(order, a_ref, x1_ref, 1, i)


def base_rows_kernel(order, a0, a1, x_ref, sums, h0, h1, h2, h3, out, rhs):
    depth = lax.axis_index("rhs")
    tall = h0.shape[0]
    for s, h in enumerate((h0, h1, h2, h3)):
        rhs[pl.ds(pl.multiple_of(jnp.bitwise_xor(depth, s) * tall, tall), tall), :] = h[...]
    for i, a_ref in enumerate((a0, a0, a1, a1)):
        at = slice(i * SN, (i + 1) * SN)
        out[at, :] = rhs[at, :].astype(F32) - (sums[at, :] + below_product(order, a_ref, x_ref, 2, i))


def last_rows_kernel(order, a0, a1, x0, x1, x2, x3, base, sol_ref, out_ref, done, sems, osem):
    copies = []
    for k, x in enumerate((x0, x1, x2, x3)):
        for q in range(2):
            at = pl.multiple_of(order[2 * k + q] * SN, SN)
            copies.append(pltpu.make_async_copy(x.at[pl.ds(q * SN, SN), :], sol_ref.at[pl.ds(at, SN), :], sems.at[2 * k + q]))
            copies[-1].start()
    for i, a_ref in enumerate((a0, a0, a1, a1)):
        at = slice(i * SN, (i + 1) * SN)
        done[at, :] = (base[at, :] - below_product(order, a_ref, x3, GROUPS - 1, i)).astype(BF16)
        copies.append(pltpu.make_async_copy(done.at[pl.ds(i * SN, SN), :], out_ref.at[pl.ds(i * SN, SN), :], osem.at[i]))
        copies[-1].start()
    for c in copies:
        c.wait()


def in_vmem(x):
    return pltpu.with_memory_space_constraint(x, pltpu.VMEM)


def in_hbm(x):
    return pltpu.with_memory_space_constraint(x, pltpu.HBM)


SMEM = pl.BlockSpec(memory_space=pltpu.SMEM)
VMEM = pl.BlockSpec(memory_space=pltpu.VMEM)
HBM = pl.BlockSpec(memory_space=pltpu.HBM)


def params(mib):
    return pltpu.CompilerParams(vmem_limit_bytes=mib * 1024 * 1024)


def cost(micros):
    return pl.CostEstimate(flops=micros * 10 ** 8, bytes_accessed=micros * 3 * 10 ** 6, transcendentals=0)


def shape_of(dims, dtype=BF16):
    return jax.ShapeDtypeStruct(dims, dtype)


def local(win_rows, anc_rows, win_pattern, anc_pattern, window_owner, sn_order, diag_inv, rhs_win, rhs_anc):
    if lax.axis_size("rows") != 8 or lax.axis_size("rhs") != 4 or anc_rows.shape[0] != 4 * SB * BS:
        win_rhs = lax.all_to_all(rhs_win, "rhs", split_axis=1, concat_axis=0, tiled=True)
        anc_rhs = lax.all_to_all(rhs_anc, "rhs", split_axis=1, concat_axis=0, tiled=True)
        return general_path(win_rows, anc_rows, win_pattern, anc_pattern, window_owner, sn_order, diag_inv, win_rhs, anc_rhs)

    def swap(x, m):
        return lax.ppermute(x, "rows", [(i, i ^ m) for i in range(8)])

    def deep(x, m):
        return lax.ppermute(x, "rhs", [(i, i ^ m) for i in range(4)])

    def neighbour(x):
        return lax.ppermute(x, "rows", [(i, i ^ (2 if i % 2 == 0 else 4)) for i in range(8)])

    def forward(x):
        return lax.ppermute(x, "rows", [(i, i ^ (4 if i % 2 == 0 else 2)) for i in range(8)])

    def mask_below(k, after):
        pattern_later, _ = lax.optimization_barrier((anc_pattern, after))
        return pl.pallas_call(
            make_below_mask_kernel(k),
            out_shape=shape_of((PAIR, NW)),
            in_specs=[VMEM, HBM],
            out_specs=VMEM,
            scratch_shapes=[pltpu.SemaphoreType.DMA((2 * SB,))],
            compiler_params=params(4),
            cost_estimate=cost(4),
            name="mask_below",
        )(pattern_later, in_hbm(anc_rows))

    columns = rhs_win.shape[1] // 4
    half = SN // 2
    tall = rhs_win.shape[0]
    w_own = in_hbm(win_rows)
    l_own = pl.pallas_call(
        factor_kernel,
        out_shape=shape_of((SN, SN)),
        in_specs=[SMEM, SMEM, VMEM, HBM],
        out_specs=VMEM,
        scratch_shapes=[pltpu.VMEM((SN, SN), BF16), pltpu.VMEM((SB, NWB), jnp.int32),
                        pltpu.SMEM((SB + 1,), jnp.int32), pltpu.SMEM((SB,), jnp.int32), pltpu.SemaphoreType.DMA],
        compiler_params=params(4),
        cost_estimate=cost(2),
        name="factor_pack",
    )(window_owner, sn_order, win_pattern, w_own)
    l_other = swap(l_own, 1)
    l_chip = pl.pallas_call(
        chip_pack_kernel,
        out_shape=shape_of((PAIR, SN)),
        in_specs=[VMEM] * 2,
        out_specs=VMEM,
        compiler_params=params(4),
        cost_estimate=cost(1),
        name="chip_pack",
    )(l_own, l_other)
    near = neighbour(l_chip)
    rhs_late, _ = lax.optimization_barrier((rhs_win, l_chip))
    sent = pl.pallas_call(
        rhs_pack_kernel,
        out_shape=(shape_of((tall, columns)),) * 4,
        in_specs=[VMEM],
        out_specs=(VMEM,) * 4,
        compiler_params=params(4),
        cost_estimate=cost(1),
        name="rhs_pack",
    )(rhs_late)
    pieces = [sent[0]] + [deep(sent[s], s) for s in (1, 2, 3)]
    w_late, _ = lax.optimization_barrier((win_rows, l_chip))
    w_other = swap(w_late, 1)
    below = [mask_below(0, l_chip)]
    w_other, below[0], *pieces = lax.optimization_barrier((w_other, *below, *pieces))
    others = [swap(x, 1) for x in pieces]
    chip_rhs, packed, part = pl.pallas_call(
        first_pack_kernel,
        out_shape=(shape_of((PAIR, columns)), shape_of((SN, columns)), shape_of((half, columns))),
        in_specs=[SMEM, SMEM] + [VMEM] * 8,
        out_specs=(VMEM,) * 3,
        scratch_shapes=[pltpu.SMEM((SB + 1,), jnp.int32)],
        compiler_params=params(4),
        cost_estimate=cost(1),
        name="first_pack",
    )(window_owner, sn_order, *pieces, *others)
    near, _ = lax.optimization_barrier((near, packed))
    near_half = pl.pallas_call(
        take_half_kernel,
        out_shape=shape_of((SN, SN)),
        in_specs=[VMEM],
        out_specs=VMEM,
        compiler_params=params(4),
        cost_estimate=cost(1),
        name="take_half",
    )(near)
    far = forward(near_half)
    owner_later, order_later, _ = lax.optimization_barrier((window_owner, sn_order, packed))
    tab, flag = pl.pallas_call(
        table_kernel,
        out_shape=(shape_of((TABLE + 1,), jnp.int32), shape_of((2,), jnp.int32)),
        in_specs=[SMEM, SMEM],
        out_specs=(SMEM, SMEM),
        compiler_params=params(4),
        cost_estimate=cost(2),
        name="tables",
    )(owner_later, order_later)
    w_other = in_vmem(w_other)
    w_own = in_vmem(win_rows)

    tile = rhs_anc.shape[0]
    sums, solved, masked = None, [], []
    diag_vmem = in_vmem(diag_inv)
    below_rows = anc_rows.shape[0]

    anc_order, anc_pieces = (2, 1, 3), [None] * 4
    for group in range(GROUPS):
        last = group == GROUPS - 1
        a_own = neighbour(packed)
        b_own = swap(part, 6)
        if group == 0:
            for k in range(GROUPS - 1):
                masked.append(pl.pallas_call(
                    make_mask_kernel(k),
                    out_shape=shape_of((SN, (k + 1) * PAIR)),
                    in_specs=[SMEM, SMEM, VMEM, VMEM, VMEM],
                    out_specs=VMEM,
                    scratch_shapes=[pltpu.VMEM((SB, NWB), jnp.int32)],
                    compiler_params=params(6),
                    cost_estimate=cost(2),
                    name="mask_rows",
                )(tab, order_later, win_pattern, w_own, w_other))
        if group == 0:
            rhs_later, _ = lax.optimization_barrier((rhs_anc, packed))
            anc_pieces = list(pl.pallas_call(
                below_rhs_kernel,
                out_shape=(shape_of((tile, columns)),) * 4,
                in_specs=[VMEM],
                out_specs=(VMEM,) * 4,
                compiler_params=params(4),
                cost_estimate=cost(1),
                name="below_rhs",
            )(in_vmem(rhs_later)))
        if not last:
            s = anc_order[group]
            moved, _ = lax.optimization_barrier((anc_pieces[s], packed))
            anc_pieces[s] = deep(moved, s)

        if group == 0:
            a_own, b_own, near, far, *masked = lax.optimization_barrier(
                (a_own, b_own, near, far, *masked))
            l_parts = [in_vmem(x) for x in (l_own, l_other, near, swap(near, 1), far, swap(far, 1))]
        operands = [tab, sn_order, diag_vmem, *l_parts]
        out_shape = [shape_of((PAIR, PAIR))]
        if not last:
            operands += [masked[group], chip_rhs, *solved]
            out_shape += [shape_of((SN, columns), F32)]
        ready = pl.pallas_call(
            make_prep_kernel(group),
            out_shape=tuple(out_shape),
            in_specs=[SMEM, SMEM] + [VMEM] * (len(operands) - 2),
            out_specs=(VMEM,) * len(out_shape),
            scratch_shapes=[pltpu.VMEM((SN, SN), BF16)],
            compiler_params=params(6),
            cost_estimate=cost(2),
            name="prep",
        )(*operands)
        hold = []
        if group == 1:
            below.append(mask_below(1, packed))
            hold = below[1:]
        elif group > 1:
            more, kernel = (solved[:2], two_rows_kernel) if group == 2 else ([solved[2], sums, *anc_pieces], base_rows_kernel)
            sums = pl.pallas_call(
                kernel,
                out_shape=shape_of((below_rows, columns), F32),
                in_specs=[SMEM] + [VMEM] * (2 + len(more)),
                out_specs=VMEM,
                scratch_shapes=[pltpu.VMEM((below_rows, columns), BF16)] if last else [],
                input_output_aliases={4: 0} if last else {},
                compiler_params=params(6),
                cost_estimate=cost(3),
                name="rows_below",
            )(sn_order, *below, *more)
            hold = [sums]
        if group > 0:
            s = anc_order[group - 1]
            a_own, b_own, anc_pieces[s], *rest = lax.optimization_barrier((a_own, b_own, anc_pieces[s], *hold, *ready))
            hold, ready = rest[:len(hold)], rest[len(hold):]
            if group == 1:
                below[1:] = hold
            else:
                sums = hold[0]
        a_swap = swap(a_own, 1)
        b_swap = swap(b_own, 1)
        ready = list(ready) if last else list(ready) + [masked[group]]

        out_shape = [shape_of((PAIR, columns))]
        if not last:
            out_shape += [shape_of((SN, columns)), shape_of((half, columns))]
        results = pl.pallas_call(
            make_solve_kernel(group),
            out_shape=tuple(out_shape),
            in_specs=[SMEM] + [VMEM] * (5 + len(ready)),
            out_specs=(VMEM,) * len(out_shape),
            scratch_shapes=[pltpu.VMEM((PAIR, columns), BF16), pltpu.VMEM((2 * PAIR, columns), BF16)],
            compiler_params=params(8),
            cost_estimate=cost(3),
            name="pair_solve",
        )(tab, packed, a_own, a_swap, b_own, b_swap, *ready)
        solved.append(results[0])
        if not last:
            packed, part = results[1:]

    outputs = pl.pallas_call(
        last_rows_kernel,
        out_shape=(shape_of((NW, columns)), shape_of((below_rows, columns))),
        in_specs=[SMEM] + [VMEM] * 7,
        out_specs=(HBM, HBM),
        scratch_shapes=[pltpu.VMEM((below_rows, columns), BF16), pltpu.SemaphoreType.DMA((2 * GROUPS,)),
                        pltpu.SemaphoreType.DMA((4,))],
        compiler_params=params(6),
        cost_estimate=cost(3),
        name="last_rows",
    )(sn_order, *below, *solved, sums)

    def again(carry):
        carry, own_pieces, below_pieces = lax.optimization_barrier((carry, pieces, anc_pieces))
        back = carry[0][1] ^ jnp.arange(4)
        win_rhs = jnp.take(jnp.stack(own_pieces), back, axis=0).reshape(4 * tall, columns)
        anc_rhs = jnp.take(jnp.stack(below_pieces), back, axis=0).reshape(4 * tile, columns)
        return jnp.zeros_like(carry[0]), *general_path(
            win_rows, anc_rows, win_pattern, anc_pattern, window_owner, sn_order, diag_inv, win_rhs, anc_rhs)

    return tuple(lax.while_loop(lambda carry: carry[0][0] != 0, again, (flag, *outputs))[1:])


def solution(mesh):
    return jax.shard_map(
        local,
        mesh=mesh,
        in_specs=(P("rows", None), P("rows", None), P(), P("rows", None), P(), P(), P(),
                  P(("rows", "rhs"), None), P(("rows", "rhs"), None)),
        out_specs=(P(None, "rhs"), P("rows", "rhs")),
        check_vma=False,
    )
```
